32 devices in a mesh: ctx: 8 (over y, x, core), wshard: 4 (over z).
Axes of the slice: x: 2, y: 2, z: 4, core: 2. Of those that a mesh axis runs over, the one named last changes fastest.
Arguments:
- tokens: bfloat16 [4, 1024, 1088], P('wshard', 'ctx'), may hold values from -6 to 6
- cotangent: bfloat16 [4, 1024, 1088], P('wshard', 'ctx'), may hold values from -6 to 6
- seq_lengths: int32 [4, 4], P('wshard'), may hold values from 1 to 512, 1024 in all within a row
- token_order: int32 [4, 1024], P('wshard'), may hold values from 0 to 1023, as said below
- attn_norm_gain: bfloat16 [1088], P('wshard'), may hold values from 0.5 to 1.5
- attn_norm_bias: bfloat16 [1088], P('wshard'), may hold values from -4 to 4
- input_weight: bfloat16 [1088, 3264], P('wshard'), may hold values from -0.1875 to 0.1875
- query_bias: bfloat16 [1088], P('wshard'), may hold values from -4 to 4
- value_bias: bfloat16 [1088], P('wshard'), may hold values from -4 to 4
- output_weight: bfloat16 [1088, 1088], P('wshard'), may hold values from -0.75 to 0.75
- output_bias: bfloat16 [1088], P('wshard'), may hold values from -4 to 4
- mlp_norm_gain: bfloat16 [1088], P('wshard'), may hold values from 0.5 to 1.5
- mlp_norm_bias: bfloat16 [1088], P('wshard'), may hold values from -4 to 4
- expand_weight: bfloat16 [1088, 4352], P('wshard'), may hold values from -0.1875 to 0.1875
- expand_bias: bfloat16 [4352], P('wshard'), may hold values from -4 to 4
- shrink_weight: bfloat16 [4352, 1088], P('wshard'), may hold values from -0.09375 to 0.09375
- shrink_bias: bfloat16 [1088], P('wshard'), may hold values from -4 to 4
Outputs:
- block_out: bfloat16 [4, 1024, 1088], P('wshard', 'ctx')
- input_grad: bfloat16 [4, 1024, 1088], P('wshard', 'ctx')
- grad_attn_norm_gain: float32 [1088], P('wshard')
- grad_attn_norm_bias: float32 [1088], P('wshard')
- grad_input_weight: float32 [1088, 3264], P('wshard')
- grad_query_bias: float32 [1088], P('wshard')
- grad_value_bias: float32 [1088], P('wshard')
- grad_output_weight: float32 [1088, 1088], P('wshard')
- grad_output_bias: float32 [1088], P('wshard')
- grad_mlp_norm_gain: float32 [1088], P('wshard')
- grad_mlp_norm_bias: float32 [1088], P('wshard')
- grad_expand_weight: float32 [1088, 4352], P('wshard')
- grad_expand_bias: float32 [4352], P('wshard')
- grad_shrink_weight: float32 [4352, 1088], P('wshard')
- grad_shrink_bias: float32 [1088], P('wshard')
The draws below stay inside these ranges and needn't reach their ends.
Inputs may be any that keep to these rules, and one draw needn't show every extreme that they name: `seq_lengths`: each row sums to 1024, and its largest entry is exactly 512. `token_order`: each group's row is a permutation of its tokens. The tokens fall into blocks of 64 consecutive tokens; each index of ctx holds two whole blocks, whose block numbers add up to one less than the number of blocks, each block's tokens in rising order.
All inputs are finite; a program needn't handle non-finite values.
Results may differ from the reference program's by a relative error of at most 0.019.
Values may be sent and summed in bfloat16 or wider, within the bound.
No kernel may reach another device: no remote copies, remote signals or barrier semaphores. Data moves between devices by JAX's collectives and lax.ppermute only.
A program may use at most 256 MiB of HBM per device.

```python
import math
import jax
import jax.numpy as jnp
import numpy as np
from jax import lax

D = 1088
HEADS = 17
HD = 64
FF = 4352
TOK_DEV = 128
NSEQ = 4
GROUPS = 4
GROUP_TOK = 1024
LONGEST = 512
N_CTX = 8
N_WSHARD = 4


def draw_token_order(key, part):
    half_block = TOK_DEV // 2

    def one_group(group_key):
        pair_key, flip_key = jax.random.split(group_key)
        pairing = jax.random.permutation(pair_key, N_CTX).astype(jnp.int32)
        flipped = jax.random.randint(flip_key, (N_CTX,), 0, 2, dtype=jnp.int32)
        first_block = jnp.where(flipped == 1, 2 * N_CTX - 1 - pairing, pairing)
        second_block = 2 * N_CTX - 1 - first_block
        block_ids = jnp.stack([first_block, second_block], axis=1).reshape(-1)
        rows_all = block_ids[:, None] * half_block + jnp.arange(half_block, dtype=jnp.int32)[None, :]
        return rows_all.reshape(-1).astype(jnp.int32)
    return jax.vmap(one_group)(jax.random.split(key, N_WSHARD))


def block_levels(stream_key, shape, cuts, smallest, largest):
    def one(axis_at, parts):
        steps = jax.random.uniform(jax.random.fold_in(jax.random.fold_in(stream_key, 6), axis_at), (parts,), jnp.float32, smallest / len(cuts), largest / len(cuts))
        return jnp.repeat(jnp.exp(steps), shape[axis_at] // parts).reshape((-1,) + (1,) * (len(shape) - axis_at - 1))

    loudness = one(*cuts[0])
    for cut in cuts[1:]:
        loudness = loudness * one(*cut)
    return loudness


def profile(amount, total, most, slope):
    loads = [(1 << 20) // math.isqrt(rank ** slope) + 1 for rank in range(2, amount + 1)]
    spare, given = total - most - (amount - 1), [1] * (amount - 1)
    while spare > 0:
        candidates = [i for i in range(amount - 1) if given[i] < most]
        whole, budget = sum([loads[i] for i in candidates]), spare
        for i in candidates:
            extra = min(most - given[i], max(1, budget * loads[i] // whole), spare)
            given[i] = given[i] + extra
            spare = spare - extra
    return np.array([most] + given)


def ragged(own_key, number_of, total, limit, lean):
    if number_of == 2:
        one = jax.random.randint(own_key, (), max(1, total - limit), min(limit, total - 1) + 1)
        return jnp.stack([one, total - one])
    sizes = jnp.asarray(profile(number_of, total, limit, lean), jnp.int32)
    pairs = (number_of - 1) // 2
    giver, receiver = sizes[1:1 + 2 * pairs:2], sizes[2:2 + 2 * pairs:2]
    margin = jnp.minimum(giver - 1, limit - receiver)
    passed = jax.random.randint(jax.random.fold_in(own_key, 1), (pairs,), 0, 1 << 20) % (margin + 1)
    sizes = sizes.at[1:1 + 2 * pairs:2].set(giver - passed).at[2:2 + 2 * pairs:2].set(receiver + passed)
    return sizes[jax.random.permutation(jax.random.fold_in(own_key, 2), number_of)]


def noise(key, shape, deviation, most, cuts=(), kind=jnp.bfloat16):
    array = jax.random.normal(key, shape, jnp.float32) * deviation
    if len(cuts) > 0:
        array = block_levels(key, shape, cuts, -0.22, 0.18) * array
    return jnp.clip(array, min=-most, max=most).astype(kind)


def setup_inputs(seed: int = 0) -> dict:
    keys = jax.random.split(jax.random.key(seed), 18)
    return {
        "tokens": noise(keys[0], (GROUPS, GROUP_TOK, D), 1.0, 6.0, ((0, 4), (1, 8))),
        "cotangent": noise(keys[1], (GROUPS, GROUP_TOK, D), 1.0, 6.0, ((0, 4), (1, 8))),
        "seq_lengths": jax.vmap(lambda own: ragged(own, NSEQ, GROUP_TOK, LONGEST, 2))(jax.random.split(keys[2], GROUPS)).reshape((GROUPS, NSEQ)).astype(jnp.int32),
        "token_order": draw_token_order(jax.random.fold_in(keys[17], 71), 0),
        "attn_norm_gain": jnp.clip(1.0 + 0.1 * jax.random.normal(keys[4], (D,), jnp.float32), 0.5, 1.5).astype(jnp.bfloat16),
        "attn_norm_bias": noise(keys[5], (D,), 0.3, 4.0, ((0, 4),)),
        "input_weight": noise(keys[6], (D, 3 * D), D ** -0.5, 0.1875, ((0, 4),)),
        "query_bias": noise(keys[7], (D,), 0.3, 4.0, ((0, 4),)),
        "value_bias": noise(keys[8], (D,), 0.3, 4.0, ((0, 4),)),
        "output_weight": noise(keys[9], (D, D), HD ** -0.5, 0.75, ((0, 4),)),
        "output_bias": noise(keys[10], (D,), 0.3, 4.0, ((0, 4),)),
        "mlp_norm_gain": jnp.clip(1.0 + 0.1 * jax.random.normal(keys[11], (D,), jnp.float32), 0.5, 1.5).astype(jnp.bfloat16),
        "mlp_norm_bias": noise(keys[12], (D,), 0.3, 4.0, ((0, 4),)),
        "expand_weight": noise(keys[13], (D, FF), D ** -0.5, 0.1875, ((0, 4),)),
        "expand_bias": noise(keys[14], (FF,), 0.3, 4.0, ((0, 4),)),
        "shrink_weight": noise(keys[15], (FF, D), FF ** -0.5, 0.09375, ((0, 4),)),
        "shrink_bias": noise(keys[16], (D,), 0.3, 4.0, ((0, 4),)),
    }


@jax.custom_vjp
def low(v):
    return lax.optimization_barrier(v.astype(jnp.bfloat16)).astype(jnp.float32)

@jax.custom_vjp
def low_back(v):
    return v

def low_keep(v):
    return (low(v), None)

def low_pass(kept, grad):
    return (grad,)

def back_keep(v):
    return (v, None)

def back_low(kept, grad):
    return (low(grad),)
low.defvjp(low_keep, low_pass)
low_back.defvjp(back_keep, back_low)
EPSILON = 1e-05
masked_fill = -1e+30
precise_mode = lax.Precision.HIGHEST

def layer_norm(values, scale_gain, shift_bias):
    center = values - lax.optimization_barrier(jnp.mean(values, axis=-1, keepdims=True))
    spread = lax.optimization_barrier(jnp.mean(center * center, axis=-1, keepdims=True))
    return center * lax.rsqrt(spread + EPSILON) * scale_gain + shift_bias

def matmul(left, right):
    return jnp.dot(left, right, precision=precise_mode, preferred_element_type=jnp.float32)

def seq_starts(positions, lengths_row):
    ends = jnp.cumsum(lengths_row, dtype=jnp.int32)
    begins = ends - lengths_row
    inside = (positions[:, None] >= begins[None, :]) & (positions[:, None] < ends[None, :])
    return lax.optimization_barrier(jnp.sum(jnp.where(inside, begins[None, :], 0), axis=1)).astype(jnp.int32)

def group_layer(group_rows, lengths_row, positions, weights):
    gain_attn, bias_attn, weight_in, bias_query, bias_value, weight_out, bias_out, gain_mlp, bias_mlp, weight_up, bias_up, weight_down, bias_down = weights
    row_count, model_width = group_rows.shape
    starts = seq_starts(positions, lengths_row)
    normed = low(layer_norm(group_rows, gain_attn, bias_attn))
    joint = matmul(normed, weight_in)
    queries = low_back(low(joint[:, :model_width] + bias_query)).reshape(row_count, HEADS, HD)
    keys_all = low_back(low(joint[:, model_width:2 * model_width])).reshape(row_count, HEADS, HD)
    values_all = low_back(low(joint[:, 2 * model_width:] + bias_value)).reshape(row_count, HEADS, HD)
    block_rows = min(512, row_count)
    block_count = row_count // block_rows

    def attend(pieces):
        query_block, query_pos, query_start = pieces
        scores = jnp.einsum('qhd,khd->hqk', query_block, keys_all, precision=precise_mode) * 0.125
        scores = low_back(scores)
        allowed = (positions[None, :] >= query_start[:, None]) & (positions[None, :] <= query_pos[:, None])
        scores = jnp.where(allowed[None], scores, masked_fill)
        row_peak = lax.optimization_barrier(jnp.max(scores, axis=-1, keepdims=True))
        expo = jnp.exp(scores - row_peak)
        probs = expo / lax.optimization_barrier(jnp.sum(expo, axis=-1, keepdims=True))
        mixed_heads = jnp.einsum('hqk,khd->qhd', low(probs), values_all, precision=precise_mode)
        return mixed_heads.reshape(block_rows, model_width)
    blocks = lax.map(jax.checkpoint(attend), (queries.reshape(block_count, block_rows, HEADS, HD), positions.reshape(block_count, block_rows), starts.reshape(block_count, block_rows)))
    attn = low_back(low(blocks.reshape(row_count, model_width)))
    mixed = group_rows + low_back(matmul(attn, weight_out) + bias_out)
    normed_two = low(layer_norm(mixed, gain_mlp, bias_mlp))
    hidden = low_back(matmul(normed_two, weight_up) + bias_up)
    active = low(jax.nn.gelu(hidden, approximate=True))
    return mixed + low_back(matmul(active, weight_down) + bias_down)

def reference(tokens, cotangent, seq_lengths, token_order, attn_norm_gain, attn_norm_bias, input_weight, query_bias, value_bias, output_weight, output_bias, mlp_norm_gain, mlp_norm_bias, expand_weight, expand_bias, shrink_weight, shrink_bias):
    params = tuple((item.astype(jnp.float32) for item in (attn_norm_gain, attn_norm_bias, input_weight, query_bias, value_bias, output_weight, output_bias, mlp_norm_gain, mlp_norm_bias, expand_weight, expand_bias, shrink_weight, shrink_bias)))

    def forward(inputs, *weights):

        def one_group(pieces):
            group_rows, lengths_row, positions = pieces
            return group_layer(group_rows, lengths_row, positions, weights)
        return lax.map(one_group, (inputs, seq_lengths, token_order))
    result, pullback = jax.vjp(forward, tokens.astype(jnp.float32), *params)
    grads = pullback(cotangent.astype(jnp.float32))
    return (result.astype(jnp.bfloat16), grads[0].astype(jnp.bfloat16), grads[1], grads[2], grads[3], grads[4], grads[5], grads[6], grads[7], grads[8], grads[9], grads[10], grads[11], grads[12], grads[13])
```

```python
import functools

import jax
import jax.numpy as jnp
from jax import lax
from jax.experimental import pallas as pl
from jax.experimental.pallas import tpu as pltpu
from jax.sharding import PartitionSpec as P

HEADS = 17
HD = 64
EPSILON = 1e-05
masked_fill = -1e30
BF = jnp.bfloat16
F32 = jnp.float32
NN = (((1,), (0,)), ((), ()))
NT = (((1,), (1,)), ((), ()))
TN = (((0,), (0,)), ((), ()))
VMEM_BYTES = 60 * 1024 * 1024
VECS = 16
WIDE = 512
WEIGHTS = {
    "attend": 1.5,
    "attend_rest": 1.5,
    "mix": 1.5,
    "pack_shared": 1.0,
    "shrink_part": 0.01,
    "back": 3.0,
    "proj_grads": 30.0,
}


def dot(left, right, dims=NN):
    return lax.dot_general(left, right, dims, preferred_element_type=F32)


VM = pl.BlockSpec(memory_space=pltpu.VMEM)
HB = pl.BlockSpec(memory_space=pl.ANY)
SM = pl.BlockSpec(memory_space=pltpu.SMEM)


def shape(dims, kind=BF):
    return jax.ShapeDtypeStruct(tuple(dims), kind)


def kernel_call(body, name, ins, outs, scratch, micros):
    micros = micros * WEIGHTS.get(name, 5.0)
    result = pl.pallas_call(
        body,
        out_shape=tuple(item for _, item in outs),
        in_specs=[spec for spec, _ in ins],
        out_specs=tuple(spec for spec, _ in outs),
        scratch_shapes=scratch,
        compiler_params=pltpu.CompilerParams(vmem_limit_bytes=VMEM_BYTES),
        cost_estimate=pl.CostEstimate(
            flops=int(micros * 4e8), bytes_accessed=int(micros * 3.4e6), transcendentals=0
        ),
        name=name,
    )(*[array for _, array in ins])
    return result


class Reader:
    def __init__(self, refs):
        self.left = list(refs)

    def one(self):
        return self.left.pop(0)

    def many(self, count):
        return [self.left.pop(0) for _ in range(count)]


def here():
    return lax.axis_index("ctx"), lax.axis_index("wshard")


def aligned(value, step):
    return pl.multiple_of(value, step)


def norm_rows(rows):
    center = rows - jnp.mean(rows, axis=-1, keepdims=True)
    spread = jnp.mean(center * center, axis=-1, keepdims=True)
    inverse = lax.rsqrt(spread + EPSILON)
    return center * inverse, inverse


def starts_of(lens):
    found, total = [], 0
    for s in range(1, lens.shape[1]):
        total = total + lens[0, s - 1]
        found.append(total)
    return found


def mask_of(starts, first_query, queries, first_key, keys):
    query_pos = first_query + lax.broadcasted_iota(jnp.int32, (queries, 1), 0)
    key_pos = first_key + lax.broadcasted_iota(jnp.int32, (1, keys), 1)
    begin = jnp.zeros((queries, 1), jnp.int32)
    for start in starts:
        begin = jnp.where(query_pos >= start, start, begin)
    return (key_pos >= begin) & (key_pos <= query_pos)


def windows(total, step):
    longest = total // 2
    for first in range(0, total, step):
        yield first, max(0, first - longest), first + step


def sorted_at(order, c, rows, k, h):
    half = rows // 2
    return aligned(order[0, rows * (c ^ k) + half * h] // half * half, half)


def full_lanes(width):
    return -(-width // 128) * 128


def places(n):
    return list(range(1, n, 2)) + list(range(0, n, 2))


def k_at(n, i):
    return jnp.where(i < n // 2, 2 * i + 1, 2 * i - n)


def start_all(pairs, sems):
    copies = [
        pltpu.make_async_copy(source, target, sems.at[i])
        for i, (source, target) in enumerate(pairs)
    ]
    for item in copies:
        item.start()
    return copies


def wait_all(copies):
    for item in copies:
        item.wait()


def piece_rows(part, n):
    return -(-(-(-part // n)) // 8) * 8


def pack_first_kernel(n, own, *refs):
    reader = Reader(refs)
    win, wout = reader.many(2)
    vectors = reader.many(8)
    (up_bias,) = reader.many(1)
    (lead,) = reader.many(1)
    qs, ks, vs, os, in_rows, out_rows, sems = reader.many(7)
    c, _ = here()
    part, width = wout.shape
    piece = piece_rows(part, n)
    off = aligned(jnp.minimum(piece * c, part - piece), 8)
    rem = own * n
    lane = aligned(own * c, 128)
    windows_in = [(0, qs), (width, ks), (2 * width, vs)]
    pairs = [
        (win.at[:, pl.ds(aligned(start // 128 * 128 + lane, 128), held.shape[1])], held)
        for start, held in windows_in
    ]
    pairs.append((wout.at[:, pl.ds(lane, own)], os))
    pairs.append((win.at[pl.ds(off, piece), :], in_rows))
    pairs.append((wout.at[pl.ds(off, piece), :], out_rows))
    copies = start_all(pairs, sems)
    base = part + 2 * piece
    lead[part:, 2 * own :] = jnp.zeros((part // 2, own), BF)
    rows = [item[...].astype(F32).reshape(1, part) for item in vectors]
    flat = up_bias[...].astype(F32)
    rows += [flat[part * i : part * (i + 1)].reshape(1, part) for i in range(width // part)]
    rows.append(jnp.zeros((VECS - len(rows), part), F32))
    small = jnp.concatenate(rows, axis=0).astype(BF)
    for t in range(-(-part // 128)):
        cut = small[:, 128 * t : min(128 * t + 128, part)]
        lead[base + VECS * t : base + VECS * (t + 1), 2 * own : 2 * own + cut.shape[1]] = cut
    wait_all(copies)
    for kind, (start, held) in enumerate(windows_in):
        skip = start % 128
        lead[:part, own * kind : own * (kind + 1)] = held[:, skip : skip + own]
    lead[part:, :own] = os[: part // 2, :]
    lead[part:, own : 2 * own] = os[part // 2 :, :]
    four = [in_rows[:, kind * width + rem : kind * width + rem + HD] for kind in range(3)]
    four.append(out_rows[:, rem : rem + HD])
    for i in range(2):
        lead[part + i * piece : part + (i + 1) * piece, 2 * own :] = jnp.concatenate(
            four[2 * i : 2 * i + 2], axis=1
        )


def pack_first(win, wout, vectors, up_bias, n, own):
    part, width = wout.shape
    piece = piece_rows(part, n)

    def held(start):
        return pltpu.VMEM((part, own + (128 if start % 128 else 0)), BF)

    return kernel_call(
        functools.partial(pack_first_kernel, n, own),
        "pack_first",
        [(HB, win), (HB, wout)] + [(VM, item) for item in (*vectors, up_bias)],
        [(VM, shape((part + part // 2, 3 * own)))],
        [
            held(0),
            held(width),
            held(2 * width),
            pltpu.VMEM((part, own), BF),
            pltpu.VMEM((piece, 3 * width), BF),
            pltpu.VMEM((piece, width), BF),
            pltpu.SemaphoreType.DMA((6,)),
        ],
        2,
    )[0]


def pack_rows_kernel(x, dm, out):
    width, rows = x.shape
    out[:rows, :width] = x[...].astype(F32).T.astype(BF)
    out[rows:, :width] = dm[...].astype(F32).T.astype(BF)
    out[:, width:] = jnp.zeros((2 * rows, out.shape[1] - width), BF)


def pack_rows(x, dm):
    rows, width = x.shape
    return kernel_call(
        pack_rows_kernel,
        "pack_rows",
        [(VM, x.T), (VM, dm.T)],
        [(VM, shape((2 * rows, full_lanes(width))))],
        [],
        2,
    )[0]


def pack_shared_kernel(part, *refs):
    nz = len(refs) - 2
    half = part // 2
    pairs = [
        (refs[j].at[pl.ds(part, half)], refs[nz].at[pl.ds(half * j, half)]) for j in range(nz)
    ]
    wait_all(start_all(pairs, refs[nz + 1]))


def pack_shared(leads, part):
    nz = len(leads)
    return kernel_call(
        functools.partial(pack_shared_kernel, part),
        "pack_shared",
        [(HB, item) for item in leads],
        [(VM, shape((part // 2 * nz, leads[0].shape[1])))],
        [pltpu.SemaphoreType.DMA((nz,))],
        1,
    )[0]


def pack_ffn_kernel(n, nz, wup, wdown, out, held, sems):
    c, _ = here()
    part, ff = wup.shape
    seg = ff // (n * nz)
    half = part // 2
    pairs, shifts = [], []
    for q in range(nz):
        start = q * seg * n + seg * c
        base = aligned(start // 128 * 128, 128)
        shifts.append(start - base)
        pairs.append((wup.at[:, pl.ds(base, 256)], held.at[q]))
    pairs.append(
        (wdown.at[pl.ds(aligned(seg * c, 8), seg), :], out.at[pl.ds(half, seg), :])
    )
    copies = start_all(pairs, sems)
    wait_all(copies[:nz])
    pieces = [
        pltpu.roll(held[q].astype(F32), lax.rem(256 - shifts[q], 256), 1)[:, :seg]
        for q in range(nz)
    ]
    whole = jnp.concatenate(pieces, axis=1)
    out[:half, :] = jnp.concatenate([whole[:half], whole[half:]], axis=1).astype(BF)
    wait_all(copies[nz:])


def pack_ffn(wup, wdown, n, nz):
    part, ff = wup.shape
    width = wdown.shape[1]
    seg = ff // (n * nz)
    return kernel_call(
        functools.partial(pack_ffn_kernel, n, nz),
        "pack_ffn",
        [(HB, wup), (HB, wdown)],
        [(VM, shape((part // 2 + seg, width)))],
        [pltpu.VMEM((nz, part, 256), BF), pltpu.SemaphoreType.DMA((nz + 1,))],
        3,
    )[0]


def attend_heads(starts, total, count, q_ref, k_ref, v_ref, o_ref):
    def head(h, carry):
        for first, low, high in windows(total, 256):
            scores = dot(q_ref[h, first : first + 256, :], k_ref[h, low:high, :], NT)
            allowed = mask_of(starts, first, 256, low, high - low)
            scores = jnp.where(allowed, scores, masked_fill)
            peak = jnp.max(scores, axis=-1, keepdims=True)
            expo = jnp.exp(scores - peak)
            weight = 1.0 / jnp.sum(expo, axis=-1, keepdims=True)
            out = dot((expo * weight).astype(BF), v_ref[h, low:high, :])
            o_ref[h, first : first + 256, :] = out.astype(BF)
        return carry

    lax.fori_loop(0, count, head, 0)


def split_joint(joint, cut, at, own, heads, q_ref, k_ref, v_ref):
    for h in range(heads):
        qa, ka, va = h * HD, own + h * HD, 2 * own + h * HD
        query = joint[cut, qa : qa + HD].astype(BF).astype(F32) * 0.125
        q_ref[h, at, :] = query.astype(BF)
        k_ref[h, at, :] = joint[cut, ka : ka + HD].astype(BF)
        v_ref[h, at, :] = joint[cut, va : va + HD].astype(BF)


def attend_kernel(n, nz, hp, *refs):
    reader = Reader(refs)
    order, lens = reader.many(2)
    xs_in, leads = reader.many(n), reader.many(nz)
    n1_ref, h_ref, w_nat, q_ref, k_ref, v_ref, own_ref, vec = reader.many(8)
    xs, small, os, sems = reader.many(4)
    c, z = here()
    rows = xs_in[0].shape[0] // 2
    half = rows // 2
    total = xs.shape[0]
    width = n1_ref.shape[1]
    part = width // nz
    own = hp * HD
    tiles = -(-part // 128)
    base = part + 2 * piece_rows(part, n)
    pairs = [
        (xs_in[k].at[pl.ds(0, rows)], xs.at[pl.ds(rows * k, rows)]) for k in range(n)
    ]
    for j in range(nz):
        to = w_nat.at[pl.ds(aligned(part * (z ^ j), part), part)]
        pairs.append((leads[j].at[pl.ds(0, part)], to))
        source = leads[j].at[pl.ds(base, VECS * tiles), pl.ds(2 * own, own)]
        pairs.append((source, small.at[z ^ j]))
    wait_all(start_all(pairs, sems))
    for q in range(nz):
        item = small[q].astype(F32)
        row = jnp.concatenate([item[VECS * t : VECS * (t + 1)] for t in range(tiles)], axis=1)
        vec[:, part * q : part * (q + 1)] = row[:, :part]
    gain, shift = vec[0:1, :], vec[1:2, :]
    lane = pl.ds(aligned(own * c, own), own)
    bias = jnp.concatenate(
        [vec[2:3, lane], jnp.zeros((1, own), F32), vec[3:4, lane]], axis=1
    )

    def normalise(k, carry):
        at = pl.ds(aligned(k * rows, rows), rows)
        normed, _ = norm_rows(xs[at, :width].astype(F32))
        hidden = (normed * gain + shift).astype(BF)
        normed = normed.astype(BF)
        for i in range(2):
            to = pl.ds(sorted_at(order, c, rows, k, i), half)
            n1_ref[to, :] = normed[i * half : (i + 1) * half]
            h_ref[to, :] = hidden[i * half : (i + 1) * half]
        return carry

    def project(p, carry):
        at = pl.ds(aligned(p * WIDE, WIDE), WIDE)
        joint = dot(h_ref[at, :], w_nat[...]) + bias
        split_joint(joint, slice(0, WIDE), at, own, hp, q_ref, k_ref, v_ref)
        return carry

    lax.fori_loop(0, n, normalise, 0)
    lax.fori_loop(0, total // WIDE, project, 0)
    attend_heads(starts_of(lens), total, hp, q_ref, k_ref, v_ref, os)
    for h in range(hp):
        own_ref[:, h * HD : (h + 1) * HD] = os[h]


def attend(order, lens, xs, leads, hp, width):
    n, nz = len(xs), len(leads)
    total = xs[0].shape[0] // 2 * n
    part, cols = width // nz, leads[0].shape[1]
    tiles = -(-part // 128)
    heads = shape((hp, total, HD))
    return kernel_call(
        functools.partial(attend_kernel, n, nz, hp),
        "attend",
        [(SM, order), (SM, lens)] + [(HB, item) for item in (*xs, *leads)],
        [
            (VM, item)
            for item in (
                shape((total, width)),
                shape((total, width)),
                shape((width, cols)),
                heads,
                heads,
                heads,
                shape((total, hp * HD)),
                shape((VECS, width), F32),
            )
        ],
        [
            pltpu.VMEM((total, full_lanes(width)), BF),
            pltpu.VMEM((nz, VECS * tiles, 128), BF),
            pltpu.VMEM((hp, total, HD), BF),
            pltpu.SemaphoreType.DMA((n + 2 * nz,)),
        ],
        11,
    )


def attend_rest_kernel(n, nz, part, *refs):
    reader = Reader(refs)
    (lens,) = reader.many(1)
    hidden, vec = reader.many(2)
    blocks = reader.many(n)
    wr, q_ref, k_ref, v_ref, o_ref, wo, wo_own = reader.many(7)
    (sems,) = reader.many(1)
    c, z = here()
    total, width = hidden.shape
    own = blocks[0].shape[1] // 3
    pairs = []
    for k in range(n):
        lane = pl.ds(aligned(own * (c ^ k), own), own)
        for j in range(nz):
            for i in range(2):
                row = pl.ds(aligned(part * (z ^ j) + i * (part // 2), 8), part // 2)
                source = blocks[k].at[pl.ds(part // 2 * j, part // 2), pl.ds(own * i, own)]
                pairs.append((source, wo.at[row, lane]))
    copies = start_all(pairs, sems)
    piece = piece_rows(part, n)
    rem = width - HD
    step = part // 2
    for k in range(n):
        off = jnp.minimum(piece * (c ^ k), part - piece)
        for j in range(nz):
            at = pl.ds(aligned(part * (z ^ j) + off, 8), piece)
            for i in range(2):
                low = step * j + i * piece
                wr[at, 128 * i : 128 * (i + 1)] = blocks[k][low : low + piece, 256:384]
    bias = jnp.concatenate(
        [vec[2:3, rem:], jnp.zeros((1, HD), F32), vec[3:4, rem:], jnp.zeros((1, HD), F32)],
        axis=1,
    )

    def project(p, carry):
        at = pl.ds(aligned(p * 256, 256), 256)
        joint = dot(hidden[at, :], wr[...]) + bias
        split_joint(joint, slice(0, 256), at, HD, 1, q_ref, k_ref, v_ref)
        return carry

    lax.fori_loop(0, total // 256, project, 0)
    attend_heads(starts_of(lens), total, 1, q_ref, k_ref, v_ref, o_ref)
    wo[:, rem:] = wr[:, 3 * HD : 4 * HD]
    wait_all(copies)
    wo_own[:own, :] = wo[pl.ds(aligned(own * c, own), own), :]
    wo_own[own:, :] = wo[rem:, :]


def attend_rest(lens, hidden, vec, blocks, nz, part):
    n = len(blocks)
    total, width = hidden.shape
    head = shape((1, total, HD))
    return kernel_call(
        functools.partial(attend_rest_kernel, n, nz, part),
        "attend_rest",
        [(SM, lens), (VM, hidden), (VM, vec)] + [(VM, item) for item in blocks],
        [
            (VM, item)
            for item in (
                shape((width, 4 * HD)),
                head,
                head,
                head,
                head,
                shape((width, width)),
                shape((blocks[0].shape[1] // 3 + HD, width)),
            )
        ],
        [pltpu.SemaphoreType.DMA((2 * n * nz,))],
        5,
    )


def gelu_parts(u):
    c0 = 0.7978845608028654
    c1 = 0.044715
    square = u * u
    t = jnp.tanh(c0 * (u + c1 * square * u))
    act = 0.5 * u * (1.0 + t)
    slope = 0.5 * (1.0 + t) + 0.5 * u * (1.0 - t * t) * (c0 * (1.0 + 3.0 * c1 * square))
    return act, slope


def put_padded(ref, at, value):
    width = value.shape[1]
    ref[at, :width] = value.astype(BF)
    ref[at, width:] = jnp.zeros((value.shape[0], ref.shape[1] - width), BF)


def mix_kernel(n, *refs):
    reader = Reader(refs)
    (order,) = reader.many(1)
    xs_in, at_in = (reader.many(n) for _ in range(2))
    at_rem, wo, vec = reader.many(3)
    att_ref, h2_ref, x2_ref = reader.many(3)
    xs, att, x2s, sems = reader.many(4)
    c, _ = here()
    total, width = h2_ref.shape
    rows = total // n
    half = rows // 2
    own = at_in[0].shape[1]
    pairs, late = [], []
    for i, k in enumerate(places(n)):
        late.append((xs_in[k].at[pl.ds(0, rows)], xs.at[pl.ds(rows * i, rows)]))
        lane = pl.ds(aligned(own * (c ^ k), own), own)
        pairs.append((at_in[k], att.at[:, lane]))
    copies = start_all(pairs + late, sems)
    att[:, own * n :] = at_rem[0]
    out_bias, gain, shift = vec[4:5, :], vec[5:6, :], vec[6:7, :]
    wait_all(copies[: len(pairs)])

    def arrange(i, carry):
        for h in range(2):
            source = pl.ds(sorted_at(order, c, rows, k_at(n, i), h), half)
            att_ref[pl.ds(aligned(i * rows + h * half, half), half), :] = att[source, :]
        return carry

    def attended(p, carry):
        at = pl.ds(aligned(p * WIDE, WIDE), WIDE)
        x2s[at, :] = dot(att_ref[at, :], wo[...])
        return carry

    def normalise(i, carry):
        at = pl.ds(aligned(i * rows, rows), rows)
        x2 = xs[at, :width].astype(F32) + x2s[at, :] + out_bias

        @pl.when(i == n // 2)
        def _():
            x2_ref[...] = x2

        normed, _ = norm_rows(x2)
        h2_ref[at, :] = (normed * gain + shift).astype(BF)
        return carry

    lax.fori_loop(0, n, arrange, 0)
    lax.fori_loop(0, total // WIDE, attended, 0)
    wait_all(copies[len(pairs) :])
    lax.fori_loop(0, n, normalise, 0)


def mix(order, xs, ats, at_rem, wo, vec):
    n = len(xs)
    width = vec.shape[1]
    rows = xs[0].shape[0] // 2
    total = rows * n
    return kernel_call(
        functools.partial(mix_kernel, n),
        "mix",
        [(SM, order)]
        + [(HB, item) for item in (*xs, *ats)]
        + [(VM, item) for item in (at_rem, wo, vec)],
        [
            (VM, item)
            for item in (
                shape((total, width)),
                shape((total, width)),
                shape((rows, width), F32),
            )
        ],
        [
            pltpu.VMEM((total, full_lanes(width)), BF),
            pltpu.VMEM((total, width), BF),
            pltpu.VMEM((total, width), F32),
            pltpu.SemaphoreType.DMA((2 * n,)),
        ],
        9,
    )


def mlp_kernel(n, nz, *refs):
    reader = Reader(refs)
    dm_in = reader.many(n)
    ffn_w, h2_ref, vec = reader.many(3)
    e_odd, e_even, act_ref, du_ref, wd = reader.many(5)
    dms, wu, us, sems = reader.many(4)
    c, _ = here()
    total, width = h2_ref.shape
    rows = total // n
    part = width // nz
    hid = wu.shape[1]
    seg = hid // nz
    pairs = [
        (dm_in[k].at[pl.ds(rows, rows)], dms.at[pl.ds(rows * i, rows)])
        for i, k in enumerate(places(n))
    ]
    copies = start_all(pairs, sems)
    for q in range(nz):
        for i in range(2):
            low = part * q + i * (part // 2)
            wu[low : low + part // 2, :] = ffn_w[q, : part // 2, i * hid : (i + 1) * hid]
        wd[seg * q : seg * (q + 1), :] = ffn_w[q, part // 2 :, :]
    fold = part // seg
    row = vec[pl.ds(8 + c // fold, 1), :]
    up_bias = jnp.zeros((1, hid), F32)
    for f in range(fold):
        cut = [row[:, part * q + seg * f : part * q + seg * (f + 1)] for q in range(nz)]
        up_bias = jnp.where(c % fold == f, jnp.concatenate(cut, axis=1), up_bias)

    def expand(p, carry):
        at = pl.ds(aligned(p * WIDE, WIDE), WIDE)
        us[at, :] = dot(h2_ref[at, :], wu[...])
        return carry

    def activate(i, carry):
        at = pl.ds(aligned(i * rows, rows), rows)
        act, slope = gelu_parts(us[at, :] + up_bias)
        act_ref[at, :] = act.astype(BF)
        us[at, :] = slope
        return carry

    def shrink(p, carry):
        at = pl.ds(aligned(p * WIDE, WIDE), WIDE)
        du_ref[at, :] = (dot(dms[at, :width], wd[...], NT) * us[at, :]).astype(BF)
        return carry

    lax.fori_loop(0, total // WIDE, expand, 0)
    lax.fori_loop(0, n, activate, 0)
    wait_all(copies)
    lax.fori_loop(0, total // WIDE, shrink, 0)
    put_padded(e_odd, slice(None), dot(du_ref[: total // 2, :], wu[...], NT))
    e_even[...] = dot(du_ref[total // 2 :, :], wu[...], NT).astype(BF)


def mlp(dms, ffn_w, h2, vec):
    n, nz = len(dms), ffn_w.shape[0]
    total, width = h2.shape
    hid = width // 2
    return kernel_call(
        functools.partial(mlp_kernel, n, nz),
        "mlp",
        [(HB, item) for item in dms] + [(VM, item) for item in (ffn_w, h2, vec)],
        [
            (VM, item)
            for item in (
                shape((total // 2, full_lanes(width))),
                shape((total // 2, width)),
                shape((total, hid)),
                shape((total, hid)),
                shape((hid, width)),
            )
        ],
        [
            pltpu.VMEM((total, full_lanes(width)), BF),
            pltpu.VMEM((width, hid), BF),
            pltpu.VMEM((total, hid), F32),
            pltpu.SemaphoreType.DMA((n,)),
        ],
        15,
    )


def shrink_part_kernel(act, wd, odd, even):
    half = odd.shape[0]
    put_padded(odd, slice(None), dot(act[:half, :], wd[...]))
    even[...] = dot(act[half:, :], wd[...]).astype(BF)


def shrink_part(act, wd):
    half, width = act.shape[0] // 2, wd.shape[1]
    return kernel_call(
        shrink_part_kernel,
        "shrink_part",
        [(VM, act), (VM, wd)],
        [(VM, shape((half, full_lanes(width)))), (VM, shape((half, width)))],
        [],
        4,
    )


def pair_sums_kernel(mine, other, *outs):
    rows, width = outs[0].shape
    for i, out in enumerate(outs):
        cut = slice(rows * i, rows * (i + 1))
        out[...] = (mine[cut].astype(F32) + other[cut, :width].astype(F32)).astype(BF)


def pair_sums(mine, other, rows):
    total, width = mine.shape
    return kernel_call(
        pair_sums_kernel,
        "pair_sums",
        [(VM, mine), (VM, other)],
        [(VM, shape((rows, width)))] * (total // rows),
        [],
        2,
    )


def blocks_of(width, step):
    return [(low, min(step, width - low)) for low in range(0, width, step)]


def ffn_grads_kernel(n, nz, *refs):
    reader = Reader(refs)
    dm_in = reader.many(n)
    h2, act, du = reader.many(3)
    out, du_sum = reader.many(2)
    dms, gu, gd, sems = reader.many(4)
    total, hid = du.shape
    width = h2.shape[1]
    rows = total // n
    part, seg = width // nz, hid // nz
    tall = part // 2 + seg
    pairs = [
        (dm_in[k].at[pl.ds(rows, rows)], dms.at[pl.ds(rows * i, rows)])
        for i, k in enumerate(places(n))
    ]
    copies = start_all(pairs, sems)
    for low, size in blocks_of(width, 256):
        gu[low : low + size, :] = dot(h2[:, low : low + size], du[...], TN).astype(BF)
    du_sum[...] = dot(jnp.ones((8, total), BF), du[...])
    wait_all(copies)
    for low, size in blocks_of(hid, 256):
        gd[low : low + size, :] = dot(act[:, low : low + size], dms[:, :width], TN).astype(BF)
    for q in range(nz):
        base = tall * q
        for i in range(2):
            low = part * q + i * (part // 2)
            out[base : base + part // 2, i * hid : (i + 1) * hid] = gu[low : low + part // 2, :]
        out[base + part // 2 : base + tall, :] = gd[seg * q : seg * (q + 1), :]


def ffn_grads(dms, h2, act, du, nz):
    n = len(dms)
    width = h2.shape[1]
    total, hid = du.shape
    part, seg = width // nz, hid // nz
    return kernel_call(
        functools.partial(ffn_grads_kernel, n, nz),
        "ffn_grads",
        [(HB, item) for item in dms] + [(VM, item) for item in (h2, act, du)],
        [(VM, shape((nz * (part // 2 + seg), width))), (VM, shape((8, hid), F32))],
        [
            pltpu.VMEM((total, full_lanes(width)), BF),
            pltpu.VMEM((width, hid), BF),
            pltpu.VMEM((hid, width), BF),
            pltpu.SemaphoreType.DMA((n,)),
        ],
        9,
    )


def norm_back(rows, gain, error):
    normed, inverse = norm_rows(rows)
    f = error * gain
    slope = inverse * (
        f
        - jnp.mean(f, axis=-1, keepdims=True)
        - normed * jnp.mean(f * normed, axis=-1, keepdims=True)
    )
    return slope, normed


def middle_kernel(count, *refs):
    reader = Reader(refs)
    parts = reader.many(count)
    x2, both, vec = reader.many(3)
    dx2_ref, db_ref, sums = reader.many(3)
    error = parts[0][...].astype(F32)
    for item in parts[1:]:
        error = error + item[...].astype(F32)
    slope, normed = norm_back(x2[...], vec[5:6, :], error)
    upstream = both[both.shape[0] // 2 :, : x2.shape[1]].astype(F32)
    dx2 = upstream + slope
    dx2_ref[...] = dx2
    db = dx2.astype(BF)
    db_ref[...] = db
    rows = [jnp.sum(item, axis=0, keepdims=True) for item in (db.astype(F32), error * normed, error, upstream)]
    sums[...] = jnp.concatenate(rows + [jnp.zeros_like(rows[0])] * 4, axis=0)


def middle(parts, x2, both, vec):
    rows, width = x2.shape
    return kernel_call(
        functools.partial(middle_kernel, len(parts)),
        "middle",
        [(VM, item) for item in (*parts, x2, both, vec)],
        [(VM, shape((rows, width), F32)), (VM, shape((rows, width))), (VM, shape((8, width), F32))],
        [],
        2,
    )


def back_heads(starts, total, count, q_ref, k_ref, v_ref, das, out, dks, dvs):
    def head(h, carry):
        dks[...] = jnp.zeros_like(dks)
        dvs[...] = jnp.zeros_like(dvs)
        for first, low, high in windows(total, 256):
            at = slice(first, first + 256)
            query = q_ref[h, at, :]
            scores = dot(query, k_ref[h, low:high, :], NT)
            allowed = mask_of(starts, first, 256, low, high - low)
            scores = jnp.where(allowed, scores, masked_fill)
            peak = jnp.max(scores, axis=-1, keepdims=True)
            expo = jnp.exp(scores - peak)
            soft = expo * (1.0 / jnp.sum(expo, axis=-1, keepdims=True))
            da = das[h, at, :]
            dp = dot(da, v_ref[h, low:high, :], NT)
            delta = jnp.sum(soft * dp, axis=-1, keepdims=True)
            ds = (soft * (dp - delta)).astype(BF)
            out[h, at, :] = (dot(ds, k_ref[h, low:high, :]) * 0.125).astype(BF)
            dks[low:high, :] += dot(ds, query, TN)
            dvs[low:high, :] += dot(soft.astype(BF), da, TN)
        out[count + h, :, :] = dks[...].astype(BF)
        out[2 * count + h, :, :] = dvs[...].astype(BF)
        return carry

    lax.fori_loop(0, count, head, 0)


def back_kernel(n, hp, *refs):
    reader = Reader(refs)
    order, lens = reader.many(2)
    db_in = reader.many(n)
    wo, w_nat, q_ref, k_ref, v_ref = reader.many(5)
    e_odd, e_even, dj_ref, das_rest = reader.many(4)
    dbs, das, out, dks, dvs, sems = reader.many(6)
    c, _ = here()
    rows, width = db_in[0].shape
    half = rows // 2
    total = rows * n
    own = hp * HD
    wait_all(start_all([(db_in[k], dbs.at[pl.ds(rows * k, rows)]) for k in range(n)], sems))

    def project(p, carry):
        at = pl.ds(aligned(p * (2 * rows), 2 * rows), 2 * rows)
        da = dot(dbs[at, :], wo[...], NT).astype(BF)
        for i in range(4):
            to = pl.ds(sorted_at(order, c, rows, 2 * p + i // 2, i % 2), half)
            for h in range(hp):
                das[h, to, :] = da[i * half : (i + 1) * half, h * HD : (h + 1) * HD]
            das_rest[0, to, :] = da[i * half : (i + 1) * half, own:]
        return carry

    lax.fori_loop(0, n // 2, project, 0)
    back_heads(starts_of(lens), total, hp, q_ref, k_ref, v_ref, das, out, dks, dvs)
    for i in range(3 * hp):
        dj_ref[:, i * HD : (i + 1) * HD] = out[i]

    def scatter(e_ref, first, p, carry):
        at = pl.ds(aligned(p * (2 * rows), 2 * rows), 2 * rows)
        pieces = []
        for i in range(4):
            k = 4 * p + 2 * (i // 2) + first
            source = pl.ds(sorted_at(order, c, rows, k, i % 2), half)
            pieces.append(dj_ref[source, :])
        error = dot(jnp.concatenate(pieces, axis=0), w_nat[...], NT)
        if e_ref.shape[1] == w_nat.shape[0]:
            e_ref[at, :] = error.astype(BF)
        else:
            put_padded(e_ref, at, error)
        return carry

    lax.fori_loop(0, n // 4, functools.partial(scatter, e_odd, 1), 0)
    lax.fori_loop(0, n // 4, functools.partial(scatter, e_even, 0), 0)


def back(order, lens, dbs, wo, w_nat, q, k, v):
    n = len(dbs)
    rows, width = dbs[0].shape
    hp, total, _ = q.shape
    big = pltpu.VMEM((total, width), BF)
    column = pltpu.VMEM((total, HD), F32)
    return kernel_call(
        functools.partial(back_kernel, n, hp),
        "back",
        [(SM, order), (SM, lens)]
        + [(HB, item) for item in dbs]
        + [(VM, item) for item in (wo, w_nat, q, k, v)],
        [
            (VM, shape((total // 2, full_lanes(width)))),
            (VM, shape((total // 2, width))),
            (VM, shape((total, 3 * hp * HD))),
            (VM, shape((1, total, HD))),
        ],
        [
            big,
            pltpu.VMEM((hp, total, HD), BF),
            pltpu.VMEM((3 * hp, total, HD), BF),
            column,
            column,
            pltpu.SemaphoreType.DMA((n,)),
        ],
        17,
    )


def back_rest_kernel(*refs):
    reader = Reader(refs)
    order, lens = reader.many(2)
    das, q_ref, k_ref, v_ref, wr = reader.many(5)
    dj_ref, e_ref = reader.many(2)
    out, dks, dvs = reader.many(3)
    c, _ = here()
    total = q_ref.shape[1]
    rows = e_ref.shape[0]
    back_heads(starts_of(lens), total, 1, q_ref, k_ref, v_ref, das, out, dks, dvs)
    for i in range(3):
        dj_ref[:, i * HD : (i + 1) * HD] = out[i]
    pieces = [dj_ref[pl.ds(sorted_at(order, c, rows, 0, i), rows // 2), :] for i in range(2)]
    e_ref[...] = dot(jnp.concatenate(pieces, axis=0), wr[:, : 3 * HD], NT)


def back_rest(order, lens, das, q, k, v, wr, rows):
    total = q.shape[1]
    column = pltpu.VMEM((total, HD), F32)
    return kernel_call(
        back_rest_kernel,
        "back_rest",
        [(SM, order), (SM, lens)] + [(VM, item) for item in (das, q, k, v, wr)],
        [(VM, shape((total, 3 * HD))), (VM, shape((rows, wr.shape[0]), F32))],
        [pltpu.VMEM((3, total, HD), BF), column, column],
        6,
    )


def weight_terms(weights, product, dj_sum):
    def summed(item):
        column = jnp.sum(item, axis=1, keepdims=True)
        return jnp.broadcast_to(column, (column.shape[0], 128)).T[0:1]

    return summed(weights * product), summed(weights * dj_sum)


def vec_columns(vec):
    tall = jnp.concatenate([vec[0:8, :]] * 16, axis=0)
    return tall.T[:, 0:8]


def proj_grads_kernel(n, nz, *refs):
    reader = Reader(refs)
    db_in = reader.many(n)
    n1, dj, w_nat, vec, att = reader.many(5)
    outs = reader.many(nz)
    (sums,) = reader.many(1)
    dbs, held, sems, out_sems = reader.many(4)
    c, z = here()
    rows, width = db_in[0].shape
    total, cols = dj.shape
    own = cols // 3
    part = width // nz
    pairs = [(db_in[k], dbs.at[pl.ds(rows * i, rows)]) for i, k in enumerate(places(n))]
    copies = start_all(pairs, sems)
    product = dot(n1[...], dj[...], TN)
    dj_sum = dot(jnp.ones((8, total), BF), dj[...])[0:1]
    weights = w_nat[...].astype(F32)
    gain, shift = weight_terms(weights, product, dj_sum)
    sums[0:1, :] = gain
    sums[1:2, :] = shift
    sums[2:8, :] = jnp.zeros((6, width), F32)
    lane = pl.ds(aligned(own * c, own), own)
    sums[2:3, lane] = dj_sum[:, :own]
    sums[3:4, lane] = dj_sum[:, 2 * own :]
    columns = vec_columns(vec)
    grad = product * columns[:, 0:1] + columns[:, 1:2] * dj_sum
    held[:, :cols] = grad.astype(BF)
    wait_all(copies)
    held[:, cols:] = dot(att[...], dbs[:, lane], TN).astype(BF)
    wait_all(
        start_all(
            [
                (held.at[pl.ds(aligned(part * (z ^ j), part), part)], outs[j])
                for j in range(nz)
            ],
            out_sems,
        )
    )


def proj_grads(dbs, n1, dj, w_nat, vec, att, nz):
    n = len(dbs)
    rows, width = dbs[0].shape
    total, cols = dj.shape
    wide = cols // 3 * 4
    out = kernel_call(
        functools.partial(proj_grads_kernel, n, nz),
        "proj_grads",
        [(HB, item) for item in dbs] + [(VM, item) for item in (n1, dj, w_nat, vec, att)],
        [(HB, shape((width // nz, wide)))] * nz + [(VM, shape((8, width), F32))],
        [
            pltpu.VMEM((total, width), BF),
            pltpu.VMEM((width, wide), BF),
            pltpu.SemaphoreType.DMA((n,)),
            pltpu.SemaphoreType.DMA((nz,)),
        ],
        5,
    )
    return out[:nz], out[nz]


def rest_grads_kernel(n, nz, *refs):
    reader = Reader(refs)
    db_in = reader.many(n)
    n1, dj, wr, vec, att, sums_mid, sums_proj, du_sum = reader.many(8)
    outs = reader.many(nz)
    dbs, grad, wide, ups, held, sems, out_sems = reader.many(7)
    c, z = here()
    rows, width = db_in[0].shape
    total = dj.shape[0]
    part = width // nz
    piece = piece_rows(part, n)
    seg = du_sum.shape[1] // nz
    rem = width - HD
    pairs = [(db_in[k], dbs.at[pl.ds(rows * i, rows)]) for i, k in enumerate(places(n))]
    copies = start_all(pairs, sems)
    product = dot(n1[...], dj[...], TN)
    dj_sum = dot(jnp.ones((8, total), BF), dj[...])[0:1]
    weights = wr[:, : 3 * HD].astype(F32)
    gain, shift = weight_terms(weights, product, dj_sum)
    once = jnp.where(c == 0, 1.0, 0.0)
    wide[0:4, :] = sums_proj[0:4, :]
    wide[0:1, :] += gain * once
    wide[1:2, :] += shift * once
    wide[2:3, rem:] += dj_sum[:, :HD] * once
    wide[3:4, rem:] += dj_sum[:, 2 * HD :] * once
    wide[4:8, :] = sums_mid[0:4, :]
    columns = vec_columns(vec)
    grad[:, : 3 * HD] = product * columns[:, 0:1] + columns[:, 1:2] * dj_sum
    fold = part // seg
    for q in range(nz):
        item = du_sum[0:1, seg * q : seg * (q + 1)]
        for r in range(width // part):
            cut = [
                jnp.where(c == r * fold + f, item, jnp.zeros_like(item)) for f in range(fold)
            ]
            ups[q, r : r + 1, :] = jnp.concatenate(cut, axis=1)
    wait_all(copies)
    grad[:, 3 * HD :] = dot(att[...], dbs[:, rem:], TN)
    off = jnp.minimum(piece * c, part - piece)
    held[...] = jnp.zeros_like(held)
    for q in range(nz):
        held[q, :piece, : 4 * HD] = grad[pl.ds(aligned(part * q + off, 8), piece), :].astype(BF)
        both = jnp.concatenate([wide[0:8, part * q : part * (q + 1)], ups[q]], axis=0)
        held[q, piece : piece + both.shape[0], :part] = both.astype(BF)
    wait_all(start_all([(held.at[z ^ j], outs[j]) for j in range(nz)], out_sems))


def rest_grads(dbs, n1, dj, wr, vec, att, sums_mid, sums_proj, du_sum, nz):
    n = len(dbs)
    rows, width = dbs[0].shape
    total = dj.shape[0]
    part = width // nz
    tall = piece_rows(part, n) + 8 + -(-(width // part) // 8) * 8
    lanes = -(-part // 128) * 128
    return kernel_call(
        functools.partial(rest_grads_kernel, n, nz),
        "rest_grads",
        [(HB, item) for item in dbs]
        + [(VM, item) for item in (n1, dj, wr, vec, att, sums_mid, sums_proj, du_sum)],
        [(HB, shape((tall, lanes)))] * nz,
        [
            pltpu.VMEM((total, width), BF),
            pltpu.VMEM((width, 4 * HD), F32),
            pltpu.VMEM((8, width), F32),
            pltpu.VMEM((nz, width // part, part), F32),
            pltpu.VMEM((nz, tall, lanes), BF),
            pltpu.SemaphoreType.DMA((n,)),
            pltpu.SemaphoreType.DMA((nz,)),
        ],
        4,
    )


def joined_sums_kernel(count, *refs):
    out = refs[2 * count]
    part = refs[0].shape[0]
    tall, lanes = refs[count].shape
    for first, low, size, wide in ((0, 0, part, out.shape[1]), (count, part, tall, lanes)):
        total = refs[first][...].astype(F32)
        for item in refs[first + 1 : first + count]:
            total = total + item[...].astype(F32)
        out[low : low + size, :wide] = total.astype(BF)
    out[part:, lanes:] = jnp.zeros((out.shape[0] - part, out.shape[1] - lanes), BF)


def joined_sums(p_terms, r_terms):
    part, wide = p_terms[0].shape
    return kernel_call(
        functools.partial(joined_sums_kernel, len(p_terms)),
        "joined_sums",
        [(VM, item) for item in (*p_terms, *r_terms)],
        [(VM, shape((part + r_terms[0].shape[0], wide)))],
        [],
        2,
    )[0]


def last_kernel(count, *refs):
    reader = Reader(refs)
    parts = reader.many(count)
    rest, both, dx2, vec = reader.many(4)
    (out,) = reader.many(1)
    rows, width = dx2.shape
    error = rest[...]
    for item in parts:
        error = error + item[...].astype(F32)
    slope, _ = norm_back(both[:rows, :width].astype(F32), vec[0:1, :], error)
    out[...] = (dx2[...] + slope).T.astype(BF)


def last(parts, rest, both, dx2, vec):
    return kernel_call(
        functools.partial(last_kernel, len(parts)),
        "last",
        [(VM, item) for item in (*parts, rest, both, dx2, vec)],
        [(VM, shape(dx2.shape[::-1]))],
        [],
        2,
    )[0].T


def block_out_kernel(count, *refs):
    reader = Reader(refs)
    parts = reader.many(count)
    x2, vec = reader.many(2)
    (out,) = reader.many(1)
    total = x2[...] + vec[7:8, :]
    for item in parts:
        total = total + item[...].astype(F32)
    out[...] = total.T.astype(BF)


def block_out_of(parts, x2, vec):
    return kernel_call(
        functools.partial(block_out_kernel, len(parts)),
        "block_out",
        [(VM, item) for item in (*parts, x2, vec)],
        [(VM, shape(x2.shape[::-1]))],
        [],
        1,
    )[0].T


def ffn_out_kernel(n, nz, blocks, up_out, down_out, held, up, down, in_sems, sems):
    part = up.shape[0]
    hid = held.shape[2] // 2
    seg = hid // nz
    half = part // 2
    arriving = start_all([(blocks.at[k], held.at[k]) for k in range(n)], in_sems)
    leaving = []
    for k in range(n):
        arriving[k].wait()
        cut = pl.ds(seg * k, seg)
        down[seg * k : seg * (k + 1), :] = held[k, half:, :].astype(F32)
        leaving.append(pltpu.make_async_copy(down.at[cut], down_out.at[cut], sems.at[k]))
        leaving[-1].start()
    for i in range(2):
        for q in range(nz):
            low = i * hid + q * seg
            pieces = [held[k, :half, low : low + seg].astype(F32) for k in range(n)]
            up[i * half : (i + 1) * half, q * seg * n : (q + 1) * seg * n] = jnp.concatenate(
                pieces, axis=1
            )
        cut = pl.ds(half * i, half)
        leaving.append(pltpu.make_async_copy(up.at[cut], up_out.at[cut], sems.at[n + i]))
        leaving[-1].start()
    wait_all(leaving)


def ffn_out(blocks, nz):
    n, tall, width = blocks.shape
    part = width // nz
    seg = tall - part // 2
    up, down = (part, seg * n * nz), (seg * n, width)
    return kernel_call(
        functools.partial(ffn_out_kernel, n, nz),
        "ffn_out",
        [(HB, blocks)],
        [(HB, shape(up, F32)), (HB, shape(down, F32))],
        [
            pltpu.VMEM((n, tall, width), BF),
            pltpu.VMEM(up, F32),
            pltpu.VMEM(down, F32),
            pltpu.SemaphoreType.DMA((n,)),
            pltpu.SemaphoreType.DMA((n + 2,)),
        ],
        8,
    )


def proj_out_kernel(n, own, piece, *refs):
    reader = Reader(refs)
    blocks = reader.many(n)
    out_in, out_o = reader.many(2)
    vectors = reader.many(8)
    (up_bias,) = reader.many(1)
    held, held_rest, rest = reader.many(3)
    c, _ = here()
    part, width = out_o.shape
    tall, lanes = held_rest.shape[1:]
    for k in range(n):
        held[c ^ k] = blocks[k][:part, :]
        held_rest[c ^ k] = blocks[k][part:, :lanes].astype(F32)
    total = held_rest[0, piece:, :]
    for k in range(1, n):
        total = total + held_rest[k, piece:, :]
    for i in range(8):
        vectors[i][...] = total[i, :part]
    for i in range(width // part):
        up_bias[part * i : part * (i + 1)] = total[8 + i, :part]
    for k in range(n):
        at = min(piece * k, part - piece)
        rest[at : at + piece, :] = held_rest[k, :piece, : 4 * HD]
    pieces = []
    for kind in range(3):
        for k in range(n):
            pieces.append(held[k, :, own * kind : own * (kind + 1)].astype(F32))
        pieces.append(rest[:, HD * kind : HD * (kind + 1)])
    out_in[...] = jnp.concatenate(pieces, axis=1)
    for k in range(n):
        out_o[:, own * k : own * (k + 1)] = held[k, :, 3 * own : 4 * own].astype(F32)
    out_o[:, own * n :] = rest[:, 3 * HD : 4 * HD]


def proj_out(blocks, part):
    n = len(blocks)
    cols = blocks[0].shape[1]
    own = cols // 4
    tall = blocks[0].shape[0] - part
    lanes = -(-part // 128) * 128
    piece = piece_rows(part, n)
    width = own * n + HD
    return kernel_call(
        functools.partial(proj_out_kernel, n, own, piece),
        "proj_out",
        [(VM, item) for item in blocks],
        [
            (VM, shape((part, 3 * width), F32)),
            (VM, shape((part, width), F32)),
        ]
        + [(VM, shape((part,), F32))] * 8
        + [(VM, shape((width,), F32))],
        [
            pltpu.VMEM((n, part, cols), BF),
            pltpu.VMEM((n, tall, lanes), F32),
            pltpu.VMEM((part, 4 * HD), F32),
        ],
        5,
    )


def swap(value, axis, size, bit, label):
    with jax.named_scope(label + str(bit)):
        return lax.ppermute(value, axis, [(i, i ^ bit) for i in range(size)])


def after(value, *others):
    return lax.optimization_barrier((value, *others))[0]


def gather_z(value, nz, label):
    order = sorted(range(1, nz), reverse=True)
    parts = {0: value}
    for j in order:
        parts[j] = swap(value, "wshard", nz, j, label)
    return [parts[j] for j in range(nz)]


def far_of(n):
    return sorted(range(2, n, 2), key=lambda k: -bin(k).count("1"))


def gather_far(value, n, label):
    parts = {0: value}
    for k in far_of(n):
        parts[k] = swap(value, "ctx", n, k, label)
    return parts


def gather_near(parts, n, label):
    for k in sorted(parts):
        parts[k ^ 1] = swap(parts[k], "ctx", n, 1, f"{label}_{k}_")
    return [parts[k] for k in range(n)]


def gather_ctx(value, n, label):
    return gather_near(gather_far(value, n, label), n, label)


def relay_far(value, n, label):
    parts = {0: value}
    for k in range(2, n, 2):
        bit = 1 << (k.bit_length() - 1)
        parts[k] = swap(parts[k ^ bit], "ctx", n, bit, f"{label}_{k}_")
    return parts


def spread_ctx(sums, n, label):
    return [sums[0]] + [swap(sums[k // 2], "ctx", n, k, label) for k in far_of(n)]


def scatter_z(chunks, nz, label):
    return [chunks[0]] + [
        swap(chunks[j], "wshard", nz, j, label) for j in sorted(range(1, nz), reverse=True)
    ]


def local_fast(
    n,
    nz,
    tokens,
    cotangent,
    seq_lengths,
    token_order,
    attn_norm_gain,
    attn_norm_bias,
    input_weight,
    query_bias,
    value_bias,
    output_weight,
    output_bias,
    mlp_norm_gain,
    mlp_norm_bias,
    expand_weight,
    expand_bias,
    shrink_weight,
    shrink_bias,
):
    rows = tokens.shape[1]
    part = input_weight.shape[0]
    hp = HEADS // n
    own = hp * HD

    vectors = (
        attn_norm_gain,
        attn_norm_bias,
        query_bias,
        value_bias,
        output_bias,
        mlp_norm_gain,
        mlp_norm_bias,
        shrink_bias,
    )
    width = tokens.shape[2]
    lead = pack_first(input_weight, output_weight, vectors, expand_bias, n, own)
    both = pack_rows(after(tokens[0], lead), cotangent[0])
    packed = pack_ffn(after(expand_weight, lead), shrink_weight, n, nz)
    far = relay_far(both, n, "rows")
    first = after(lead, packed, far[2 % n])
    leads = [lead] + [
        swap(first if j == 1 else lead, "wshard", nz, j, "lead") for j in range(1, nz)
    ]
    arrived = lax.optimization_barrier((packed, tuple(leads), far))
    packed, leads, far = arrived
    boths = gather_near(far, n, "rows")
    ffn_w = lax.all_gather(packed, "wshard")
    shared_far = gather_far(pack_shared(leads, part), n, "shared")

    n1, hidden, w_nat, q, k, v, at_own, vec = attend(
        token_order, seq_lengths, boths, leads, hp, width
    )
    shared = gather_near({k: after(shared_far[k], at_own) for k in shared_far}, n, "shared")
    at_far = gather_far(at_own, n, "attn")
    wr, q_r, k_r, v_r, at_rest, wo, wo_own = attend_rest(
        seq_lengths, hidden, vec, shared, nz, part
    )
    ats = gather_near({k: after(at_far[k], at_rest) for k in at_far}, n, "attn")
    att, h2, x2 = mix(token_order, boths, ats, at_rest, wo, vec)
    e_odd, e_even, act, du, wd = mlp(boths, ffn_w, h2, vec)

    e_sums = pair_sums(e_even, swap(e_odd, "ctx", n, 1, "e2_"), rows)
    e_terms = spread_ctx(e_sums, n, "e2_far")
    f_chunks, du_sum = ffn_grads(boths, h2, act, after(du, *e_sums), nz)
    m_odd, m_even = shrink_part(after(act, du_sum), wd)
    dx2, db_own, sums_mid = middle(e_terms, after(x2, m_odd), both, vec)
    f_chunks = after(f_chunks, *e_terms)
    f_sum = lax.psum_scatter(f_chunks, "wshard", scatter_dimension=0, tiled=True)
    db_far = gather_far(db_own, n, "db")
    m_other = swap(after(m_odd, db_own), "ctx", n, 1, "out_")
    m_sums = pair_sums(m_even, m_other, rows)
    dbs = gather_near({k: after(db_far[k], *m_sums) for k in db_far}, n, "db")
    m_terms = spread_ctx([after(item, *dbs) for item in m_sums], n, "out_far")

    e1_odd, e1_even, dj, das_rest = back(
        token_order, seq_lengths, dbs, wo_own, w_nat, q, k, v
    )
    e1_other = swap(e1_odd, "ctx", n, 1, "e1_")
    p_chunks, sums_proj = proj_grads(dbs, after(n1, *m_terms), dj, w_nat, vec, att, nz)
    p_terms = scatter_z(p_chunks, nz, "proj")
    e1_sums = pair_sums(after(e1_even, *p_chunks), e1_other, rows)
    e1_terms = spread_ctx(e1_sums, n, "e1_far")
    dj_rest, e1_rest = back_rest(
        token_order, seq_lengths, after(das_rest, *e1_sums), q_r, k_r, v_r, wr, rows
    )
    f_blocks = lax.all_gather(after(f_sum, dj), "ctx")
    r_chunks = rest_grads(dbs, n1, dj_rest, wr, vec, att, sums_mid, sums_proj, du_sum, nz)
    r_terms = scatter_z(r_chunks, nz, "rest")
    p_terms[0] = after(p_terms[0], *e1_terms)

    grads_far = gather_far(joined_sums(p_terms, r_terms), n, "grads")
    block_out = block_out_of(m_terms, x2, vec)[None]
    input_grad = last(e1_terms, e1_rest, both, dx2, vec)[None]
    out_up, out_down = ffn_out(f_blocks, nz)
    blocks = {k: after(grads_far[k], block_out, input_grad, out_up) for k in grads_far}
    blocks = gather_near(blocks, n, "grads")
    out_in, out_o, *small = proj_out(blocks, part)
    return (
        block_out,
        input_grad,
        small[0],
        small[1],
        out_in,
        small[2],
        small[3],
        out_o,
        small[4],
        small[5],
        small[6],
        out_up,
        small[8],
        out_down,
        small[7],
    )


def layer_norm(values, scale_gain, shift_bias):
    center = values - jnp.mean(values, axis=-1, keepdims=True)
    spread = jnp.mean(center * center, axis=-1, keepdims=True)
    return center * lax.rsqrt(spread + EPSILON) * scale_gain + shift_bias


def gelu_act(values):
    return jax.nn.gelu(values, approximate=True)


def outer_sum(left, right):
    return lax.dot_general(
        left, right, (((0,), (0,)), ((), ())), preferred_element_type=jnp.float32
    )


def times_t(left, right):
    return lax.dot_general(
        left, right, (((1,), (1,)), ((), ())), preferred_element_type=jnp.float32
    )


def seq_starts(positions, lengths_row):
    ends = jnp.cumsum(lengths_row, dtype=jnp.int32)
    begins = ends - lengths_row
    inside = (positions[:, None] >= begins[None, :]) & (positions[:, None] < ends[None, :])
    return jnp.sum(jnp.where(inside, begins[None, :], 0), axis=1)


def take_rows(source, block_index, size):
    return lax.dynamic_slice_in_dim(source, block_index * size, size)


def scores_of(query_heads, key_heads, query_pos, query_start, key_pos):
    scores = (
        jnp.einsum("qhd,khd->hqk", query_heads, key_heads, preferred_element_type=jnp.float32)
        * 0.125
    )
    allowed = (key_pos[None, :] >= query_start[:, None]) & (key_pos[None, :] <= query_pos[:, None])
    return jnp.where(allowed[None], scores, masked_fill)


def local_plain(
    tokens,
    cotangent,
    seq_lengths,
    token_order,
    attn_norm_gain,
    attn_norm_bias,
    input_weight,
    query_bias,
    value_bias,
    output_weight,
    output_bias,
    mlp_norm_gain,
    mlp_norm_bias,
    expand_weight,
    expand_bias,
    shrink_weight,
    shrink_bias,
):
    gathered = (
        lax.all_gather(input_weight, "wshard", axis=0, tiled=True),
        lax.all_gather(output_weight, "wshard", axis=0, tiled=True),
        lax.all_gather(expand_weight, "wshard", axis=0, tiled=True),
        lax.all_gather(shrink_weight, "wshard", axis=0, tiled=True),
        lax.all_gather(attn_norm_gain, "wshard", axis=0, tiled=True),
        lax.all_gather(attn_norm_bias, "wshard", axis=0, tiled=True),
        lax.all_gather(query_bias, "wshard", axis=0, tiled=True),
        lax.all_gather(value_bias, "wshard", axis=0, tiled=True),
        lax.all_gather(output_bias, "wshard", axis=0, tiled=True),
        lax.all_gather(mlp_norm_gain, "wshard", axis=0, tiled=True),
        lax.all_gather(mlp_norm_bias, "wshard", axis=0, tiled=True),
        lax.all_gather(expand_bias, "wshard", axis=0, tiled=True),
        lax.all_gather(shrink_bias, "wshard", axis=0, tiled=True),
    )
    (
        weight_in,
        weight_out,
        weight_up,
        weight_down,
        gain_attn,
        bias_attn,
        bias_query,
        bias_value,
        bias_out,
        gain_mlp,
        bias_mlp,
        bias_up,
        bias_down,
    ) = gathered
    head_count = HEADS
    head_dim = HD
    inputs = tokens[0].astype(jnp.float32)
    row_count, model_width = inputs.shape
    group_len = token_order.shape[1]
    ctx_index = lax.axis_index("ctx")
    all_pos = token_order[0]
    all_start = seq_starts(all_pos, seq_lengths[0])
    my_pos = lax.dynamic_slice_in_dim(all_pos, ctx_index * row_count, row_count)
    my_start = lax.dynamic_slice_in_dim(all_start, ctx_index * row_count, row_count)
    block_rows = min(512, group_len)
    block_count = group_len // block_rows
    block_ids = jnp.arange(block_count, dtype=jnp.int32)
    normed_full, norm_pull = jax.vjp(
        layer_norm, inputs, gain_attn.astype(jnp.float32), bias_attn.astype(jnp.float32)
    )
    normed = normed_full.astype(jnp.bfloat16)
    joint = jnp.dot(normed, weight_in, preferred_element_type=jnp.float32)
    queries = (joint[:, :model_width] + bias_query.astype(jnp.float32)).astype(jnp.bfloat16)
    keys_own = joint[:, model_width : 2 * model_width].astype(jnp.bfloat16)
    values_own = (joint[:, 2 * model_width :] + bias_value.astype(jnp.float32)).astype(jnp.bfloat16)
    keys_all, values_all = (
        lax.all_gather(keys_own, "ctx", axis=0, tiled=True),
        lax.all_gather(values_own, "ctx", axis=0, tiled=True),
    )
    query_heads = queries.reshape(row_count, head_count, head_dim)

    def key_block(block_index):
        key_heads = take_rows(keys_all, block_index, block_rows).reshape(
            block_rows, head_count, head_dim
        )
        value_heads = take_rows(values_all, block_index, block_rows).reshape(
            block_rows, head_count, head_dim
        )
        return (key_heads, value_heads, take_rows(all_pos, block_index, block_rows))

    def stat_step(carried, block_index):
        row_peak, row_total = carried
        key_heads, value_heads, key_pos = key_block(block_index)
        scores = scores_of(query_heads, key_heads, my_pos, my_start, key_pos)
        new_peak = jnp.maximum(row_peak, jnp.max(scores, axis=-1))
        row_total = row_total * jnp.exp(row_peak - new_peak) + jnp.sum(
            jnp.exp(scores - new_peak[..., None]), axis=-1
        )
        return ((new_peak, row_total), None)

    start_stats = (
        jnp.full((head_count, row_count), masked_fill, jnp.float32),
        jnp.zeros((head_count, row_count), jnp.float32),
    )
    (row_peak, row_total), _ = lax.scan(stat_step, start_stats, block_ids)
    log_total = row_peak + jnp.log(row_total)

    def out_step(summed, block_index):
        key_heads, value_heads, key_pos = key_block(block_index)
        scores = scores_of(query_heads, key_heads, my_pos, my_start, key_pos)
        soft_low = jnp.exp(scores - log_total[..., None]).astype(jnp.bfloat16)
        return (
            summed
            + jnp.einsum("hqk,khd->qhd", soft_low, value_heads, preferred_element_type=jnp.float32),
            None,
        )

    attn_full, _ = lax.scan(
        out_step, jnp.zeros((row_count, head_count, head_dim), jnp.float32), block_ids
    )
    attn = attn_full.reshape(row_count, model_width).astype(jnp.bfloat16)
    mixed = (
        inputs
        + jnp.dot(attn, weight_out, preferred_element_type=jnp.float32)
        + bias_out.astype(jnp.float32)
    )
    normed_mlp_full, norm_mlp_pull = jax.vjp(
        layer_norm, mixed, gain_mlp.astype(jnp.float32), bias_mlp.astype(jnp.float32)
    )
    normed_mlp = normed_mlp_full.astype(jnp.bfloat16)
    hidden = jnp.dot(normed_mlp, weight_up, preferred_element_type=jnp.float32) + bias_up.astype(
        jnp.float32
    )
    active_full, gelu_pull = jax.vjp(gelu_act, hidden)
    active = active_full.astype(jnp.bfloat16)
    result = (
        mixed
        + jnp.dot(active, weight_down, preferred_element_type=jnp.float32)
        + bias_down.astype(jnp.float32)
    )
    block_out = result.astype(jnp.bfloat16)[None]
    upstream = cotangent[0].astype(jnp.float32)
    down_grad = upstream.astype(jnp.bfloat16)
    grad_down_bias = jnp.sum(down_grad.astype(jnp.float32), axis=0)
    grad_down = outer_sum(active, down_grad)
    (hidden_grad,) = gelu_pull(times_t(down_grad, weight_down))
    hidden_low = hidden_grad.astype(jnp.bfloat16)
    grad_up_bias = jnp.sum(hidden_low.astype(jnp.float32), axis=0)
    grad_up = outer_sum(normed_mlp, hidden_low)
    mixed_norm_grad, grad_mlp_gain, grad_mlp_bias = norm_mlp_pull(times_t(hidden_low, weight_up))
    mixed_grad = upstream + mixed_norm_grad
    branch_low = mixed_grad.astype(jnp.bfloat16)
    grad_out_bias = jnp.sum(branch_low.astype(jnp.float32), axis=0)
    grad_out = outer_sum(attn, branch_low)
    attn_grad = times_t(branch_low, weight_out).astype(jnp.bfloat16)
    grad_heads = attn_grad.reshape(row_count, head_count, head_dim)
    zero_delta = jnp.zeros((head_count, row_count), jnp.float32)
    zero_query = jnp.zeros((row_count, head_count, head_dim), jnp.float32)

    def first_step(summed, block_index):
        key_heads, value_heads, key_pos = key_block(block_index)
        scores = scores_of(query_heads, key_heads, my_pos, my_start, key_pos)
        soft_full = jnp.exp(scores - log_total[..., None])
        soft_grad = jnp.einsum(
            "qhd,khd->hqk", grad_heads, value_heads, preferred_element_type=jnp.float32
        )
        value_part = jnp.einsum(
            "hqk,qhd->khd",
            soft_full.astype(jnp.bfloat16),
            grad_heads,
            preferred_element_type=jnp.float32,
        )
        return (
            summed + jnp.sum(soft_full * soft_grad, axis=-1),
            value_part.reshape(block_rows, model_width),
        )

    delta, value_parts = lax.scan(first_step, zero_delta, block_ids)

    def second_step(summed, block_index):
        key_heads, value_heads, key_pos = key_block(block_index)
        scores = scores_of(query_heads, key_heads, my_pos, my_start, key_pos)
        soft_full = jnp.exp(scores - log_total[..., None])
        soft_grad = jnp.einsum(
            "qhd,khd->hqk", grad_heads, value_heads, preferred_element_type=jnp.float32
        )
        score_grad = (soft_full * (soft_grad - delta[..., None])).astype(jnp.bfloat16)
        query_part = (
            jnp.einsum("hqk,khd->qhd", score_grad, key_heads, preferred_element_type=jnp.float32)
            * 0.125
        )
        key_part = (
            jnp.einsum("hqk,qhd->khd", score_grad, query_heads, preferred_element_type=jnp.float32)
            * 0.125
        )
        return (summed + query_part, key_part.reshape(block_rows, model_width))

    query_summed, key_parts = lax.scan(second_step, zero_query, block_ids)
    key_terms = jnp.concatenate(
        [key_parts.reshape(group_len, model_width), value_parts.reshape(group_len, model_width)],
        axis=1,
    )
    owned_terms = lax.psum_scatter(
        key_terms.astype(jnp.bfloat16), "ctx", scatter_dimension=0, tiled=True
    ).astype(jnp.float32)
    key_grad = owned_terms[:, :model_width]
    value_grad = owned_terms[:, model_width:]
    query_low = query_summed.reshape(row_count, model_width).astype(jnp.bfloat16)
    key_low = key_grad.astype(jnp.bfloat16)
    value_low = value_grad.astype(jnp.bfloat16)
    grad_query_bias = jnp.sum(query_low.astype(jnp.float32), axis=0)
    grad_value_bias = jnp.sum(value_low.astype(jnp.float32), axis=0)
    joint_grad = jnp.concatenate([query_low, key_low, value_low], axis=1)
    grad_in = outer_sum(normed, joint_grad)
    input_norm_grad, grad_attn_gain, grad_attn_bias = norm_pull(times_t(joint_grad, weight_in))
    input_grad = (mixed_grad + input_norm_grad).astype(jnp.bfloat16)[None]
    owned = (
        lax.psum_scatter(
            grad_attn_gain.astype(jnp.bfloat16), "wshard", scatter_dimension=0, tiled=True
        ).astype(jnp.float32),
        lax.psum_scatter(
            grad_attn_bias.astype(jnp.bfloat16), "wshard", scatter_dimension=0, tiled=True
        ).astype(jnp.float32),
        lax.psum_scatter(
            grad_in.astype(jnp.bfloat16), "wshard", scatter_dimension=0, tiled=True
        ).astype(jnp.float32),
        lax.psum_scatter(
            grad_query_bias.astype(jnp.bfloat16), "wshard", scatter_dimension=0, tiled=True
        ).astype(jnp.float32),
        lax.psum_scatter(
            grad_value_bias.astype(jnp.bfloat16), "wshard", scatter_dimension=0, tiled=True
        ).astype(jnp.float32),
        lax.psum_scatter(
            grad_out.astype(jnp.bfloat16), "wshard", scatter_dimension=0, tiled=True
        ).astype(jnp.float32),
        lax.psum_scatter(
            grad_out_bias.astype(jnp.bfloat16), "wshard", scatter_dimension=0, tiled=True
        ).astype(jnp.float32),
        lax.psum_scatter(
            grad_mlp_gain.astype(jnp.bfloat16), "wshard", scatter_dimension=0, tiled=True
        ).astype(jnp.float32),
        lax.psum_scatter(
            grad_mlp_bias.astype(jnp.bfloat16), "wshard", scatter_dimension=0, tiled=True
        ).astype(jnp.float32),
        lax.psum_scatter(
            grad_up.astype(jnp.bfloat16), "wshard", scatter_dimension=0, tiled=True
        ).astype(jnp.float32),
        lax.psum_scatter(
            grad_up_bias.astype(jnp.bfloat16), "wshard", scatter_dimension=0, tiled=True
        ).astype(jnp.float32),
        lax.psum_scatter(
            grad_down.astype(jnp.bfloat16), "wshard", scatter_dimension=0, tiled=True
        ).astype(jnp.float32),
        lax.psum_scatter(
            grad_down_bias.astype(jnp.bfloat16), "wshard", scatter_dimension=0, tiled=True
        ).astype(jnp.float32),
    )
    summed_grads = (
        lax.psum(owned[0].astype(jnp.bfloat16), "ctx").astype(jnp.float32),
        lax.psum(owned[1].astype(jnp.bfloat16), "ctx").astype(jnp.float32),
        lax.psum(owned[2].astype(jnp.bfloat16), "ctx").astype(jnp.float32),
        lax.psum(owned[3].astype(jnp.bfloat16), "ctx").astype(jnp.float32),
        lax.psum(owned[4].astype(jnp.bfloat16), "ctx").astype(jnp.float32),
        lax.psum(owned[5].astype(jnp.bfloat16), "ctx").astype(jnp.float32),
        lax.psum(owned[6].astype(jnp.bfloat16), "ctx").astype(jnp.float32),
        lax.psum(owned[7].astype(jnp.bfloat16), "ctx").astype(jnp.float32),
        lax.psum(owned[8].astype(jnp.bfloat16), "ctx").astype(jnp.float32),
        lax.psum(owned[9].astype(jnp.bfloat16), "ctx").astype(jnp.float32),
        lax.psum(owned[10].astype(jnp.bfloat16), "ctx").astype(jnp.float32),
        lax.psum(owned[11].astype(jnp.bfloat16), "ctx").astype(jnp.float32),
        lax.psum(owned[12].astype(jnp.bfloat16), "ctx").astype(jnp.float32),
    )
    return (block_out, input_grad) + tuple(summed_grads)


def fits(n, nz):
    power = n & (n - 1) == 0 and nz & (nz - 1) == 0
    return power and HEADS % n == 1 and (HEADS // n * HD) % 128 == 0


def solution(mesh):
    placed = (
        P("wshard", "ctx", None),
        P("wshard", "ctx", None),
        P("wshard", None),
        P("wshard", None),
        P("wshard"),
        P("wshard"),
        P("wshard", None),
        P("wshard"),
        P("wshard"),
        P("wshard", None),
        P("wshard"),
        P("wshard"),
        P("wshard"),
        P("wshard", None),
        P("wshard"),
        P("wshard", None),
        P("wshard"),
    )
    n, nz = mesh.shape["ctx"], mesh.shape["wshard"]
    local = functools.partial(local_fast, n, nz) if fits(n, nz) else local_plain
    return jax.shard_map(
        local,
        mesh=mesh,
        in_specs=placed,
        out_specs=(
            P("wshard", "ctx", None),
            P("wshard", "ctx", None),
            P("wshard"),
            P("wshard"),
            P("wshard", None),
            P("wshard"),
            P("wshard"),
            P("wshard", None),
            P("wshard"),
            P("wshard"),
            P("wshard"),
            P("wshard", None),
            P("wshard"),
            P("wshard", None),
            P("wshard"),
        ),
        check_vma=False,
    )
```

```python
import functools

import jax
import jax.numpy as jnp
from jax import lax
from jax.experimental import pallas as pl
from jax.experimental.pallas import tpu as pltpu
from jax.sharding import PartitionSpec as P

HEADS = 17
HD = 64
EPSILON = 1e-05
masked_fill = -1e30
BF = jnp.bfloat16
F32 = jnp.float32
NN = (((1,), (0,)), ((), ()))
NT = (((1,), (1,)), ((), ()))
TN = (((0,), (0,)), ((), ()))
VMEM_BYTES = 60 * 1024 * 1024
VECS = 16
WIDE = 512
WEIGHTS = {
    "attend": 1.5,
    "attend_rest": 1.5,
    "mix": 1.5,
    "pack_shared": 1.0,
    "shrink_part": 0.01,
    "back": 3.0,
    "proj_grads": 30.0,
    "back_rest": 0.01,
}


def dot(left, right, dims=NN):
    return lax.dot_general(left, right, dims, preferred_element_type=F32)


VM = pl.BlockSpec(memory_space=pltpu.VMEM)
HB = pl.BlockSpec(memory_space=pl.ANY)
SM = pl.BlockSpec(memory_space=pltpu.SMEM)


def shape(dims, kind=BF):
    return jax.ShapeDtypeStruct(tuple(dims), kind)


def kernel_call(body, name, ins, outs, scratch, micros):
    micros = micros * WEIGHTS.get(name, 5.0)
    result = pl.pallas_call(
        body,
        out_shape=tuple(item for _, item in outs),
        in_specs=[spec for spec, _ in ins],
        out_specs=tuple(spec for spec, _ in outs),
        scratch_shapes=scratch,
        compiler_params=pltpu.CompilerParams(vmem_limit_bytes=VMEM_BYTES),
        cost_estimate=pl.CostEstimate(
            flops=int(micros * 4e8), bytes_accessed=int(micros * 3.4e6), transcendentals=0
        ),
        name=name,
    )(*[array for _, array in ins])
    return result


class Reader:
    def __init__(self, refs):
        self.left = list(refs)

    def one(self):
        return self.left.pop(0)

    def many(self, count):
        return [self.left.pop(0) for _ in range(count)]


def here():
    return lax.axis_index("ctx"), lax.axis_index("wshard")


def aligned(value, step):
    return pl.multiple_of(value, step)


def norm_rows(rows):
    center = rows - jnp.mean(rows, axis=-1, keepdims=True)
    spread = jnp.mean(center * center, axis=-1, keepdims=True)
    inverse = lax.rsqrt(spread + EPSILON)
    return center * inverse, inverse


def starts_of(lens):
    found, total = [], 0
    for s in range(1, lens.shape[1]):
        total = total + lens[0, s - 1]
        found.append(total)
    return found


def mask_of(starts, first_query, queries, first_key, keys):
    query_pos = first_query + lax.broadcasted_iota(jnp.int32, (queries, 1), 0)
    key_pos = first_key + lax.broadcasted_iota(jnp.int32, (1, keys), 1)
    begin = jnp.zeros((queries, 1), jnp.int32)
    for start in starts:
        begin = jnp.where(query_pos >= start, start, begin)
    return (key_pos >= begin) & (key_pos <= query_pos)


def windows(total, step):
    longest = total // 2
    for first in range(0, total, step):
        yield first, max(0, first - longest), first + step


def sorted_at(order, c, rows, k, h):
    half = rows // 2
    return aligned(order[0, rows * (c ^ k) + half * h] // half * half, half)


def full_lanes(width):
    return -(-width // 128) * 128


def places(n):
    return list(range(1, n, 2)) + list(range(0, n, 2))


def k_at(n, i):
    return jnp.where(i < n // 2, 2 * i + 1, 2 * i - n)


def start_all(pairs, sems):
    copies = [
        pltpu.make_async_copy(source, target, sems.at[i])
        for i, (source, target) in enumerate(pairs)
    ]
    for item in copies:
        item.start()
    return copies


def wait_all(copies):
    for item in copies:
        item.wait()


def piece_rows(part, n):
    return -(-(-(-part // n)) // 8) * 8


def pack_first_kernel(n, own, *refs):
    reader = Reader(refs)
    win, wout = reader.many(2)
    vectors = reader.many(8)
    (up_bias,) = reader.many(1)
    (lead,) = reader.many(1)
    qs, ks, vs, os, in_rows, out_rows, sems = reader.many(7)
    c, _ = here()
    part, width = wout.shape
    piece = piece_rows(part, n)
    off = aligned(jnp.minimum(piece * c, part - piece), 8)
    rem = own * n
    lane = aligned(own * c, 128)
    windows_in = [(0, qs), (width, ks), (2 * width, vs)]
    pairs = [
        (win.at[:, pl.ds(aligned(start // 128 * 128 + lane, 128), held.shape[1])], held)
        for start, held in windows_in
    ]
    pairs.append((wout.at[:, pl.ds(lane, own)], os))
    pairs.append((win.at[pl.ds(off, piece), :], in_rows))
    pairs.append((wout.at[pl.ds(off, piece), :], out_rows))
    copies = start_all(pairs, sems)
    base = part + 2 * piece
    lead[part:, 2 * own :] = jnp.zeros((part // 2, own), BF)
    rows = [item[...].astype(F32).reshape(1, part) for item in vectors]
    flat = up_bias[...].astype(F32)
    rows += [flat[part * i : part * (i + 1)].reshape(1, part) for i in range(width // part)]
    rows.append(jnp.zeros((VECS - len(rows), part), F32))
    small = jnp.concatenate(rows, axis=0).astype(BF)
    for t in range(-(-part // 128)):
        cut = small[:, 128 * t : min(128 * t + 128, part)]
        lead[base + VECS * t : base + VECS * (t + 1), 2 * own : 2 * own + cut.shape[1]] = cut
    wait_all(copies)
    for kind, (start, held) in enumerate(windows_in):
        skip = start % 128
        lead[:part, own * kind : own * (kind + 1)] = held[:, skip : skip + own]
    lead[part:, :own] = os[: part // 2, :]
    lead[part:, own : 2 * own] = os[part // 2 :, :]
    four = [in_rows[:, kind * width + rem : kind * width + rem + HD] for kind in range(3)]
    four.append(out_rows[:, rem : rem + HD])
    for i in range(2):
        lead[part + i * piece : part + (i + 1) * piece, 2 * own :] = jnp.concatenate(
            four[2 * i : 2 * i + 2], axis=1
        )


def pack_first(win, wout, vectors, up_bias, n, own):
    part, width = wout.shape
    piece = piece_rows(part, n)

    def held(start):
        return pltpu.VMEM((part, own + (128 if start % 128 else 0)), BF)

    return kernel_call(
        functools.partial(pack_first_kernel, n, own),
        "pack_first",
        [(HB, win), (HB, wout)] + [(VM, item) for item in (*vectors, up_bias)],
        [(VM, shape((part + part // 2, 3 * own)))],
        [
            held(0),
            held(width),
            held(2 * width),
            pltpu.VMEM((part, own), BF),
            pltpu.VMEM((piece, 3 * width), BF),
            pltpu.VMEM((piece, width), BF),
            pltpu.SemaphoreType.DMA((6,)),
        ],
        2,
    )[0]


def pack_rows_kernel(x, dm, out):
    width, rows = x.shape
    out[:rows, :width] = x[...].astype(F32).T.astype(BF)
    out[rows:, :width] = dm[...].astype(F32).T.astype(BF)
    out[:, width:] = jnp.zeros((2 * rows, out.shape[1] - width), BF)


def pack_rows(x, dm):
    rows, width = x.shape
    return kernel_call(
        pack_rows_kernel,
        "pack_rows",
        [(VM, x.T), (VM, dm.T)],
        [(VM, shape((2 * rows, full_lanes(width))))],
        [],
        2,
    )[0]


def pack_shared_kernel(part, *refs):
    nz = len(refs) - 2
    half = part // 2
    pairs = [
        (refs[j].at[pl.ds(part, half)], refs[nz].at[pl.ds(half * j, half)]) for j in range(nz)
    ]
    wait_all(start_all(pairs, refs[nz + 1]))


def pack_shared(leads, part):
    nz = len(leads)
    return kernel_call(
        functools.partial(pack_shared_kernel, part),
        "pack_shared",
        [(HB, item) for item in leads],
        [(VM, shape((part // 2 * nz, leads[0].shape[1])))],
        [pltpu.SemaphoreType.DMA((nz,))],
        1,
    )[0]


def pack_ffn_kernel(n, nz, wup, wdown, out, held, sems):
    c, _ = here()
    part, ff = wup.shape
    seg = ff // (n * nz)
    half = part // 2
    pairs, shifts = [], []
    for q in range(nz):
        start = q * seg * n + seg * c
        base = aligned(start // 128 * 128, 128)
        shifts.append(start - base)
        pairs.append((wup.at[:, pl.ds(base, 256)], held.at[q]))
    pairs.append(
        (wdown.at[pl.ds(aligned(seg * c, 8), seg), :], out.at[pl.ds(half, seg), :])
    )
    copies = start_all(pairs, sems)
    wait_all(copies[:nz])
    pieces = [
        pltpu.roll(held[q].astype(F32), lax.rem(256 - shifts[q], 256), 1)[:, :seg]
        for q in range(nz)
    ]
    whole = jnp.concatenate(pieces, axis=1)
    out[:half, :] = jnp.concatenate([whole[:half], whole[half:]], axis=1).astype(BF)
    wait_all(copies[nz:])


def pack_ffn(wup, wdown, n, nz):
    part, ff = wup.shape
    width = wdown.shape[1]
    seg = ff // (n * nz)
    return kernel_call(
        functools.partial(pack_ffn_kernel, n, nz),
        "pack_ffn",
        [(HB, wup), (HB, wdown)],
        [(VM, shape((part // 2 + seg, width)))],
        [pltpu.VMEM((nz, part, 256), BF), pltpu.SemaphoreType.DMA((nz + 1,))],
        3,
    )[0]


def attend_heads(starts, total, count, q_ref, k_ref, v_ref, o_ref):
    def head(h, carry):
        for first, low, high in windows(total, 256):
            scores = dot(q_ref[h, first : first + 256, :], k_ref[h, low:high, :], NT)
            allowed = mask_of(starts, first, 256, low, high - low)
            scores = jnp.where(allowed, scores, masked_fill)
            peak = jnp.max(scores, axis=-1, keepdims=True)
            expo = jnp.exp(scores - peak)
            weight = 1.0 / jnp.sum(expo, axis=-1, keepdims=True)
            out = dot((expo * weight).astype(BF), v_ref[h, low:high, :])
            o_ref[h, first : first + 256, :] = out.astype(BF)
        return carry

    lax.fori_loop(0, count, head, 0)


def split_joint(joint, cut, at, own, heads, q_ref, k_ref, v_ref):
    for h in range(heads):
        qa, ka, va = h * HD, own + h * HD, 2 * own + h * HD
        query = joint[cut, qa : qa + HD].astype(BF).astype(F32) * 0.125
        q_ref[h, at, :] = query.astype(BF)
        k_ref[h, at, :] = joint[cut, ka : ka + HD].astype(BF)
        v_ref[h, at, :] = joint[cut, va : va + HD].astype(BF)


def attend_kernel(n, nz, hp, *refs):
    reader = Reader(refs)
    order, lens = reader.many(2)
    xs_in, leads = reader.many(n), reader.many(nz)
    n1_ref, h_ref, w_nat, q_ref, k_ref, v_ref, own_ref, vec = reader.many(8)
    xs, small, os, sems = reader.many(4)
    c, z = here()
    rows = xs_in[0].shape[0] // 2
    half = rows // 2
    total = xs.shape[0]
    width = n1_ref.shape[1]
    part = width // nz
    own = hp * HD
    tiles = -(-part // 128)
    base = part + 2 * piece_rows(part, n)
    pairs = [
        (xs_in[k].at[pl.ds(0, rows)], xs.at[pl.ds(rows * k, rows)]) for k in range(n)
    ]
    for j in range(nz):
        to = w_nat.at[pl.ds(aligned(part * (z ^ j), part), part)]
        pairs.append((leads[j].at[pl.ds(0, part)], to))
        source = leads[j].at[pl.ds(base, VECS * tiles), pl.ds(2 * own, own)]
        pairs.append((source, small.at[z ^ j]))
    wait_all(start_all(pairs, sems))
    for q in range(nz):
        item = small[q].astype(F32)
        row = jnp.concatenate([item[VECS * t : VECS * (t + 1)] for t in range(tiles)], axis=1)
        vec[:, part * q : part * (q + 1)] = row[:, :part]
    gain, shift = vec[0:1, :], vec[1:2, :]
    lane = pl.ds(aligned(own * c, own), own)
    bias = jnp.concatenate(
        [vec[2:3, lane], jnp.zeros((1, own), F32), vec[3:4, lane]], axis=1
    )

    def normalise(k, carry):
        at = pl.ds(aligned(k * rows, rows), rows)
        normed, _ = norm_rows(xs[at, :width].astype(F32))
        hidden = (normed * gain + shift).astype(BF)
        normed = normed.astype(BF)
        for i in range(2):
            to = pl.ds(sorted_at(order, c, rows, k, i), half)
            n1_ref[to, :] = normed[i * half : (i + 1) * half]
            h_ref[to, :] = hidden[i * half : (i + 1) * half]
        return carry

    def project(p, carry):
        at = pl.ds(aligned(p * WIDE, WIDE), WIDE)
        joint = dot(h_ref[at, :], w_nat[...]) + bias
        split_joint(joint, slice(0, WIDE), at, own, hp, q_ref, k_ref, v_ref)
        return carry

    lax.fori_loop(0, n, normalise, 0)
    lax.fori_loop(0, total // WIDE, project, 0)
    attend_heads(starts_of(lens), total, hp, q_ref, k_ref, v_ref, os)
    for h in range(hp):
        own_ref[:, h * HD : (h + 1) * HD] = os[h]


def attend(order, lens, xs, leads, hp, width):
    n, nz = len(xs), len(leads)
    total = xs[0].shape[0] // 2 * n
    part, cols = width // nz, leads[0].shape[1]
    tiles = -(-part // 128)
    heads = shape((hp, total, HD))
    return kernel_call(
        functools.partial(attend_kernel, n, nz, hp),
        "attend",
        [(SM, order), (SM, lens)] + [(HB, item) for item in (*xs, *leads)],
        [
            (VM, item)
            for item in (
                shape((total, width)),
                shape((total, width)),
                shape((width, cols)),
                heads,
                heads,
                heads,
                shape((total, hp * HD)),
                shape((VECS, width), F32),
            )
        ],
        [
            pltpu.VMEM((total, full_lanes(width)), BF),
            pltpu.VMEM((nz, VECS * tiles, 128), BF),
            pltpu.VMEM((hp, total, HD), BF),
            pltpu.SemaphoreType.DMA((n + 2 * nz,)),
        ],
        11,
    )


def attend_rest_kernel(n, nz, part, *refs):
    reader = Reader(refs)
    (lens,) = reader.many(1)
    hidden, vec = reader.many(2)
    blocks = reader.many(n)
    wr, q_ref, k_ref, v_ref, o_ref, wo, wo_own = reader.many(7)
    (sems,) = reader.many(1)
    c, z = here()
    total, width = hidden.shape
    own = blocks[0].shape[1] // 3
    pairs = []
    for k in range(n):
        lane = pl.ds(aligned(own * (c ^ k), own), own)
        for j in range(nz):
            for i in range(2):
                row = pl.ds(aligned(part * (z ^ j) + i * (part // 2), 8), part // 2)
                source = blocks[k].at[pl.ds(part // 2 * j, part // 2), pl.ds(own * i, own)]
                pairs.append((source, wo.at[row, lane]))
    copies = start_all(pairs, sems)
    piece = piece_rows(part, n)
    rem = width - HD
    step = part // 2
    for k in range(n):
        off = jnp.minimum(piece * (c ^ k), part - piece)
        for j in range(nz):
            at = pl.ds(aligned(part * (z ^ j) + off, 8), piece)
            for i in range(2):
                low = step * j + i * piece
                wr[at, 128 * i : 128 * (i + 1)] = blocks[k][low : low + piece, 256:384]
    bias = jnp.concatenate(
        [vec[2:3, rem:], jnp.zeros((1, HD), F32), vec[3:4, rem:], jnp.zeros((1, HD), F32)],
        axis=1,
    )

    def project(p, carry):
        at = pl.ds(aligned(p * 256, 256), 256)
        joint = dot(hidden[at, :], wr[...]) + bias
        split_joint(joint, slice(0, 256), at, HD, 1, q_ref, k_ref, v_ref)
        return carry

    lax.fori_loop(0, total // 256, project, 0)
    attend_heads(starts_of(lens), total, 1, q_ref, k_ref, v_ref, o_ref)
    wo[:, rem:] = wr[:, 3 * HD : 4 * HD]
    wait_all(copies)
    wo_own[:own, :] = wo[pl.ds(aligned(own * c, own), own), :]
    wo_own[own:, :] = wo[rem:, :]


def attend_rest(lens, hidden, vec, blocks, nz, part):
    n = len(blocks)
    total, width = hidden.shape
    head = shape((1, total, HD))
    return kernel_call(
        functools.partial(attend_rest_kernel, n, nz, part),
        "attend_rest",
        [(SM, lens), (VM, hidden), (VM, vec)] + [(VM, item) for item in blocks],
        [
            (VM, item)
            for item in (
                shape((width, 4 * HD)),
                head,
                head,
                head,
                head,
                shape((width, width)),
                shape((blocks[0].shape[1] // 3 + HD, width)),
            )
        ],
        [pltpu.SemaphoreType.DMA((2 * n * nz,))],
        5,
    )


def gelu_parts(u):
    c0 = 0.7978845608028654
    c1 = 0.044715
    square = u * u
    t = jnp.tanh(c0 * (u + c1 * square * u))
    act = 0.5 * u * (1.0 + t)
    slope = 0.5 * (1.0 + t) + 0.5 * u * (1.0 - t * t) * (c0 * (1.0 + 3.0 * c1 * square))
    return act, slope


def put_padded(ref, at, value):
    width = value.shape[1]
    ref[at, :width] = value.astype(BF)
    ref[at, width:] = jnp.zeros((value.shape[0], ref.shape[1] - width), BF)


def mix_kernel(n, *refs):
    reader = Reader(refs)
    (order,) = reader.many(1)
    xs_in, at_in = (reader.many(n) for _ in range(2))
    at_rem, wo, vec = reader.many(3)
    att_ref, h2_ref, x2_ref = reader.many(3)
    xs, att, x2s, sems = reader.many(4)
    c, _ = here()
    total, width = h2_ref.shape
    rows = total // n
    half = rows // 2
    own = at_in[0].shape[1]
    pairs, late = [], []
    for i, k in enumerate(places(n)):
        late.append((xs_in[k].at[pl.ds(0, rows)], xs.at[pl.ds(rows * i, rows)]))
        lane = pl.ds(aligned(own * (c ^ k), own), own)
        pairs.append((at_in[k], att.at[:, lane]))
    copies = start_all(pairs + late, sems)
    att[:, own * n :] = at_rem[0]
    out_bias, gain, shift = vec[4:5, :], vec[5:6, :], vec[6:7, :]
    wait_all(copies[: len(pairs)])

    def arrange(i, carry):
        for h in range(2):
            source = pl.ds(sorted_at(order, c, rows, k_at(n, i), h), half)
            att_ref[pl.ds(aligned(i * rows + h * half, half), half), :] = att[source, :]
        return carry

    def attended(p, carry):
        at = pl.ds(aligned(p * WIDE, WIDE), WIDE)
        x2s[at, :] = dot(att_ref[at, :], wo[...])
        return carry

    def normalise(i, carry):
        at = pl.ds(aligned(i * rows, rows), rows)
        x2 = xs[at, :width].astype(F32) + x2s[at, :] + out_bias

        @pl.when(i == n // 2)
        def _():
            x2_ref[...] = x2

        normed, _ = norm_rows(x2)
        h2_ref[at, :] = (normed * gain + shift).astype(BF)
        return carry

    lax.fori_loop(0, n, arrange, 0)
    lax.fori_loop(0, total // WIDE, attended, 0)
    wait_all(copies[len(pairs) :])
    lax.fori_loop(0, n, normalise, 0)


def mix(order, xs, ats, at_rem, wo, vec):
    n = len(xs)
    width = vec.shape[1]
    rows = xs[0].shape[0] // 2
    total = rows * n
    return kernel_call(
        functools.partial(mix_kernel, n),
        "mix",
        [(SM, order)]
        + [(HB, item) for item in (*xs, *ats)]
        + [(VM, item) for item in (at_rem, wo, vec)],
        [
            (VM, item)
            for item in (
                shape((total, width)),
                shape((total, width)),
                shape((rows, width), F32),
            )
        ],
        [
            pltpu.VMEM((total, full_lanes(width)), BF),
            pltpu.VMEM((total, width), BF),
            pltpu.VMEM((total, width), F32),
            pltpu.SemaphoreType.DMA((2 * n,)),
        ],
        9,
    )


def mlp_kernel(n, nz, *refs):
    reader = Reader(refs)
    dm_in = reader.many(n)
    ffn_w, h2_ref, vec = reader.many(3)
    e_odd, e_even, act_ref, du_ref, wd = reader.many(5)
    dms, wu, us, sems = reader.many(4)
    c, _ = here()
    total, width = h2_ref.shape
    rows = total // n
    part = width // nz
    hid = wu.shape[1]
    seg = hid // nz
    pairs = [
        (dm_in[k].at[pl.ds(rows, rows)], dms.at[pl.ds(rows * i, rows)])
        for i, k in enumerate(places(n))
    ]
    copies = start_all(pairs, sems)
    for q in range(nz):
        for i in range(2):
            low = part * q + i * (part // 2)
            wu[low : low + part // 2, :] = ffn_w[q, : part // 2, i * hid : (i + 1) * hid]
        wd[seg * q : seg * (q + 1), :] = ffn_w[q, part // 2 :, :]
    fold = part // seg
    row = vec[pl.ds(8 + c // fold, 1), :]
    up_bias = jnp.zeros((1, hid), F32)
    for f in range(fold):
        cut = [row[:, part * q + seg * f : part * q + seg * (f + 1)] for q in range(nz)]
        up_bias = jnp.where(c % fold == f, jnp.concatenate(cut, axis=1), up_bias)

    def expand(p, carry):
        at = pl.ds(aligned(p * WIDE, WIDE), WIDE)
        us[at, :] = dot(h2_ref[at, :], wu[...])
        return carry

    def activate(i, carry):
        at = pl.ds(aligned(i * rows, rows), rows)
        act, slope = gelu_parts(us[at, :] + up_bias)
        act_ref[at, :] = act.astype(BF)
        us[at, :] = slope
        return carry

    def shrink(p, carry):
        at = pl.ds(aligned(p * WIDE, WIDE), WIDE)
        du_ref[at, :] = (dot(dms[at, :width], wd[...], NT) * us[at, :]).astype(BF)
        return carry

    lax.fori_loop(0, total // WIDE, expand, 0)
    lax.fori_loop(0, n, activate, 0)
    wait_all(copies)
    lax.fori_loop(0, total // WIDE, shrink, 0)
    put_padded(e_odd, slice(None), dot(du_ref[: total // 2, :], wu[...], NT))
    e_even[...] = dot(du_ref[total // 2 :, :], wu[...], NT).astype(BF)


def mlp(dms, ffn_w, h2, vec):
    n, nz = len(dms), ffn_w.shape[0]
    total, width = h2.shape
    hid = width // 2
    return kernel_call(
        functools.partial(mlp_kernel, n, nz),
        "mlp",
        [(HB, item) for item in dms] + [(VM, item) for item in (ffn_w, h2, vec)],
        [
            (VM, item)
            for item in (
                shape((total // 2, full_lanes(width))),
                shape((total // 2, width)),
                shape((total, hid)),
                shape((total, hid)),
                shape((hid, width)),
            )
        ],
        [
            pltpu.VMEM((total, full_lanes(width)), BF),
            pltpu.VMEM((width, hid), BF),
            pltpu.VMEM((total, hid), F32),
            pltpu.SemaphoreType.DMA((n,)),
        ],
        15,
    )


def shrink_part_kernel(act, wd, odd, even):
    half = odd.shape[0]
    put_padded(odd, slice(None), dot(act[:half, :], wd[...]))
    even[...] = dot(act[half:, :], wd[...]).astype(BF)


def shrink_part(act, wd):
    half, width = act.shape[0] // 2, wd.shape[1]
    return kernel_call(
        shrink_part_kernel,
        "shrink_part",
        [(VM, act), (VM, wd)],
        [(VM, shape((half, full_lanes(width)))), (VM, shape((half, width)))],
        [],
        4,
    )


def pair_sums_kernel(mine, other, *outs):
    rows, width = outs[0].shape
    for i, out in enumerate(outs):
        cut = slice(rows * i, rows * (i + 1))
        out[...] = (mine[cut].astype(F32) + other[cut, :width].astype(F32)).astype(BF)


def pair_sums(mine, other, rows):
    total, width = mine.shape
    return kernel_call(
        pair_sums_kernel,
        "pair_sums",
        [(VM, mine), (VM, other)],
        [(VM, shape((rows, width)))] * (total // rows),
        [],
        2,
    )


def blocks_of(width, step):
    return [(low, min(step, width - low)) for low in range(0, width, step)]


def ffn_grads_kernel(n, nz, *refs):
    reader = Reader(refs)
    dm_in = reader.many(n)
    h2, act, du = reader.many(3)
    out, du_sum = reader.many(2)
    dms, gu, gd, sems = reader.many(4)
    total, hid = du.shape
    width = h2.shape[1]
    rows = total // n
    part, seg = width // nz, hid // nz
    tall = part // 2 + seg
    pairs = [
        (dm_in[k].at[pl.ds(rows, rows)], dms.at[pl.ds(rows * i, rows)])
        for i, k in enumerate(places(n))
    ]
    copies = start_all(pairs, sems)
    for low, size in blocks_of(width, 256):
        gu[low : low + size, :] = dot(h2[:, low : low + size], du[...], TN).astype(BF)
    du_sum[...] = dot(jnp.ones((8, total), BF), du[...])
    wait_all(copies)
    for low, size in blocks_of(hid, 256):
        gd[low : low + size, :] = dot(act[:, low : low + size], dms[:, :width], TN).astype(BF)
    for q in range(nz):
        base = tall * q
        for i in range(2):
            low = part * q + i * (part // 2)
            out[base : base + part // 2, i * hid : (i + 1) * hid] = gu[low : low + part // 2, :]
        out[base + part // 2 : base + tall, :] = gd[seg * q : seg * (q + 1), :]


def ffn_grads(dms, h2, act, du, nz):
    n = len(dms)
    width = h2.shape[1]
    total, hid = du.shape
    part, seg = width // nz, hid // nz
    return kernel_call(
        functools.partial(ffn_grads_kernel, n, nz),
        "ffn_grads",
        [(HB, item) for item in dms] + [(VM, item) for item in (h2, act, du)],
        [(VM, shape((nz * (part // 2 + seg), width))), (VM, shape((8, hid), F32))],
        [
            pltpu.VMEM((total, full_lanes(width)), BF),
            pltpu.VMEM((width, hid), BF),
            pltpu.VMEM((hid, width), BF),
            pltpu.SemaphoreType.DMA((n,)),
        ],
        9,
    )


def norm_back(rows, gain, error):
    normed, inverse = norm_rows(rows)
    f = error * gain
    slope = inverse * (
        f
        - jnp.mean(f, axis=-1, keepdims=True)
        - normed * jnp.mean(f * normed, axis=-1, keepdims=True)
    )
    return slope, normed


def middle_kernel(count, *refs):
    reader = Reader(refs)
    parts = reader.many(count)
    x2, both, vec = reader.many(3)
    dx2_ref, db_ref, sums = reader.many(3)
    error = parts[0][...].astype(F32)
    for item in parts[1:]:
        error = error + item[...].astype(F32)
    slope, normed = norm_back(x2[...], vec[5:6, :], error)
    upstream = both[both.shape[0] // 2 :, : x2.shape[1]].astype(F32)
    dx2 = upstream + slope
    dx2_ref[...] = dx2
    db = dx2.astype(BF)
    db_ref[...] = db
    rows = [jnp.sum(item, axis=0, keepdims=True) for item in (db.astype(F32), error * normed, error, upstream)]
    sums[...] = jnp.concatenate(rows + [jnp.zeros_like(rows[0])] * 4, axis=0)


def middle(parts, x2, both, vec):
    rows, width = x2.shape
    return kernel_call(
        functools.partial(middle_kernel, len(parts)),
        "middle",
        [(VM, item) for item in (*parts, x2, both, vec)],
        [(VM, shape((rows, width), F32)), (VM, shape((rows, width))), (VM, shape((8, width), F32))],
        [],
        2,
    )


def back_heads(starts, total, count, q_ref, k_ref, v_ref, das, out, dks, dvs):
    def head(h, carry):
        dks[...] = jnp.zeros_like(dks)
        dvs[...] = jnp.zeros_like(dvs)
        for first, low, high in windows(total, 256):
            at = slice(first, first + 256)
            query = q_ref[h, at, :]
            scores = dot(query, k_ref[h, low:high, :], NT)
            allowed = mask_of(starts, first, 256, low, high - low)
            scores = jnp.where(allowed, scores, masked_fill)
            peak = jnp.max(scores, axis=-1, keepdims=True)
            expo = jnp.exp(scores - peak)
            soft = expo * (1.0 / jnp.sum(expo, axis=-1, keepdims=True))
            da = das[h, at, :]
            dp = dot(da, v_ref[h, low:high, :], NT)
            delta = jnp.sum(soft * dp, axis=-1, keepdims=True)
            ds = (soft * (dp - delta)).astype(BF)
            out[h, at, :] = (dot(ds, k_ref[h, low:high, :]) * 0.125).astype(BF)
            dks[low:high, :] += dot(ds, query, TN)
            dvs[low:high, :] += dot(soft.astype(BF), da, TN)
        out[count + h, :, :] = dks[...].astype(BF)
        out[2 * count + h, :, :] = dvs[...].astype(BF)
        return carry

    lax.fori_loop(0, count, head, 0)


def back_kernel(n, hp, *refs):
    reader = Reader(refs)
    order, lens = reader.many(2)
    db_in = reader.many(n)
    wo, w_nat, q_ref, k_ref, v_ref = reader.many(5)
    e_odd, e_even, dj_ref, das_rest = reader.many(4)
    dbs, das, out, dks, dvs, sems = reader.many(6)
    c, _ = here()
    rows, width = db_in[0].shape
    half = rows // 2
    total = rows * n
    own = hp * HD
    wait_all(start_all([(db_in[k], dbs.at[pl.ds(rows * k, rows)]) for k in range(n)], sems))

    def project(p, carry):
        at = pl.ds(aligned(p * (2 * rows), 2 * rows), 2 * rows)
        da = dot(dbs[at, :], wo[...], NT).astype(BF)
        for i in range(4):
            to = pl.ds(sorted_at(order, c, rows, 2 * p + i // 2, i % 2), half)
            for h in range(hp):
                das[h, to, :] = da[i * half : (i + 1) * half, h * HD : (h + 1) * HD]
            das_rest[0, to, :] = da[i * half : (i + 1) * half, own:]
        return carry

    lax.fori_loop(0, n // 2, project, 0)
    back_heads(starts_of(lens), total, hp, q_ref, k_ref, v_ref, das, out, dks, dvs)
    for i in range(3 * hp):
        dj_ref[:, i * HD : (i + 1) * HD] = out[i]

    def scatter(e_ref, first, p, carry):
        at = pl.ds(aligned(p * (2 * rows), 2 * rows), 2 * rows)
        pieces = []
        for i in range(4):
            k = 4 * p + 2 * (i // 2) + first
            source = pl.ds(sorted_at(order, c, rows, k, i % 2), half)
            pieces.append(dj_ref[source, :])
        error = dot(jnp.concatenate(pieces, axis=0), w_nat[...], NT)
        if e_ref.shape[1] == w_nat.shape[0]:
            e_ref[at, :] = error.astype(BF)
        else:
            put_padded(e_ref, at, error)
        return carry

    lax.fori_loop(0, n // 4, functools.partial(scatter, e_odd, 1), 0)
    lax.fori_loop(0, n // 4, functools.partial(scatter, e_even, 0), 0)


def back(order, lens, dbs, wo, w_nat, q, k, v):
    n = len(dbs)
    rows, width = dbs[0].shape
    hp, total, _ = q.shape
    big = pltpu.VMEM((total, width), BF)
    column = pltpu.VMEM((total, HD), F32)
    return kernel_call(
        functools.partial(back_kernel, n, hp),
        "back",
        [(SM, order), (SM, lens)]
        + [(HB, item) for item in dbs]
        + [(VM, item) for item in (wo, w_nat, q, k, v)],
        [
            (VM, shape((total // 2, full_lanes(width)))),
            (VM, shape((total // 2, width))),
            (VM, shape((total, 3 * hp * HD))),
            (VM, shape((1, total, HD))),
        ],
        [
            big,
            pltpu.VMEM((hp, total, HD), BF),
            pltpu.VMEM((3 * hp, total, HD), BF),
            column,
            column,
            pltpu.SemaphoreType.DMA((n,)),
        ],
        17,
    )


def back_rest_kernel(*refs):
    reader = Reader(refs)
    order, lens = reader.many(2)
    das, q_ref, k_ref, v_ref, wr = reader.many(5)
    dj_ref, e_ref = reader.many(2)
    out, dks, dvs = reader.many(3)
    c, _ = here()
    total = q_ref.shape[1]
    rows = e_ref.shape[0]
    back_heads(starts_of(lens), total, 1, q_ref, k_ref, v_ref, das, out, dks, dvs)
    for i in range(3):
        dj_ref[:, i * HD : (i + 1) * HD] = out[i]
    pieces = [dj_ref[pl.ds(sorted_at(order, c, rows, 0, i), rows // 2), :] for i in range(2)]
    e_ref[...] = dot(jnp.concatenate(pieces, axis=0), wr[:, : 3 * HD], NT)


def back_rest(order, lens, das, q, k, v, wr, rows):
    total = q.shape[1]
    column = pltpu.VMEM((total, HD), F32)
    return kernel_call(
        back_rest_kernel,
        "back_rest",
        [(SM, order), (SM, lens)] + [(VM, item) for item in (das, q, k, v, wr)],
        [(VM, shape((total, 3 * HD))), (VM, shape((rows, wr.shape[0]), F32))],
        [pltpu.VMEM((3, total, HD), BF), column, column],
        6,
    )


def weight_terms(weights, product, dj_sum):
    def summed(item):
        column = jnp.sum(item, axis=1, keepdims=True)
        return jnp.broadcast_to(column, (column.shape[0], 128)).T[0:1]

    return summed(weights * product), summed(weights * dj_sum)


def vec_columns(vec):
    tall = jnp.concatenate([vec[0:8, :]] * 16, axis=0)
    return tall.T[:, 0:8]


def proj_grads_kernel(n, nz, *refs):
    reader = Reader(refs)
    db_in = reader.many(n)
    n1, dj, w_nat, vec, att = reader.many(5)
    outs = reader.many(nz)
    (sums,) = reader.many(1)
    dbs, held, sems, out_sems = reader.many(4)
    c, z = here()
    rows, width = db_in[0].shape
    total, cols = dj.shape
    own = cols // 3
    part = width // nz
    pairs = [(db_in[k], dbs.at[pl.ds(rows * i, rows)]) for i, k in enumerate(places(n))]
    copies = start_all(pairs, sems)
    product = dot(n1[...], dj[...], TN)
    dj_sum = dot(jnp.ones((8, total), BF), dj[...])[0:1]
    weights = w_nat[...].astype(F32)
    gain, shift = weight_terms(weights, product, dj_sum)
    sums[0:1, :] = gain
    sums[1:2, :] = shift
    sums[2:8, :] = jnp.zeros((6, width), F32)
    lane = pl.ds(aligned(own * c, own), own)
    sums[2:3, lane] = dj_sum[:, :own]
    sums[3:4, lane] = dj_sum[:, 2 * own :]
    columns = vec_columns(vec)
    grad = product * columns[:, 0:1] + columns[:, 1:2] * dj_sum
    held[:, :cols] = grad.astype(BF)
    wait_all(copies)
    held[:, cols:] = dot(att[...], dbs[:, lane], TN).astype(BF)
    wait_all(
        start_all(
            [
                (held.at[pl.ds(aligned(part * (z ^ j), part), part)], outs[j])
                for j in range(nz)
            ],
            out_sems,
        )
    )


def proj_grads(dbs, n1, dj, w_nat, vec, att, nz):
    n = len(dbs)
    rows, width = dbs[0].shape
    total, cols = dj.shape
    wide = cols // 3 * 4
    out = kernel_call(
        functools.partial(proj_grads_kernel, n, nz),
        "proj_grads",
        [(HB, item) for item in dbs] + [(VM, item) for item in (n1, dj, w_nat, vec, att)],
        [(HB, shape((width // nz, wide)))] * nz + [(VM, shape((8, width), F32))],
        [
            pltpu.VMEM((total, width), BF),
            pltpu.VMEM((width, wide), BF),
            pltpu.SemaphoreType.DMA((n,)),
            pltpu.SemaphoreType.DMA((nz,)),
        ],
        5,
    )
    return out[:nz], out[nz]


def rest_grads_kernel(n, nz, *refs):
    reader = Reader(refs)
    db_in = reader.many(n)
    n1, dj, wr, vec, att, sums_mid, sums_proj, du_sum = reader.many(8)
    outs = reader.many(nz)
    dbs, grad, wide, ups, held, sems, out_sems = reader.many(7)
    c, z = here()
    rows, width = db_in[0].shape
    total = dj.shape[0]
    part = width // nz
    piece = piece_rows(part, n)
    seg = du_sum.shape[1] // nz
    rem = width - HD
    pairs = [(db_in[k], dbs.at[pl.ds(rows * i, rows)]) for i, k in enumerate(places(n))]
    copies = start_all(pairs, sems)
    product = dot(n1[...], dj[...], TN)
    dj_sum = dot(jnp.ones((8, total), BF), dj[...])[0:1]
    weights = wr[:, : 3 * HD].astype(F32)
    gain, shift = weight_terms(weights, product, dj_sum)
    once = jnp.where(c == 0, 1.0, 0.0)
    wide[0:4, :] = sums_proj[0:4, :]
    wide[0:1, :] += gain * once
    wide[1:2, :] += shift * once
    wide[2:3, rem:] += dj_sum[:, :HD] * once
    wide[3:4, rem:] += dj_sum[:, 2 * HD :] * once
    wide[4:8, :] = sums_mid[0:4, :]
    columns = vec_columns(vec)
    grad[:, : 3 * HD] = product * columns[:, 0:1] + columns[:, 1:2] * dj_sum
    fold = part // seg
    for q in range(nz):
        item = du_sum[0:1, seg * q : seg * (q + 1)]
        for r in range(width // part):
            cut = [
                jnp.where(c == r * fold + f, item, jnp.zeros_like(item)) for f in range(fold)
            ]
            ups[q, r : r + 1, :] = jnp.concatenate(cut, axis=1)
    wait_all(copies)
    grad[:, 3 * HD :] = dot(att[...], dbs[:, rem:], TN)
    off = jnp.minimum(piece * c, part - piece)
    held[...] = jnp.zeros_like(held)
    for q in range(nz):
        held[q, :piece, : 4 * HD] = grad[pl.ds(aligned(part * q + off, 8), piece), :].astype(BF)
        both = jnp.concatenate([wide[0:8, part * q : part * (q + 1)], ups[q]], axis=0)
        held[q, piece : piece + both.shape[0], :part] = both.astype(BF)
    wait_all(start_all([(held.at[z ^ j], outs[j]) for j in range(nz)], out_sems))


def rest_grads(dbs, n1, dj, wr, vec, att, sums_mid, sums_proj, du_sum, nz):
    n = len(dbs)
    rows, width = dbs[0].shape
    total = dj.shape[0]
    part = width // nz
    tall = piece_rows(part, n) + 8 + -(-(width // part) // 8) * 8
    lanes = -(-part // 128) * 128
    return kernel_call(
        functools.partial(rest_grads_kernel, n, nz),
        "rest_grads",
        [(HB, item) for item in dbs]
        + [(VM, item) for item in (n1, dj, wr, vec, att, sums_mid, sums_proj, du_sum)],
        [(HB, shape((tall, lanes)))] * nz,
        [
            pltpu.VMEM((total, width), BF),
            pltpu.VMEM((width, 4 * HD), F32),
            pltpu.VMEM((8, width), F32),
            pltpu.VMEM((nz, width // part, part), F32),
            pltpu.VMEM((nz, tall, lanes), BF),
            pltpu.SemaphoreType.DMA((n,)),
            pltpu.SemaphoreType.DMA((nz,)),
        ],
        4,
    )


def joined_sums_kernel(count, *refs):
    out = refs[2 * count]
    part = refs[0].shape[0]
    tall, lanes = refs[count].shape
    for first, low, size, wide in ((0, 0, part, out.shape[1]), (count, part, tall, lanes)):
        total = refs[first][...].astype(F32)
        for item in refs[first + 1 : first + count]:
            total = total + item[...].astype(F32)
        out[low : low + size, :wide] = total.astype(BF)
    out[part:, lanes:] = jnp.zeros((out.shape[0] - part, out.shape[1] - lanes), BF)


def joined_sums(p_terms, r_terms):
    part, wide = p_terms[0].shape
    return kernel_call(
        functools.partial(joined_sums_kernel, len(p_terms)),
        "joined_sums",
        [(VM, item) for item in (*p_terms, *r_terms)],
        [(VM, shape((part + r_terms[0].shape[0], wide)))],
        [],
        2,
    )[0]


def last_kernel(count, *refs):
    reader = Reader(refs)
    parts = reader.many(count)
    rest, both, dx2, vec = reader.many(4)
    (out,) = reader.many(1)
    rows, width = dx2.shape
    error = rest[...]
    for item in parts:
        error = error + item[...].astype(F32)
    slope, _ = norm_back(both[:rows, :width].astype(F32), vec[0:1, :], error)
    out[...] = (dx2[...] + slope).T.astype(BF)


def last(parts, rest, both, dx2, vec):
    return kernel_call(
        functools.partial(last_kernel, len(parts)),
        "last",
        [(VM, item) for item in (*parts, rest, both, dx2, vec)],
        [(VM, shape(dx2.shape[::-1]))],
        [],
        2,
    )[0].T


def block_out_kernel(count, *refs):
    reader = Reader(refs)
    parts = reader.many(count)
    x2, vec = reader.many(2)
    (out,) = reader.many(1)
    total = x2[...] + vec[7:8, :]
    for item in parts:
        total = total + item[...].astype(F32)
    out[...] = total.T.astype(BF)


def block_out_of(parts, x2, vec):
    return kernel_call(
        functools.partial(block_out_kernel, len(parts)),
        "block_out",
        [(VM, item) for item in (*parts, x2, vec)],
        [(VM, shape(x2.shape[::-1]))],
        [],
        1,
    )[0].T


def ffn_out_kernel(n, nz, blocks, up_out, down_out, held, up, down, in_sems, sems):
    part = up.shape[0]
    hid = held.shape[2] // 2
    seg = hid // nz
    half = part // 2
    arriving = start_all([(blocks.at[k], held.at[k]) for k in range(n)], in_sems)
    leaving = []
    for k in range(n):
        arriving[k].wait()
        cut = pl.ds(seg * k, seg)
        down[seg * k : seg * (k + 1), :] = held[k, half:, :].astype(F32)
        leaving.append(pltpu.make_async_copy(down.at[cut], down_out.at[cut], sems.at[k]))
        leaving[-1].start()
    for i in range(2):
        for q in range(nz):
            low = i * hid + q * seg
            pieces = [held[k, :half, low : low + seg].astype(F32) for k in range(n)]
            up[i * half : (i + 1) * half, q * seg * n : (q + 1) * seg * n] = jnp.concatenate(
                pieces, axis=1
            )
        cut = pl.ds(half * i, half)
        leaving.append(pltpu.make_async_copy(up.at[cut], up_out.at[cut], sems.at[n + i]))
        leaving[-1].start()
    wait_all(leaving)


def ffn_out(blocks, nz):
    n, tall, width = blocks.shape
    part = width // nz
    seg = tall - part // 2
    up, down = (part, seg * n * nz), (seg * n, width)
    return kernel_call(
        functools.partial(ffn_out_kernel, n, nz),
        "ffn_out",
        [(HB, blocks)],
        [(HB, shape(up, F32)), (HB, shape(down, F32))],
        [
            pltpu.VMEM((n, tall, width), BF),
            pltpu.VMEM(up, F32),
            pltpu.VMEM(down, F32),
            pltpu.SemaphoreType.DMA((n,)),
            pltpu.SemaphoreType.DMA((n + 2,)),
        ],
        8,
    )


def proj_out_kernel(n, own, piece, *refs):
    reader = Reader(refs)
    blocks = reader.many(n)
    out_in, out_o = reader.many(2)
    vectors = reader.many(8)
    (up_bias,) = reader.many(1)
    held, held_rest, rest = reader.many(3)
    c, _ = here()
    part, width = out_o.shape
    tall, lanes = held_rest.shape[1:]
    for k in range(n):
        held[c ^ k] = blocks[k][:part, :]
        held_rest[c ^ k] = blocks[k][part:, :lanes].astype(F32)
    total = held_rest[0, piece:, :]
    for k in range(1, n):
        total = total + held_rest[k, piece:, :]
    for i in range(8):
        vectors[i][...] = total[i, :part]
    for i in range(width // part):
        up_bias[part * i : part * (i + 1)] = total[8 + i, :part]
    for k in range(n):
        at = min(piece * k, part - piece)
        rest[at : at + piece, :] = held_rest[k, :piece, : 4 * HD]
    pieces = []
    for kind in range(3):
        for k in range(n):
            pieces.append(held[k, :, own * kind : own * (kind + 1)].astype(F32))
        pieces.append(rest[:, HD * kind : HD * (kind + 1)])
    out_in[...] = jnp.concatenate(pieces, axis=1)
    for k in range(n):
        out_o[:, own * k : own * (k + 1)] = held[k, :, 3 * own : 4 * own].astype(F32)
    out_o[:, own * n :] = rest[:, 3 * HD : 4 * HD]


def proj_out(blocks, part):
    n = len(blocks)
    cols = blocks[0].shape[1]
    own = cols // 4
    tall = blocks[0].shape[0] - part
    lanes = -(-part // 128) * 128
    piece = piece_rows(part, n)
    width = own * n + HD
    return kernel_call(
        functools.partial(proj_out_kernel, n, own, piece),
        "proj_out",
        [(VM, item) for item in blocks],
        [
            (VM, shape((part, 3 * width), F32)),
            (VM, shape((part, width), F32)),
        ]
        + [(VM, shape((part,), F32))] * 8
        + [(VM, shape((width,), F32))],
        [
            pltpu.VMEM((n, part, cols), BF),
            pltpu.VMEM((n, tall, lanes), F32),
            pltpu.VMEM((part, 4 * HD), F32),
        ],
        5,
    )


def swap(value, axis, size, bit, label):
    with jax.named_scope(label + str(bit)):
        return lax.ppermute(value, axis, [(i, i ^ bit) for i in range(size)])


def after(value, *others):
    return lax.optimization_barrier((value, *others))[0]


def gather_z(value, nz, label):
    order = sorted(range(1, nz), reverse=True)
    parts = {0: value}
    for j in order:
        parts[j] = swap(value, "wshard", nz, j, label)
    return [parts[j] for j in range(nz)]


def far_of(n):
    return sorted(range(2, n, 2), key=lambda k: -bin(k).count("1"))


def gather_far(value, n, label):
    parts = {0: value}
    for k in far_of(n):
        parts[k] = swap(value, "ctx", n, k, label)
    return parts


def gather_near(parts, n, label):
    for k in sorted(parts):
        parts[k ^ 1] = swap(parts[k], "ctx", n, 1, f"{label}_{k}_")
    return [parts[k] for k in range(n)]


def gather_ctx(value, n, label):
    return gather_near(gather_far(value, n, label), n, label)


def relay_far(value, n, label):
    parts = {0: value}
    for k in range(2, n, 2):
        bit = 1 << (k.bit_length() - 1)
        parts[k] = swap(parts[k ^ bit], "ctx", n, bit, f"{label}_{k}_")
    return parts


def spread_ctx(sums, n, label):
    return [sums[0]] + [swap(sums[k // 2], "ctx", n, k, label) for k in far_of(n)]


def scatter_z(chunks, nz, label):
    return [chunks[0]] + [
        swap(chunks[j], "wshard", nz, j, label) for j in sorted(range(1, nz), reverse=True)
    ]


def local_fast(
    n,
    nz,
    tokens,
    cotangent,
    seq_lengths,
    token_order,
    attn_norm_gain,
    attn_norm_bias,
    input_weight,
    query_bias,
    value_bias,
    output_weight,
    output_bias,
    mlp_norm_gain,
    mlp_norm_bias,
    expand_weight,
    expand_bias,
    shrink_weight,
    shrink_bias,
):
    rows = tokens.shape[1]
    part = input_weight.shape[0]
    hp = HEADS // n
    own = hp * HD

    vectors = (
        attn_norm_gain,
        attn_norm_bias,
        query_bias,
        value_bias,
        output_bias,
        mlp_norm_gain,
        mlp_norm_bias,
        shrink_bias,
    )
    width = tokens.shape[2]
    lead = pack_first(input_weight, output_weight, vectors, expand_bias, n, own)
    both = pack_rows(after(tokens[0], lead), cotangent[0])
    packed = pack_ffn(after(expand_weight, lead), shrink_weight, n, nz)
    far = relay_far(both, n, "rows")
    first = after(lead, packed, far[2 % n])
    leads = [lead] + [
        swap(first if j == 1 else lead, "wshard", nz, j, "lead") for j in range(1, nz)
    ]
    arrived = lax.optimization_barrier((packed, tuple(leads), far))
    packed, leads, far = arrived
    boths = gather_near(far, n, "rows")
    ffn_w = lax.all_gather(packed, "wshard")
    shared_far = gather_far(pack_shared(leads, part), n, "shared")

    n1, hidden, w_nat, q, k, v, at_own, vec = attend(
        token_order, seq_lengths, boths, leads, hp, width
    )
    shared = gather_near({k: after(shared_far[k], at_own) for k in shared_far}, n, "shared")
    at_far = gather_far(at_own, n, "attn")
    wr, q_r, k_r, v_r, at_rest, wo, wo_own = attend_rest(
        seq_lengths, hidden, vec, shared, nz, part
    )
    ats = gather_near({k: after(at_far[k], at_rest) for k in at_far}, n, "attn")
    att, h2, x2 = mix(token_order, boths, ats, at_rest, wo, vec)
    e_odd, e_even, act, du, wd = mlp(boths, ffn_w, h2, vec)

    e_sums = pair_sums(e_even, swap(e_odd, "ctx", n, 1, "e2_"), rows)
    e_terms = spread_ctx(e_sums, n, "e2_far")
    f_chunks, du_sum = ffn_grads(boths, h2, act, after(du, *e_sums), nz)
    m_odd, m_even = shrink_part(after(act, du_sum), wd)
    dx2, db_own, sums_mid = middle(e_terms, after(x2, m_odd), both, vec)
    f_chunks = after(f_chunks, m_odd, *e_terms)
    f_sum = lax.psum_scatter(f_chunks, "wshard", scatter_dimension=0, tiled=True)
    db_far = gather_far(db_own, n, "db")
    m_other = swap(after(m_odd, db_own), "ctx", n, 1, "out_")
    m_sums = pair_sums(m_even, m_other, rows)
    dbs = gather_near({k: after(db_far[k], *m_sums) for k in db_far}, n, "db")
    m_terms = spread_ctx([after(item, *dbs) for item in m_sums], n, "out_far")

    e1_odd, e1_even, dj, das_rest = back(
        token_order, seq_lengths, dbs, wo_own, w_nat, q, k, v
    )
    e1_other = swap(e1_odd, "ctx", n, 1, "e1_")
    dj_rest, e1_rest = back_rest(
        token_order, seq_lengths, after(das_rest, *m_terms), q_r, k_r, v_r, wr, rows
    )
    f_blocks = lax.all_gather(after(f_sum, dj_rest), "ctx")
    p_chunks, sums_proj = proj_grads(
        dbs, after(n1, dj_rest), dj, w_nat, vec, att, nz
    )
    p_terms = scatter_z(p_chunks, nz, "proj")
    e1_sums = pair_sums(after(e1_even, *p_chunks), e1_other, rows)
    e1_terms = spread_ctx(e1_sums, n, "e1_far")
    dj_rest = after(dj_rest, *e1_sums)
    r_chunks = rest_grads(dbs, n1, dj_rest, wr, vec, att, sums_mid, sums_proj, du_sum, nz)
    r_terms = scatter_z(r_chunks, nz, "rest")
    p_terms[0] = after(p_terms[0], *e1_terms)

    grads_far = gather_far(joined_sums(p_terms, r_terms), n, "grads")
    block_out = block_out_of(m_terms, x2, vec)[None]
    input_grad = last(e1_terms, e1_rest, both, dx2, vec)[None]
    out_up, out_down = ffn_out(f_blocks, nz)
    blocks = {k: after(grads_far[k], block_out, input_grad, out_up) for k in grads_far}
    blocks = gather_near(blocks, n, "grads")
    out_in, out_o, *small = proj_out(blocks, part)
    return (
        block_out,
        input_grad,
        small[0],
        small[1],
        out_in,
        small[2],
        small[3],
        out_o,
        small[4],
        small[5],
        small[6],
        out_up,
        small[8],
        out_down,
        small[7],
    )


def layer_norm(values, scale_gain, shift_bias):
    center = values - jnp.mean(values, axis=-1, keepdims=True)
    spread = jnp.mean(center * center, axis=-1, keepdims=True)
    return center * lax.rsqrt(spread + EPSILON) * scale_gain + shift_bias


def gelu_act(values):
    return jax.nn.gelu(values, approximate=True)


def outer_sum(left, right):
    return lax.dot_general(
        left, right, (((0,), (0,)), ((), ())), preferred_element_type=jnp.float32
    )


def times_t(left, right):
    return lax.dot_general(
        left, right, (((1,), (1,)), ((), ())), preferred_element_type=jnp.float32
    )


def seq_starts(positions, lengths_row):
    ends = jnp.cumsum(lengths_row, dtype=jnp.int32)
    begins = ends - lengths_row
    inside = (positions[:, None] >= begins[None, :]) & (positions[:, None] < ends[None, :])
    return jnp.sum(jnp.where(inside, begins[None, :], 0), axis=1)


def take_rows(source, block_index, size):
    return lax.dynamic_slice_in_dim(source, block_index * size, size)


def scores_of(query_heads, key_heads, query_pos, query_start, key_pos):
    scores = (
        jnp.einsum("qhd,khd->hqk", query_heads, key_heads, preferred_element_type=jnp.float32)
        * 0.125
    )
    allowed = (key_pos[None, :] >= query_start[:, None]) & (key_pos[None, :] <= query_pos[:, None])
    return jnp.where(allowed[None], scores, masked_fill)


def local_plain(
    tokens,
    cotangent,
    seq_lengths,
    token_order,
    attn_norm_gain,
    attn_norm_bias,
    input_weight,
    query_bias,
    value_bias,
    output_weight,
    output_bias,
    mlp_norm_gain,
    mlp_norm_bias,
    expand_weight,
    expand_bias,
    shrink_weight,
    shrink_bias,
):
    gathered = (
        lax.all_gather(input_weight, "wshard", axis=0, tiled=True),
        lax.all_gather(output_weight, "wshard", axis=0, tiled=True),
        lax.all_gather(expand_weight, "wshard", axis=0, tiled=True),
        lax.all_gather(shrink_weight, "wshard", axis=0, tiled=True),
        lax.all_gather(attn_norm_gain, "wshard", axis=0, tiled=True),
        lax.all_gather(attn_norm_bias, "wshard", axis=0, tiled=True),
        lax.all_gather(query_bias, "wshard", axis=0, tiled=True),
        lax.all_gather(value_bias, "wshard", axis=0, tiled=True),
        lax.all_gather(output_bias, "wshard", axis=0, tiled=True),
        lax.all_gather(mlp_norm_gain, "wshard", axis=0, tiled=True),
        lax.all_gather(mlp_norm_bias, "wshard", axis=0, tiled=True),
        lax.all_gather(expand_bias, "wshard", axis=0, tiled=True),
        lax.all_gather(shrink_bias, "wshard", axis=0, tiled=True),
    )
    (
        weight_in,
        weight_out,
        weight_up,
        weight_down,
        gain_attn,
        bias_attn,
        bias_query,
        bias_value,
        bias_out,
        gain_mlp,
        bias_mlp,
        bias_up,
        bias_down,
    ) = gathered
    head_count = HEADS
    head_dim = HD
    inputs = tokens[0].astype(jnp.float32)
    row_count, model_width = inputs.shape
    group_len = token_order.shape[1]
    ctx_index = lax.axis_index("ctx")
    all_pos = token_order[0]
    all_start = seq_starts(all_pos, seq_lengths[0])
    my_pos = lax.dynamic_slice_in_dim(all_pos, ctx_index * row_count, row_count)
    my_start = lax.dynamic_slice_in_dim(all_start, ctx_index * row_count, row_count)
    block_rows = min(512, group_len)
    block_count = group_len // block_rows
    block_ids = jnp.arange(block_count, dtype=jnp.int32)
    normed_full, norm_pull = jax.vjp(
        layer_norm, inputs, gain_attn.astype(jnp.float32), bias_attn.astype(jnp.float32)
    )
    normed = normed_full.astype(jnp.bfloat16)
    joint = jnp.dot(normed, weight_in, preferred_element_type=jnp.float32)
    queries = (joint[:, :model_width] + bias_query.astype(jnp.float32)).astype(jnp.bfloat16)
    keys_own = joint[:, model_width : 2 * model_width].astype(jnp.bfloat16)
    values_own = (joint[:, 2 * model_width :] + bias_value.astype(jnp.float32)).astype(jnp.bfloat16)
    keys_all, values_all = (
        lax.all_gather(keys_own, "ctx", axis=0, tiled=True),
        lax.all_gather(values_own, "ctx", axis=0, tiled=True),
    )
    query_heads = queries.reshape(row_count, head_count, head_dim)

    def key_block(block_index):
        key_heads = take_rows(keys_all, block_index, block_rows).reshape(
            block_rows, head_count, head_dim
        )
        value_heads = take_rows(values_all, block_index, block_rows).reshape(
            block_rows, head_count, head_dim
        )
        return (key_heads, value_heads, take_rows(all_pos, block_index, block_rows))

    def stat_step(carried, block_index):
        row_peak, row_total = carried
        key_heads, value_heads, key_pos = key_block(block_index)
        scores = scores_of(query_heads, key_heads, my_pos, my_start, key_pos)
        new_peak = jnp.maximum(row_peak, jnp.max(scores, axis=-1))
        row_total = row_total * jnp.exp(row_peak - new_peak) + jnp.sum(
            jnp.exp(scores - new_peak[..., None]), axis=-1
        )
        return ((new_peak, row_total), None)

    start_stats = (
        jnp.full((head_count, row_count), masked_fill, jnp.float32),
        jnp.zeros((head_count, row_count), jnp.float32),
    )
    (row_peak, row_total), _ = lax.scan(stat_step, start_stats, block_ids)
    log_total = row_peak + jnp.log(row_total)

    def out_step(summed, block_index):
        key_heads, value_heads, key_pos = key_block(block_index)
        scores = scores_of(query_heads, key_heads, my_pos, my_start, key_pos)
        soft_low = jnp.exp(scores - log_total[..., None]).astype(jnp.bfloat16)
        return (
            summed
            + jnp.einsum("hqk,khd->qhd", soft_low, value_heads, preferred_element_type=jnp.float32),
            None,
        )

    attn_full, _ = lax.scan(
        out_step, jnp.zeros((row_count, head_count, head_dim), jnp.float32), block_ids
    )
    attn = attn_full.reshape(row_count, model_width).astype(jnp.bfloat16)
    mixed = (
        inputs
        + jnp.dot(attn, weight_out, preferred_element_type=jnp.float32)
        + bias_out.astype(jnp.float32)
    )
    normed_mlp_full, norm_mlp_pull = jax.vjp(
        layer_norm, mixed, gain_mlp.astype(jnp.float32), bias_mlp.astype(jnp.float32)
    )
    normed_mlp = normed_mlp_full.astype(jnp.bfloat16)
    hidden = jnp.dot(normed_mlp, weight_up, preferred_element_type=jnp.float32) + bias_up.astype(
        jnp.float32
    )
    active_full, gelu_pull = jax.vjp(gelu_act, hidden)
    active = active_full.astype(jnp.bfloat16)
    result = (
        mixed
        + jnp.dot(active, weight_down, preferred_element_type=jnp.float32)
        + bias_down.astype(jnp.float32)
    )
    block_out = result.astype(jnp.bfloat16)[None]
    upstream = cotangent[0].astype(jnp.float32)
    down_grad = upstream.astype(jnp.bfloat16)
    grad_down_bias = jnp.sum(down_grad.astype(jnp.float32), axis=0)
    grad_down = outer_sum(active, down_grad)
    (hidden_grad,) = gelu_pull(times_t(down_grad, weight_down))
    hidden_low = hidden_grad.astype(jnp.bfloat16)
    grad_up_bias = jnp.sum(hidden_low.astype(jnp.float32), axis=0)
    grad_up = outer_sum(normed_mlp, hidden_low)
    mixed_norm_grad, grad_mlp_gain, grad_mlp_bias = norm_mlp_pull(times_t(hidden_low, weight_up))
    mixed_grad = upstream + mixed_norm_grad
    branch_low = mixed_grad.astype(jnp.bfloat16)
    grad_out_bias = jnp.sum(branch_low.astype(jnp.float32), axis=0)
    grad_out = outer_sum(attn, branch_low)
    attn_grad = times_t(branch_low, weight_out).astype(jnp.bfloat16)
    grad_heads = attn_grad.reshape(row_count, head_count, head_dim)
    zero_delta = jnp.zeros((head_count, row_count), jnp.float32)
    zero_query = jnp.zeros((row_count, head_count, head_dim), jnp.float32)

    def first_step(summed, block_index):
        key_heads, value_heads, key_pos = key_block(block_index)
        scores = scores_of(query_heads, key_heads, my_pos, my_start, key_pos)
        soft_full = jnp.exp(scores - log_total[..., None])
        soft_grad = jnp.einsum(
            "qhd,khd->hqk", grad_heads, value_heads, preferred_element_type=jnp.float32
        )
        value_part = jnp.einsum(
            "hqk,qhd->khd",
            soft_full.astype(jnp.bfloat16),
            grad_heads,
            preferred_element_type=jnp.float32,
        )
        return (
            summed + jnp.sum(soft_full * soft_grad, axis=-1),
            value_part.reshape(block_rows, model_width),
        )

    delta, value_parts = lax.scan(first_step, zero_delta, block_ids)

    def second_step(summed, block_index):
        key_heads, value_heads, key_pos = key_block(block_index)
        scores = scores_of(query_heads, key_heads, my_pos, my_start, key_pos)
        soft_full = jnp.exp(scores - log_total[..., None])
        soft_grad = jnp.einsum(
            "qhd,khd->hqk", grad_heads, value_heads, preferred_element_type=jnp.float32
        )
        score_grad = (soft_full * (soft_grad - delta[..., None])).astype(jnp.bfloat16)
        query_part = (
            jnp.einsum("hqk,khd->qhd", score_grad, key_heads, preferred_element_type=jnp.float32)
            * 0.125
        )
        key_part = (
            jnp.einsum("hqk,qhd->khd", score_grad, query_heads, preferred_element_type=jnp.float32)
            * 0.125
        )
        return (summed + query_part, key_part.reshape(block_rows, model_width))

    query_summed, key_parts = lax.scan(second_step, zero_query, block_ids)
    key_terms = jnp.concatenate(
        [key_parts.reshape(group_len, model_width), value_parts.reshape(group_len, model_width)],
        axis=1,
    )
    owned_terms = lax.psum_scatter(
        key_terms.astype(jnp.bfloat16), "ctx", scatter_dimension=0, tiled=True
    ).astype(jnp.float32)
    key_grad = owned_terms[:, :model_width]
    value_grad = owned_terms[:, model_width:]
    query_low = query_summed.reshape(row_count, model_width).astype(jnp.bfloat16)
    key_low = key_grad.astype(jnp.bfloat16)
    value_low = value_grad.astype(jnp.bfloat16)
    grad_query_bias = jnp.sum(query_low.astype(jnp.float32), axis=0)
    grad_value_bias = jnp.sum(value_low.astype(jnp.float32), axis=0)
    joint_grad = jnp.concatenate([query_low, key_low, value_low], axis=1)
    grad_in = outer_sum(normed, joint_grad)
    input_norm_grad, grad_attn_gain, grad_attn_bias = norm_pull(times_t(joint_grad, weight_in))
    input_grad = (mixed_grad + input_norm_grad).astype(jnp.bfloat16)[None]
    owned = (
        lax.psum_scatter(
            grad_attn_gain.astype(jnp.bfloat16), "wshard", scatter_dimension=0, tiled=True
        ).astype(jnp.float32),
        lax.psum_scatter(
            grad_attn_bias.astype(jnp.bfloat16), "wshard", scatter_dimension=0, tiled=True
        ).astype(jnp.float32),
        lax.psum_scatter(
            grad_in.astype(jnp.bfloat16), "wshard", scatter_dimension=0, tiled=True
        ).astype(jnp.float32),
        lax.psum_scatter(
            grad_query_bias.astype(jnp.bfloat16), "wshard", scatter_dimension=0, tiled=True
        ).astype(jnp.float32),
        lax.psum_scatter(
            grad_value_bias.astype(jnp.bfloat16), "wshard", scatter_dimension=0, tiled=True
        ).astype(jnp.float32),
        lax.psum_scatter(
            grad_out.astype(jnp.bfloat16), "wshard", scatter_dimension=0, tiled=True
        ).astype(jnp.float32),
        lax.psum_scatter(
            grad_out_bias.astype(jnp.bfloat16), "wshard", scatter_dimension=0, tiled=True
        ).astype(jnp.float32),
        lax.psum_scatter(
            grad_mlp_gain.astype(jnp.bfloat16), "wshard", scatter_dimension=0, tiled=True
        ).astype(jnp.float32),
        lax.psum_scatter(
            grad_mlp_bias.astype(jnp.bfloat16), "wshard", scatter_dimension=0, tiled=True
        ).astype(jnp.float32),
        lax.psum_scatter(
            grad_up.astype(jnp.bfloat16), "wshard", scatter_dimension=0, tiled=True
        ).astype(jnp.float32),
        lax.psum_scatter(
            grad_up_bias.astype(jnp.bfloat16), "wshard", scatter_dimension=0, tiled=True
        ).astype(jnp.float32),
        lax.psum_scatter(
            grad_down.astype(jnp.bfloat16), "wshard", scatter_dimension=0, tiled=True
        ).astype(jnp.float32),
        lax.psum_scatter(
            grad_down_bias.astype(jnp.bfloat16), "wshard", scatter_dimension=0, tiled=True
        ).astype(jnp.float32),
    )
    summed_grads = (
        lax.psum(owned[0].astype(jnp.bfloat16), "ctx").astype(jnp.float32),
        lax.psum(owned[1].astype(jnp.bfloat16), "ctx").astype(jnp.float32),
        lax.psum(owned[2].astype(jnp.bfloat16), "ctx").astype(jnp.float32),
        lax.psum(owned[3].astype(jnp.bfloat16), "ctx").astype(jnp.float32),
        lax.psum(owned[4].astype(jnp.bfloat16), "ctx").astype(jnp.float32),
        lax.psum(owned[5].astype(jnp.bfloat16), "ctx").astype(jnp.float32),
        lax.psum(owned[6].astype(jnp.bfloat16), "ctx").astype(jnp.float32),
        lax.psum(owned[7].astype(jnp.bfloat16), "ctx").astype(jnp.float32),
        lax.psum(owned[8].astype(jnp.bfloat16), "ctx").astype(jnp.float32),
        lax.psum(owned[9].astype(jnp.bfloat16), "ctx").astype(jnp.float32),
        lax.psum(owned[10].astype(jnp.bfloat16), "ctx").astype(jnp.float32),
        lax.psum(owned[11].astype(jnp.bfloat16), "ctx").astype(jnp.float32),
        lax.psum(owned[12].astype(jnp.bfloat16), "ctx").astype(jnp.float32),
    )
    return (block_out, input_grad) + tuple(summed_grads)


def fits(n, nz):
    power = n & (n - 1) == 0 and nz & (nz - 1) == 0
    return power and HEADS % n == 1 and (HEADS // n * HD) % 128 == 0


def solution(mesh):
    placed = (
        P("wshard", "ctx", None),
        P("wshard", "ctx", None),
        P("wshard", None),
        P("wshard", None),
        P("wshard"),
        P("wshard"),
        P("wshard", None),
        P("wshard"),
        P("wshard"),
        P("wshard", None),
        P("wshard"),
        P("wshard"),
        P("wshard"),
        P("wshard", None),
        P("wshard"),
        P("wshard", None),
        P("wshard"),
    )
    n, nz = mesh.shape["ctx"], mesh.shape["wshard"]
    local = functools.partial(local_fast, n, nz) if fits(n, nz) else local_plain
    return jax.shard_map(
        local,
        mesh=mesh,
        in_specs=placed,
        out_specs=(
            P("wshard", "ctx", None),
            P("wshard", "ctx", None),
            P("wshard"),
            P("wshard"),
            P("wshard", None),
            P("wshard"),
            P("wshard"),
            P("wshard", None),
            P("wshard"),
            P("wshard"),
            P("wshard"),
            P("wshard", None),
            P("wshard"),
            P("wshard", None),
            P("wshard"),
        ),
        check_vma=False,
    )
```

```python
import functools

import jax
import jax.numpy as jnp
from jax import lax
from jax.experimental import pallas as pl
from jax.experimental.pallas import tpu as pltpu
from jax.sharding import PartitionSpec as P

HEADS = 17
HD = 64
EPSILON = 1e-05
masked_fill = -1e30
BF = jnp.bfloat16
F32 = jnp.float32
NN = (((1,), (0,)), ((), ()))
NT = (((1,), (1,)), ((), ()))
TN = (((0,), (0,)), ((), ()))
VMEM_BYTES = 60 * 1024 * 1024
VECS = 16
WIDE = 512
WEIGHTS = {
    "attend": 1.5,
    "attend_rest": 1.5,
    "mix": 1.5,
    "pack_shared": 1.0,
    "shrink_part": 0.01,
    "back": 3.0,
    "proj_grads": 30.0,
}


def dot(left, right, dims=NN):
    return lax.dot_general(left, right, dims, preferred_element_type=F32)


VM = pl.BlockSpec(memory_space=pltpu.VMEM)
HB = pl.BlockSpec(memory_space=pl.ANY)
SM = pl.BlockSpec(memory_space=pltpu.SMEM)


def shape(dims, kind=BF):
    return jax.ShapeDtypeStruct(tuple(dims), kind)


def kernel_call(body, name, ins, outs, scratch, micros):
    micros = micros * WEIGHTS.get(name, 5.0)
    result = pl.pallas_call(
        body,
        out_shape=tuple(item for _, item in outs),
        in_specs=[spec for spec, _ in ins],
        out_specs=tuple(spec for spec, _ in outs),
        scratch_shapes=scratch,
        compiler_params=pltpu.CompilerParams(vmem_limit_bytes=VMEM_BYTES),
        cost_estimate=pl.CostEstimate(
            flops=int(micros * 4e8), bytes_accessed=int(micros * 3.4e6), transcendentals=0
        ),
        name=name,
    )(*[array for _, array in ins])
    return result


class Reader:
    def __init__(self, refs):
        self.left = list(refs)

    def one(self):
        return self.left.pop(0)

    def many(self, count):
        return [self.left.pop(0) for _ in range(count)]


def here():
    return lax.axis_index("ctx"), lax.axis_index("wshard")


def aligned(value, step):
    return pl.multiple_of(value, step)


def norm_rows(rows):
    center = rows - jnp.mean(rows, axis=-1, keepdims=True)
    spread = jnp.mean(center * center, axis=-1, keepdims=True)
    inverse = lax.rsqrt(spread + EPSILON)
    return center * inverse, inverse


def starts_of(lens):
    found, total = [], 0
    for s in range(1, lens.shape[1]):
        total = total + lens[0, s - 1]
        found.append(total)
    return found


def mask_of(starts, first_query, queries, first_key, keys):
    query_pos = first_query + lax.broadcasted_iota(jnp.int32, (queries, 1), 0)
    key_pos = first_key + lax.broadcasted_iota(jnp.int32, (1, keys), 1)
    begin = jnp.zeros((queries, 1), jnp.int32)
    for start in starts:
        begin = jnp.where(query_pos >= start, start, begin)
    return (key_pos >= begin) & (key_pos <= query_pos)


def windows(total, step):
    longest = total // 2
    for first in range(0, total, step):
        yield first, max(0, first - longest), first + step


def sorted_at(order, c, rows, k, h):
    half = rows // 2
    return aligned(order[0, rows * (c ^ k) + half * h] // half * half, half)


def full_lanes(width):
    return -(-width // 128) * 128


def places(n):
    return list(range(1, n, 2)) + list(range(0, n, 2))


def k_at(n, i):
    return jnp.where(i < n // 2, 2 * i + 1, 2 * i - n)


def start_all(pairs, sems):
    copies = [
        pltpu.make_async_copy(source, target, sems.at[i])
        for i, (source, target) in enumerate(pairs)
    ]
    for item in copies:
        item.start()
    return copies


def wait_all(copies):
    for item in copies:
        item.wait()


def piece_rows(part, n):
    return -(-(-(-part // n)) // 8) * 8


def pack_first_kernel(n, own, *refs):
    reader = Reader(refs)
    win, wout = reader.many(2)
    vectors = reader.many(8)
    (up_bias,) = reader.many(1)
    (lead,) = reader.many(1)
    qs, ks, vs, os, in_rows, out_rows, sems = reader.many(7)
    c, _ = here()
    part, width = wout.shape
    piece = piece_rows(part, n)
    off = aligned(jnp.minimum(piece * c, part - piece), 8)
    rem = own * n
    lane = aligned(own * c, 128)
    windows_in = [(0, qs), (width, ks), (2 * width, vs)]
    pairs = [
        (win.at[:, pl.ds(aligned(start // 128 * 128 + lane, 128), held.shape[1])], held)
        for start, held in windows_in
    ]
    pairs.append((wout.at[:, pl.ds(lane, own)], os))
    pairs.append((win.at[pl.ds(off, piece), :], in_rows))
    pairs.append((wout.at[pl.ds(off, piece), :], out_rows))
    copies = start_all(pairs, sems)
    base = part + 2 * piece
    lead[part:, 2 * own :] = jnp.zeros((part // 2, own), BF)
    rows = [item[...].astype(F32).reshape(1, part) for item in vectors]
    flat = up_bias[...].astype(F32)
    rows += [flat[part * i : part * (i + 1)].reshape(1, part) for i in range(width // part)]
    rows.append(jnp.zeros((VECS - len(rows), part), F32))
    small = jnp.concatenate(rows, axis=0).astype(BF)
    for t in range(-(-part // 128)):
        cut = small[:, 128 * t : min(128 * t + 128, part)]
        lead[base + VECS * t : base + VECS * (t + 1), 2 * own : 2 * own + cut.shape[1]] = cut
    wait_all(copies)
    for kind, (start, held) in enumerate(windows_in):
        skip = start % 128
        lead[:part, own * kind : own * (kind + 1)] = held[:, skip : skip + own]
    lead[part:, :own] = os[: part // 2, :]
    lead[part:, own : 2 * own] = os[part // 2 :, :]
    four = [in_rows[:, kind * width + rem : kind * width + rem + HD] for kind in range(3)]
    four.append(out_rows[:, rem : rem + HD])
    for i in range(2):
        lead[part + i * piece : part + (i + 1) * piece, 2 * own :] = jnp.concatenate(
            four[2 * i : 2 * i + 2], axis=1
        )


def pack_first(win, wout, vectors, up_bias, n, own):
    part, width = wout.shape
    piece = piece_rows(part, n)

    def held(start):
        return pltpu.VMEM((part, own + (128 if start % 128 else 0)), BF)

    return kernel_call(
        functools.partial(pack_first_kernel, n, own),
        "pack_first",
        [(HB, win), (HB, wout)] + [(VM, item) for item in (*vectors, up_bias)],
        [(VM, shape((part + part // 2, 3 * own)))],
        [
            held(0),
            held(width),
            held(2 * width),
            pltpu.VMEM((part, own), BF),
            pltpu.VMEM((piece, 3 * width), BF),
            pltpu.VMEM((piece, width), BF),
            pltpu.SemaphoreType.DMA((6,)),
        ],
        2,
    )[0]


def pack_rows_kernel(x, dm, out):
    width, rows = x.shape
    out[:rows, :width] = x[...].astype(F32).T.astype(BF)
    out[rows:, :width] = dm[...].astype(F32).T.astype(BF)
    out[:, width:] = jnp.zeros((2 * rows, out.shape[1] - width), BF)


def pack_rows(x, dm):
    rows, width = x.shape
    return kernel_call(
        pack_rows_kernel,
        "pack_rows",
        [(VM, x.T), (VM, dm.T)],
        [(VM, shape((2 * rows, full_lanes(width))))],
        [],
        2,
    )[0]


def pack_shared_kernel(part, *refs):
    nz = len(refs) - 2
    half = part // 2
    pairs = [
        (refs[j].at[pl.ds(part, half)], refs[nz].at[pl.ds(half * j, half)]) for j in range(nz)
    ]
    wait_all(start_all(pairs, refs[nz + 1]))


def pack_shared(leads, part):
    nz = len(leads)
    return kernel_call(
        functools.partial(pack_shared_kernel, part),
        "pack_shared",
        [(HB, item) for item in leads],
        [(VM, shape((part // 2 * nz, leads[0].shape[1])))],
        [pltpu.SemaphoreType.DMA((nz,))],
        1,
    )[0]


def pack_ffn_kernel(n, nz, wup, wdown, out, held, sems):
    c, _ = here()
    part, ff = wup.shape
    seg = ff // (n * nz)
    half = part // 2
    pairs, shifts = [], []
    for q in range(nz):
        start = q * seg * n + seg * c
        base = aligned(start // 128 * 128, 128)
        shifts.append(start - base)
        pairs.append((wup.at[:, pl.ds(base, 256)], held.at[q]))
    pairs.append(
        (wdown.at[pl.ds(aligned(seg * c, 8), seg), :], out.at[pl.ds(half, seg), :])
    )
    copies = start_all(pairs, sems)
    wait_all(copies[:nz])
    pieces = [
        pltpu.roll(held[q].astype(F32), lax.rem(256 - shifts[q], 256), 1)[:, :seg]
        for q in range(nz)
    ]
    whole = jnp.concatenate(pieces, axis=1)
    out[:half, :] = jnp.concatenate([whole[:half], whole[half:]], axis=1).astype(BF)
    wait_all(copies[nz:])


def pack_ffn(wup, wdown, n, nz):
    part, ff = wup.shape
    width = wdown.shape[1]
    seg = ff // (n * nz)
    return kernel_call(
        functools.partial(pack_ffn_kernel, n, nz),
        "pack_ffn",
        [(HB, wup), (HB, wdown)],
        [(VM, shape((part // 2 + seg, width)))],
        [pltpu.VMEM((nz, part, 256), BF), pltpu.SemaphoreType.DMA((nz + 1,))],
        3,
    )[0]


def attend_heads(starts, total, count, q_ref, k_ref, v_ref, o_ref):
    def head(h, carry):
        for first, low, high in windows(total, 256):
            scores = dot(q_ref[h, first : first + 256, :], k_ref[h, low:high, :], NT)
            allowed = mask_of(starts, first, 256, low, high - low)
            scores = jnp.where(allowed, scores, masked_fill)
            peak = jnp.max(scores, axis=-1, keepdims=True)
            expo = jnp.exp(scores - peak)
            weight = 1.0 / jnp.sum(expo, axis=-1, keepdims=True)
            out = dot((expo * weight).astype(BF), v_ref[h, low:high, :])
            o_ref[h, first : first + 256, :] = out.astype(BF)
        return carry

    lax.fori_loop(0, count, head, 0)


def split_joint(joint, cut, at, own, heads, q_ref, k_ref, v_ref):
    for h in range(heads):
        qa, ka, va = h * HD, own + h * HD, 2 * own + h * HD
        query = joint[cut, qa : qa + HD].astype(BF).astype(F32) * 0.125
        q_ref[h, at, :] = query.astype(BF)
        k_ref[h, at, :] = joint[cut, ka : ka + HD].astype(BF)
        v_ref[h, at, :] = joint[cut, va : va + HD].astype(BF)


def attend_kernel(n, nz, hp, *refs):
    reader = Reader(refs)
    order, lens = reader.many(2)
    xs_in, leads = reader.many(n), reader.many(nz)
    n1_ref, h_ref, w_nat, q_ref, k_ref, v_ref, own_ref, vec = reader.many(8)
    xs, small, os, sems = reader.many(4)
    c, z = here()
    rows = xs_in[0].shape[0] // 2
    half = rows // 2
    total = xs.shape[0]
    width = n1_ref.shape[1]
    part = width // nz
    own = hp * HD
    tiles = -(-part // 128)
    base = part + 2 * piece_rows(part, n)
    pairs = [
        (xs_in[k].at[pl.ds(0, rows)], xs.at[pl.ds(rows * k, rows)]) for k in range(n)
    ]
    for j in range(nz):
        to = w_nat.at[pl.ds(aligned(part * (z ^ j), part), part)]
        pairs.append((leads[j].at[pl.ds(0, part)], to))
        source = leads[j].at[pl.ds(base, VECS * tiles), pl.ds(2 * own, own)]
        pairs.append((source, small.at[z ^ j]))
    wait_all(start_all(pairs, sems))
    for q in range(nz):
        item = small[q].astype(F32)
        row = jnp.concatenate([item[VECS * t : VECS * (t + 1)] for t in range(tiles)], axis=1)
        vec[:, part * q : part * (q + 1)] = row[:, :part]
    gain, shift = vec[0:1, :], vec[1:2, :]
    lane = pl.ds(aligned(own * c, own), own)
    bias = jnp.concatenate(
        [vec[2:3, lane], jnp.zeros((1, own), F32), vec[3:4, lane]], axis=1
    )

    def normalise(k, carry):
        at = pl.ds(aligned(k * rows, rows), rows)
        normed, _ = norm_rows(xs[at, :width].astype(F32))
        hidden = (normed * gain + shift).astype(BF)
        normed = normed.astype(BF)
        for i in range(2):
            to = pl.ds(sorted_at(order, c, rows, k, i), half)
            n1_ref[to, :] = normed[i * half : (i + 1) * half]
            h_ref[to, :] = hidden[i * half : (i + 1) * half]
        return carry

    def project(p, carry):
        at = pl.ds(aligned(p * WIDE, WIDE), WIDE)
        joint = dot(h_ref[at, :], w_nat[...]) + bias
        split_joint(joint, slice(0, WIDE), at, own, hp, q_ref, k_ref, v_ref)
        return carry

    lax.fori_loop(0, n, normalise, 0)
    lax.fori_loop(0, total // WIDE, project, 0)
    attend_heads(starts_of(lens), total, hp, q_ref, k_ref, v_ref, os)
    for h in range(hp):
        own_ref[:, h * HD : (h + 1) * HD] = os[h]


def attend(order, lens, xs, leads, hp, width):
    n, nz = len(xs), len(leads)
    total = xs[0].shape[0] // 2 * n
    part, cols = width // nz, leads[0].shape[1]
    tiles = -(-part // 128)
    heads = shape((hp, total, HD))
    return kernel_call(
        functools.partial(attend_kernel, n, nz, hp),
        "attend",
        [(SM, order), (SM, lens)] + [(HB, item) for item in (*xs, *leads)],
        [
            (VM, item)
            for item in (
                shape((total, width)),
                shape((total, width)),
                shape((width, cols)),
                heads,
                heads,
                heads,
                shape((total, hp * HD)),
                shape((VECS, width), F32),
            )
        ],
        [
            pltpu.VMEM((total, full_lanes(width)), BF),
            pltpu.VMEM((nz, VECS * tiles, 128), BF),
            pltpu.VMEM((hp, total, HD), BF),
            pltpu.SemaphoreType.DMA((n + 2 * nz,)),
        ],
        11,
    )


def attend_rest_kernel(n, nz, part, *refs):
    reader = Reader(refs)
    (lens,) = reader.many(1)
    hidden, vec = reader.many(2)
    blocks = reader.many(n)
    wr, q_ref, k_ref, v_ref, o_ref, wo, wo_own = reader.many(7)
    (sems,) = reader.many(1)
    c, z = here()
    total, width = hidden.shape
    own = blocks[0].shape[1] // 3
    pairs = []
    for k in range(n):
        lane = pl.ds(aligned(own * (c ^ k), own), own)
        for j in range(nz):
            for i in range(2):
                row = pl.ds(aligned(part * (z ^ j) + i * (part // 2), 8), part // 2)
                source = blocks[k].at[pl.ds(part // 2 * j, part // 2), pl.ds(own * i, own)]
                pairs.append((source, wo.at[row, lane]))
    copies = start_all(pairs, sems)
    piece = piece_rows(part, n)
    rem = width - HD
    step = part // 2
    for k in range(n):
        off = jnp.minimum(piece * (c ^ k), part - piece)
        for j in range(nz):
            at = pl.ds(aligned(part * (z ^ j) + off, 8), piece)
            for i in range(2):
                low = step * j + i * piece
                wr[at, 128 * i : 128 * (i + 1)] = blocks[k][low : low + piece, 256:384]
    bias = jnp.concatenate(
        [vec[2:3, rem:], jnp.zeros((1, HD), F32), vec[3:4, rem:], jnp.zeros((1, HD), F32)],
        axis=1,
    )

    def project(p, carry):
        at = pl.ds(aligned(p * 256, 256), 256)
        joint = dot(hidden[at, :], wr[...]) + bias
        split_joint(joint, slice(0, 256), at, HD, 1, q_ref, k_ref, v_ref)
        return carry

    lax.fori_loop(0, total // 256, project, 0)
    attend_heads(starts_of(lens), total, 1, q_ref, k_ref, v_ref, o_ref)
    wo[:, rem:] = wr[:, 3 * HD : 4 * HD]
    wait_all(copies)
    wo_own[:own, :] = wo[pl.ds(aligned(own * c, own), own), :]
    wo_own[own:, :] = wo[rem:, :]


def attend_rest(lens, hidden, vec, blocks, nz, part):
    n = len(blocks)
    total, width = hidden.shape
    head = shape((1, total, HD))
    return kernel_call(
        functools.partial(attend_rest_kernel, n, nz, part),
        "attend_rest",
        [(SM, lens), (VM, hidden), (VM, vec)] + [(VM, item) for item in blocks],
        [
            (VM, item)
            for item in (
                shape((width, 4 * HD)),
                head,
                head,
                head,
                head,
                shape((width, width)),
                shape((blocks[0].shape[1] // 3 + HD, width)),
            )
        ],
        [pltpu.SemaphoreType.DMA((2 * n * nz,))],
        5,
    )


def gelu_parts(u):
    c0 = 0.7978845608028654
    c1 = 0.044715
    square = u * u
    t = jnp.tanh(c0 * (u + c1 * square * u))
    act = 0.5 * u * (1.0 + t)
    slope = 0.5 * (1.0 + t) + 0.5 * u * (1.0 - t * t) * (c0 * (1.0 + 3.0 * c1 * square))
    return act, slope


def put_padded(ref, at, value):
    width = value.shape[1]
    ref[at, :width] = value.astype(BF)
    ref[at, width:] = jnp.zeros((value.shape[0], ref.shape[1] - width), BF)


def mix_kernel(n, *refs):
    reader = Reader(refs)
    (order,) = reader.many(1)
    xs_in, at_in = (reader.many(n) for _ in range(2))
    at_rem, wo, vec = reader.many(3)
    att_ref, h2_ref, x2_ref = reader.many(3)
    xs, att, x2s, sems = reader.many(4)
    c, _ = here()
    total, width = h2_ref.shape
    rows = total // n
    half = rows // 2
    own = at_in[0].shape[1]
    pairs, late = [], []
    for i, k in enumerate(places(n)):
        late.append((xs_in[k].at[pl.ds(0, rows)], xs.at[pl.ds(rows * i, rows)]))
        lane = pl.ds(aligned(own * (c ^ k), own), own)
        pairs.append((at_in[k], att.at[:, lane]))
    copies = start_all(pairs + late, sems)
    att[:, own * n :] = at_rem[0]
    out_bias, gain, shift = vec[4:5, :], vec[5:6, :], vec[6:7, :]
    wait_all(copies[: len(pairs)])

    def arrange(i, carry):
        for h in range(2):
            source = pl.ds(sorted_at(order, c, rows, k_at(n, i), h), half)
            att_ref[pl.ds(aligned(i * rows + h * half, half), half), :] = att[source, :]
        return carry

    def attended(p, carry):
        at = pl.ds(aligned(p * WIDE, WIDE), WIDE)
        x2s[at, :] = dot(att_ref[at, :], wo[...])
        return carry

    def normalise(i, carry):
        at = pl.ds(aligned(i * rows, rows), rows)
        x2 = xs[at, :width].astype(F32) + x2s[at, :] + out_bias

        @pl.when(i == n // 2)
        def _():
            x2_ref[...] = x2

        normed, _ = norm_rows(x2)
        h2_ref[at, :] = (normed * gain + shift).astype(BF)
        return carry

    lax.fori_loop(0, n, arrange, 0)
    lax.fori_loop(0, total // WIDE, attended, 0)
    wait_all(copies[len(pairs) :])
    lax.fori_loop(0, n, normalise, 0)


def mix(order, xs, ats, at_rem, wo, vec):
    n = len(xs)
    width = vec.shape[1]
    rows = xs[0].shape[0] // 2
    total = rows * n
    return kernel_call(
        functools.partial(mix_kernel, n),
        "mix",
        [(SM, order)]
        + [(HB, item) for item in (*xs, *ats)]
        + [(VM, item) for item in (at_rem, wo, vec)],
        [
            (VM, item)
            for item in (
                shape((total, width)),
                shape((total, width)),
                shape((rows, width), F32),
            )
        ],
        [
            pltpu.VMEM((total, full_lanes(width)), BF),
            pltpu.VMEM((total, width), BF),
            pltpu.VMEM((total, width), F32),
            pltpu.SemaphoreType.DMA((2 * n,)),
        ],
        9,
    )


def mlp_kernel(n, nz, *refs):
    reader = Reader(refs)
    dm_in = reader.many(n)
    ffn_w, h2_ref, vec = reader.many(3)
    e_odd, e_even, act_ref, du_ref, wd = reader.many(5)
    dms, wu, us, sems = reader.many(4)
    c, _ = here()
    total, width = h2_ref.shape
    rows = total // n
    part = width // nz
    hid = wu.shape[1]
    seg = hid // nz
    pairs = [
        (dm_in[k].at[pl.ds(rows, rows)], dms.at[pl.ds(rows * i, rows)])
        for i, k in enumerate(places(n))
    ]
    copies = start_all(pairs, sems)
    for q in range(nz):
        for i in range(2):
            low = part * q + i * (part // 2)
            wu[low : low + part // 2, :] = ffn_w[q, : part // 2, i * hid : (i + 1) * hid]
        wd[seg * q : seg * (q + 1), :] = ffn_w[q, part // 2 :, :]
    fold = part // seg
    row = vec[pl.ds(8 + c // fold, 1), :]
    up_bias = jnp.zeros((1, hid), F32)
    for f in range(fold):
        cut = [row[:, part * q + seg * f : part * q + seg * (f + 1)] for q in range(nz)]
        up_bias = jnp.where(c % fold == f, jnp.concatenate(cut, axis=1), up_bias)

    def expand(p, carry):
        at = pl.ds(aligned(p * WIDE, WIDE), WIDE)
        us[at, :] = dot(h2_ref[at, :], wu[...])
        return carry

    def activate(i, carry):
        at = pl.ds(aligned(i * rows, rows), rows)
        act, slope = gelu_parts(us[at, :] + up_bias)
        act_ref[at, :] = act.astype(BF)
        us[at, :] = slope
        return carry

    def shrink(p, carry):
        at = pl.ds(aligned(p * WIDE, WIDE), WIDE)
        du_ref[at, :] = (dot(dms[at, :width], wd[...], NT) * us[at, :]).astype(BF)
        return carry

    lax.fori_loop(0, total // WIDE, expand, 0)
    lax.fori_loop(0, n, activate, 0)
    wait_all(copies)
    lax.fori_loop(0, total // WIDE, shrink, 0)
    put_padded(e_odd, slice(None), dot(du_ref[: total // 2, :], wu[...], NT))
    e_even[...] = dot(du_ref[total // 2 :, :], wu[...], NT).astype(BF)


def mlp(dms, ffn_w, h2, vec):
    n, nz = len(dms), ffn_w.shape[0]
    total, width = h2.shape
    hid = width // 2
    return kernel_call(
        functools.partial(mlp_kernel, n, nz),
        "mlp",
        [(HB, item) for item in dms] + [(VM, item) for item in (ffn_w, h2, vec)],
        [
            (VM, item)
            for item in (
                shape((total // 2, full_lanes(width))),
                shape((total // 2, width)),
                shape((total, hid)),
                shape((total, hid)),
                shape((hid, width)),
            )
        ],
        [
            pltpu.VMEM((total, full_lanes(width)), BF),
            pltpu.VMEM((width, hid), BF),
            pltpu.VMEM((total, hid), F32),
            pltpu.SemaphoreType.DMA((n,)),
        ],
        15,
    )


def shrink_part_kernel(act, wd, odd, even):
    half = odd.shape[0]
    put_padded(odd, slice(None), dot(act[:half, :], wd[...]))
    even[...] = dot(act[half:, :], wd[...]).astype(BF)


def shrink_part(act, wd):
    half, width = act.shape[0] // 2, wd.shape[1]
    return kernel_call(
        shrink_part_kernel,
        "shrink_part",
        [(VM, act), (VM, wd)],
        [(VM, shape((half, full_lanes(width)))), (VM, shape((half, width)))],
        [],
        4,
    )


def pair_sums_kernel(mine, other, *outs):
    rows, width = outs[0].shape
    for i, out in enumerate(outs):
        cut = slice(rows * i, rows * (i + 1))
        out[...] = (mine[cut].astype(F32) + other[cut, :width].astype(F32)).astype(BF)


def pair_sums(mine, other, rows):
    total, width = mine.shape
    return kernel_call(
        pair_sums_kernel,
        "pair_sums",
        [(VM, mine), (VM, other)],
        [(VM, shape((rows, width)))] * (total // rows),
        [],
        2,
    )


def blocks_of(width, step):
    return [(low, min(step, width - low)) for low in range(0, width, step)]


def ffn_grads_kernel(n, nz, *refs):
    reader = Reader(refs)
    dm_in = reader.many(n)
    h2, act, du = reader.many(3)
    out, du_sum = reader.many(2)
    dms, gu, gd, sems = reader.many(4)
    total, hid = du.shape
    width = h2.shape[1]
    rows = total // n
    part, seg = width // nz, hid // nz
    tall = part // 2 + seg
    pairs = [
        (dm_in[k].at[pl.ds(rows, rows)], dms.at[pl.ds(rows * i, rows)])
        for i, k in enumerate(places(n))
    ]
    copies = start_all(pairs, sems)
    for low, size in blocks_of(width, 256):
        gu[low : low + size, :] = dot(h2[:, low : low + size], du[...], TN).astype(BF)
    du_sum[...] = dot(jnp.ones((8, total), BF), du[...])
    wait_all(copies)
    for low, size in blocks_of(hid, 256):
        gd[low : low + size, :] = dot(act[:, low : low + size], dms[:, :width], TN).astype(BF)
    for q in range(nz):
        base = tall * q
        for i in range(2):
            low = part * q + i * (part // 2)
            out[base : base + part // 2, i * hid : (i + 1) * hid] = gu[low : low + part // 2, :]
        out[base + part // 2 : base + tall, :] = gd[seg * q : seg * (q + 1), :]


def ffn_grads(dms, h2, act, du, nz):
    n = len(dms)
    width = h2.shape[1]
    total, hid = du.shape
    part, seg = width // nz, hid // nz
    return kernel_call(
        functools.partial(ffn_grads_kernel, n, nz),
        "ffn_grads",
        [(HB, item) for item in dms] + [(VM, item) for item in (h2, act, du)],
        [(VM, shape((nz * (part // 2 + seg), width))), (VM, shape((8, hid), F32))],
        [
            pltpu.VMEM((total, full_lanes(width)), BF),
            pltpu.VMEM((width, hid), BF),
            pltpu.VMEM((hid, width), BF),
            pltpu.SemaphoreType.DMA((n,)),
        ],
        9,
    )


def norm_back(rows, gain, error):
    normed, inverse = norm_rows(rows)
    f = error * gain
    slope = inverse * (
        f
        - jnp.mean(f, axis=-1, keepdims=True)
        - normed * jnp.mean(f * normed, axis=-1, keepdims=True)
    )
    return slope, normed


def middle_kernel(count, *refs):
    reader = Reader(refs)
    parts = reader.many(count)
    x2, both, vec = reader.many(3)
    dx2_ref, db_ref, sums = reader.many(3)
    error = parts[0][...].astype(F32)
    for item in parts[1:]:
        error = error + item[...].astype(F32)
    slope, normed = norm_back(x2[...], vec[5:6, :], error)
    upstream = both[both.shape[0] // 2 :, : x2.shape[1]].astype(F32)
    dx2 = upstream + slope
    dx2_ref[...] = dx2
    db = dx2.astype(BF)
    db_ref[...] = db
    rows = [jnp.sum(item, axis=0, keepdims=True) for item in (db.astype(F32), error * normed, error, upstream)]
    sums[...] = jnp.concatenate(rows + [jnp.zeros_like(rows[0])] * 4, axis=0)


def middle(parts, x2, both, vec):
    rows, width = x2.shape
    return kernel_call(
        functools.partial(middle_kernel, len(parts)),
        "middle",
        [(VM, item) for item in (*parts, x2, both, vec)],
        [(VM, shape((rows, width), F32)), (VM, shape((rows, width))), (VM, shape((8, width), F32))],
        [],
        2,
    )


def back_heads(starts, total, count, q_ref, k_ref, v_ref, das, out, dks, dvs):
    def head(h, carry):
        dks[...] = jnp.zeros_like(dks)
        dvs[...] = jnp.zeros_like(dvs)
        for first, low, high in windows(total, 256):
            at = slice(first, first + 256)
            query = q_ref[h, at, :]
            scores = dot(query, k_ref[h, low:high, :], NT)
            allowed = mask_of(starts, first, 256, low, high - low)
            scores = jnp.where(allowed, scores, masked_fill)
            peak = jnp.max(scores, axis=-1, keepdims=True)
            expo = jnp.exp(scores - peak)
            soft = expo * (1.0 / jnp.sum(expo, axis=-1, keepdims=True))
            da = das[h, at, :]
            dp = dot(da, v_ref[h, low:high, :], NT)
            delta = jnp.sum(soft * dp, axis=-1, keepdims=True)
            ds = (soft * (dp - delta)).astype(BF)
            out[h, at, :] = (dot(ds, k_ref[h, low:high, :]) * 0.125).astype(BF)
            dks[low:high, :] += dot(ds, query, TN)
            dvs[low:high, :] += dot(soft.astype(BF), da, TN)
        out[count + h, :, :] = dks[...].astype(BF)
        out[2 * count + h, :, :] = dvs[...].astype(BF)
        return carry

    lax.fori_loop(0, count, head, 0)


def back_kernel(n, hp, *refs):
    reader = Reader(refs)
    order, lens = reader.many(2)
    db_in = reader.many(n)
    wo, w_nat, q_ref, k_ref, v_ref = reader.many(5)
    e_odd, e_even, dj_ref, das_rest = reader.many(4)
    dbs, das, out, dks, dvs, sems = reader.many(6)
    c, _ = here()
    rows, width = db_in[0].shape
    half = rows // 2
    total = rows * n
    own = hp * HD
    wait_all(start_all([(db_in[k], dbs.at[pl.ds(rows * k, rows)]) for k in range(n)], sems))

    def project(p, carry):
        at = pl.ds(aligned(p * (2 * rows), 2 * rows), 2 * rows)
        da = dot(dbs[at, :], wo[...], NT).astype(BF)
        for i in range(4):
            to = pl.ds(sorted_at(order, c, rows, 2 * p + i // 2, i % 2), half)
            for h in range(hp):
                das[h, to, :] = da[i * half : (i + 1) * half, h * HD : (h + 1) * HD]
            das_rest[0, to, :] = da[i * half : (i + 1) * half, own:]
        return carry

    lax.fori_loop(0, n // 2, project, 0)
    back_heads(starts_of(lens), total, hp, q_ref, k_ref, v_ref, das, out, dks, dvs)
    for i in range(3 * hp):
        dj_ref[:, i * HD : (i + 1) * HD] = out[i]

    def scatter(e_ref, first, p, carry):
        at = pl.ds(aligned(p * (2 * rows), 2 * rows), 2 * rows)
        pieces = []
        for i in range(4):
            k = 4 * p + 2 * (i // 2) + first
            source = pl.ds(sorted_at(order, c, rows, k, i % 2), half)
            pieces.append(dj_ref[source, :])
        error = dot(jnp.concatenate(pieces, axis=0), w_nat[...], NT)
        if e_ref.shape[1] == w_nat.shape[0]:
            e_ref[at, :] = error.astype(BF)
        else:
            put_padded(e_ref, at, error)
        return carry

    lax.fori_loop(0, n // 4, functools.partial(scatter, e_odd, 1), 0)
    lax.fori_loop(0, n // 4, functools.partial(scatter, e_even, 0), 0)


def back(order, lens, dbs, wo, w_nat, q, k, v):
    n = len(dbs)
    rows, width = dbs[0].shape
    hp, total, _ = q.shape
    big = pltpu.VMEM((total, width), BF)
    column = pltpu.VMEM((total, HD), F32)
    return kernel_call(
        functools.partial(back_kernel, n, hp),
        "back",
        [(SM, order), (SM, lens)]
        + [(HB, item) for item in dbs]
        + [(VM, item) for item in (wo, w_nat, q, k, v)],
        [
            (VM, shape((total // 2, full_lanes(width)))),
            (VM, shape((total // 2, width))),
            (VM, shape((total, 3 * hp * HD))),
            (VM, shape((1, total, HD))),
        ],
        [
            big,
            pltpu.VMEM((hp, total, HD), BF),
            pltpu.VMEM((3 * hp, total, HD), BF),
            column,
            column,
            pltpu.SemaphoreType.DMA((n,)),
        ],
        17,
    )


def back_rest_kernel(*refs):
    reader = Reader(refs)
    order, lens = reader.many(2)
    das, q_ref, k_ref, v_ref, wr = reader.many(5)
    dj_ref, e_ref = reader.many(2)
    out, dks, dvs = reader.many(3)
    c, _ = here()
    total = q_ref.shape[1]
    rows = e_ref.shape[0]
    back_heads(starts_of(lens), total, 1, q_ref, k_ref, v_ref, das, out, dks, dvs)
    for i in range(3):
        dj_ref[:, i * HD : (i + 1) * HD] = out[i]
    pieces = [dj_ref[pl.ds(sorted_at(order, c, rows, 0, i), rows // 2), :] for i in range(2)]
    e_ref[...] = dot(jnp.concatenate(pieces, axis=0), wr[:, : 3 * HD], NT)


def back_rest(order, lens, das, q, k, v, wr, rows):
    total = q.shape[1]
    column = pltpu.VMEM((total, HD), F32)
    return kernel_call(
        back_rest_kernel,
        "back_rest",
        [(SM, order), (SM, lens)] + [(VM, item) for item in (das, q, k, v, wr)],
        [(VM, shape((total, 3 * HD))), (VM, shape((rows, wr.shape[0]), F32))],
        [pltpu.VMEM((3, total, HD), BF), column, column],
        6,
    )


def weight_terms(weights, product, dj_sum):
    def summed(item):
        column = jnp.sum(item, axis=1, keepdims=True)
        return jnp.broadcast_to(column, (column.shape[0], 128)).T[0:1]

    return summed(weights * product), summed(weights * dj_sum)


def vec_columns(vec):
    tall = jnp.concatenate([vec[0:8, :]] * 16, axis=0)
    return tall.T[:, 0:8]


def proj_grads_kernel(n, nz, *refs):
    reader = Reader(refs)
    db_in = reader.many(n)
    n1, dj, w_nat, vec, att = reader.many(5)
    outs = reader.many(nz)
    (sums,) = reader.many(1)
    dbs, held, sems, out_sems = reader.many(4)
    c, z = here()
    rows, width = db_in[0].shape
    total, cols = dj.shape
    own = cols // 3
    part = width // nz
    pairs = [(db_in[k], dbs.at[pl.ds(rows * i, rows)]) for i, k in enumerate(places(n))]
    copies = start_all(pairs, sems)
    product = dot(n1[...], dj[...], TN)
    dj_sum = dot(jnp.ones((8, total), BF), dj[...])[0:1]
    weights = w_nat[...].astype(F32)
    gain, shift = weight_terms(weights, product, dj_sum)
    sums[0:1, :] = gain
    sums[1:2, :] = shift
    sums[2:8, :] = jnp.zeros((6, width), F32)
    lane = pl.ds(aligned(own * c, own), own)
    sums[2:3, lane] = dj_sum[:, :own]
    sums[3:4, lane] = dj_sum[:, 2 * own :]
    columns = vec_columns(vec)
    grad = product * columns[:, 0:1] + columns[:, 1:2] * dj_sum
    held[:, :cols] = grad.astype(BF)
    wait_all(copies)
    held[:, cols:] = dot(att[...], dbs[:, lane], TN).astype(BF)
    wait_all(
        start_all(
            [
                (held.at[pl.ds(aligned(part * (z ^ j), part), part)], outs[j])
                for j in range(nz)
            ],
            out_sems,
        )
    )


def proj_grads(dbs, n1, dj, w_nat, vec, att, nz):
    n = len(dbs)
    rows, width = dbs[0].shape
    total, cols = dj.shape
    wide = cols // 3 * 4
    out = kernel_call(
        functools.partial(proj_grads_kernel, n, nz),
        "proj_grads",
        [(HB, item) for item in dbs] + [(VM, item) for item in (n1, dj, w_nat, vec, att)],
        [(HB, shape((width // nz, wide)))] * nz + [(VM, shape((8, width), F32))],
        [
            pltpu.VMEM((total, width), BF),
            pltpu.VMEM((width, wide), BF),
            pltpu.SemaphoreType.DMA((n,)),
            pltpu.SemaphoreType.DMA((nz,)),
        ],
        5,
    )
    return out[:nz], out[nz]


def rest_grads_kernel(n, nz, *refs):
    reader = Reader(refs)
    db_in = reader.many(n)
    n1, dj, wr, vec, att, sums_mid, sums_proj, du_sum = reader.many(8)
    outs = reader.many(nz)
    dbs, grad, wide, ups, held, sems, out_sems = reader.many(7)
    c, z = here()
    rows, width = db_in[0].shape
    total = dj.shape[0]
    part = width // nz
    piece = piece_rows(part, n)
    seg = du_sum.shape[1] // nz
    rem = width - HD
    pairs = [(db_in[k], dbs.at[pl.ds(rows * i, rows)]) for i, k in enumerate(places(n))]
    copies = start_all(pairs, sems)
    product = dot(n1[...], dj[...], TN)
    dj_sum = dot(jnp.ones((8, total), BF), dj[...])[0:1]
    weights = wr[:, : 3 * HD].astype(F32)
    gain, shift = weight_terms(weights, product, dj_sum)
    once = jnp.where(c == 0, 1.0, 0.0)
    wide[0:4, :] = sums_proj[0:4, :]
    wide[0:1, :] += gain * once
    wide[1:2, :] += shift * once
    wide[2:3, rem:] += dj_sum[:, :HD] * once
    wide[3:4, rem:] += dj_sum[:, 2 * HD :] * once
    wide[4:8, :] = sums_mid[0:4, :]
    columns = vec_columns(vec)
    grad[:, : 3 * HD] = product * columns[:, 0:1] + columns[:, 1:2] * dj_sum
    fold = part // seg
    for q in range(nz):
        item = du_sum[0:1, seg * q : seg * (q + 1)]
        for r in range(width // part):
            cut = [
                jnp.where(c == r * fold + f, item, jnp.zeros_like(item)) for f in range(fold)
            ]
            ups[q, r : r + 1, :] = jnp.concatenate(cut, axis=1)
    wait_all(copies)
    grad[:, 3 * HD :] = dot(att[...], dbs[:, rem:], TN)
    off = jnp.minimum(piece * c, part - piece)
    held[...] = jnp.zeros_like(held)
    for q in range(nz):
        held[q, :piece, : 4 * HD] = grad[pl.ds(aligned(part * q + off, 8), piece), :].astype(BF)
        both = jnp.concatenate([wide[0:8, part * q : part * (q + 1)], ups[q]], axis=0)
        held[q, piece : piece + both.shape[0], :part] = both.astype(BF)
    wait_all(start_all([(held.at[z ^ j], outs[j]) for j in range(nz)], out_sems))


def rest_grads(dbs, n1, dj, wr, vec, att, sums_mid, sums_proj, du_sum, nz):
    n = len(dbs)
    rows, width = dbs[0].shape
    total = dj.shape[0]
    part = width // nz
    tall = piece_rows(part, n) + 8 + -(-(width // part) // 8) * 8
    lanes = -(-part // 128) * 128
    return kernel_call(
        functools.partial(rest_grads_kernel, n, nz),
        "rest_grads",
        [(HB, item) for item in dbs]
        + [(VM, item) for item in (n1, dj, wr, vec, att, sums_mid, sums_proj, du_sum)],
        [(HB, shape((tall, lanes)))] * nz,
        [
            pltpu.VMEM((total, width), BF),
            pltpu.VMEM((width, 4 * HD), F32),
            pltpu.VMEM((8, width), F32),
            pltpu.VMEM((nz, width // part, part), F32),
            pltpu.VMEM((nz, tall, lanes), BF),
            pltpu.SemaphoreType.DMA((n,)),
            pltpu.SemaphoreType.DMA((nz,)),
        ],
        4,
    )


def joined_sums_kernel(count, *refs):
    out = refs[2 * count]
    part = refs[0].shape[0]
    tall, lanes = refs[count].shape
    for first, low, size, wide in ((0, 0, part, out.shape[1]), (count, part, tall, lanes)):
        total = refs[first][...].astype(F32)
        for item in refs[first + 1 : first + count]:
            total = total + item[...].astype(F32)
        out[low : low + size, :wide] = total.astype(BF)
    out[part:, lanes:] = jnp.zeros((out.shape[0] - part, out.shape[1] - lanes), BF)


def joined_sums(p_terms, r_terms):
    part, wide = p_terms[0].shape
    return kernel_call(
        functools.partial(joined_sums_kernel, len(p_terms)),
        "joined_sums",
        [(VM, item) for item in (*p_terms, *r_terms)],
        [(VM, shape((part + r_terms[0].shape[0], wide)))],
        [],
        2,
    )[0]


def last_kernel(count, *refs):
    reader = Reader(refs)
    parts = reader.many(count)
    rest, both, dx2, vec = reader.many(4)
    (out,) = reader.many(1)
    rows, width = dx2.shape
    error = rest[...]
    for item in parts:
        error = error + item[...].astype(F32)
    slope, _ = norm_back(both[:rows, :width].astype(F32), vec[0:1, :], error)
    out[...] = (dx2[...] + slope).T.astype(BF)


def last(parts, rest, both, dx2, vec):
    return kernel_call(
        functools.partial(last_kernel, len(parts)),
        "last",
        [(VM, item) for item in (*parts, rest, both, dx2, vec)],
        [(VM, shape(dx2.shape[::-1]))],
        [],
        2,
    )[0].T


def block_out_kernel(count, *refs):
    reader = Reader(refs)
    parts = reader.many(count)
    x2, vec = reader.many(2)
    (out,) = reader.many(1)
    total = x2[...] + vec[7:8, :]
    for item in parts:
        total = total + item[...].astype(F32)
    out[...] = total.T.astype(BF)


def block_out_of(parts, x2, vec):
    return kernel_call(
        functools.partial(block_out_kernel, len(parts)),
        "block_out",
        [(VM, item) for item in (*parts, x2, vec)],
        [(VM, shape(x2.shape[::-1]))],
        [],
        1,
    )[0].T


def ffn_out_kernel(n, nz, blocks, up_out, down_out, held, up, down, in_sems, sems):
    part = up.shape[0]
    hid = held.shape[2] // 2
    seg = hid // nz
    half = part // 2
    arriving = start_all([(blocks.at[k], held.at[k]) for k in range(n)], in_sems)
    leaving = []
    for k in range(n):
        arriving[k].wait()
        cut = pl.ds(seg * k, seg)
        down[seg * k : seg * (k + 1), :] = held[k, half:, :].astype(F32)
        leaving.append(pltpu.make_async_copy(down.at[cut], down_out.at[cut], sems.at[k]))
        leaving[-1].start()
    for i in range(2):
        for q in range(nz):
            low = i * hid + q * seg
            pieces = [held[k, :half, low : low + seg].astype(F32) for k in range(n)]
            up[i * half : (i + 1) * half, q * seg * n : (q + 1) * seg * n] = jnp.concatenate(
                pieces, axis=1
            )
        cut = pl.ds(half * i, half)
        leaving.append(pltpu.make_async_copy(up.at[cut], up_out.at[cut], sems.at[n + i]))
        leaving[-1].start()
    wait_all(leaving)


def ffn_out(blocks, nz):
    n, tall, width = blocks.shape
    part = width // nz
    seg = tall - part // 2
    up, down = (part, seg * n * nz), (seg * n, width)
    return kernel_call(
        functools.partial(ffn_out_kernel, n, nz),
        "ffn_out",
        [(HB, blocks)],
        [(HB, shape(up, F32)), (HB, shape(down, F32))],
        [
            pltpu.VMEM((n, tall, width), BF),
            pltpu.VMEM(up, F32),
            pltpu.VMEM(down, F32),
            pltpu.SemaphoreType.DMA((n,)),
            pltpu.SemaphoreType.DMA((n + 2,)),
        ],
        8,
    )


def proj_out_kernel(n, own, piece, *refs):
    reader = Reader(refs)
    blocks = reader.many(n)
    out_in, out_o = reader.many(2)
    vectors = reader.many(8)
    (up_bias,) = reader.many(1)
    held, held_rest, rest = reader.many(3)
    c, _ = here()
    part, width = out_o.shape
    tall, lanes = held_rest.shape[1:]
    for k in range(n):
        held[c ^ k] = blocks[k][:part, :]
        held_rest[c ^ k] = blocks[k][part:, :lanes].astype(F32)
    total = held_rest[0, piece:, :]
    for k in range(1, n):
        total = total + held_rest[k, piece:, :]
    for i in range(8):
        vectors[i][...] = total[i, :part]
    for i in range(width // part):
        up_bias[part * i : part * (i + 1)] = total[8 + i, :part]
    for k in range(n):
        at = min(piece * k, part - piece)
        rest[at : at + piece, :] = held_rest[k, :piece, : 4 * HD]
    pieces = []
    for kind in range(3):
        for k in range(n):
            pieces.append(held[k, :, own * kind : own * (kind + 1)].astype(F32))
        pieces.append(rest[:, HD * kind : HD * (kind + 1)])
    out_in[...] = jnp.concatenate(pieces, axis=1)
    for k in range(n):
        out_o[:, own * k : own * (k + 1)] = held[k, :, 3 * own : 4 * own].astype(F32)
    out_o[:, own * n :] = rest[:, 3 * HD : 4 * HD]


def proj_out(blocks, part):
    n = len(blocks)
    cols = blocks[0].shape[1]
    own = cols // 4
    tall = blocks[0].shape[0] - part
    lanes = -(-part // 128) * 128
    piece = piece_rows(part, n)
    width = own * n + HD
    return kernel_call(
        functools.partial(proj_out_kernel, n, own, piece),
        "proj_out",
        [(VM, item) for item in blocks],
        [
            (VM, shape((part, 3 * width), F32)),
            (VM, shape((part, width), F32)),
        ]
        + [(VM, shape((part,), F32))] * 8
        + [(VM, shape((width,), F32))],
        [
            pltpu.VMEM((n, part, cols), BF),
            pltpu.VMEM((n, tall, lanes), F32),
            pltpu.VMEM((part, 4 * HD), F32),
        ],
        5,
    )


def swap(value, axis, size, bit, label):
    with jax.named_scope(label + str(bit)):
        return lax.ppermute(value, axis, [(i, i ^ bit) for i in range(size)])


def after(value, *others):
    return lax.optimization_barrier((value, *others))[0]


def gather_z(value, nz, label):
    order = sorted(range(1, nz), reverse=True)
    parts = {0: value}
    for j in order:
        parts[j] = swap(value, "wshard", nz, j, label)
    return [parts[j] for j in range(nz)]


def far_of(n):
    return sorted(range(2, n, 2), key=lambda k: -bin(k).count("1"))


def gather_far(value, n, label):
    parts = {0: value}
    for k in far_of(n):
        parts[k] = swap(value, "ctx", n, k, label)
    return parts


def gather_near(parts, n, label):
    for k in sorted(parts):
        parts[k ^ 1] = swap(parts[k], "ctx", n, 1, f"{label}_{k}_")
    return [parts[k] for k in range(n)]


def gather_ctx(value, n, label):
    return gather_near(gather_far(value, n, label), n, label)


def relay_far(value, n, label):
    parts = {0: value}
    for k in range(2, n, 2):
        bit = 1 << (k.bit_length() - 1)
        parts[k] = swap(parts[k ^ bit], "ctx", n, bit, f"{label}_{k}_")
    return parts


def spread_ctx(sums, n, label):
    return [sums[0]] + [swap(sums[k // 2], "ctx", n, k, label) for k in far_of(n)]


def scatter_z(chunks, nz, label):
    return [chunks[0]] + [
        swap(chunks[j], "wshard", nz, j, label) for j in sorted(range(1, nz), reverse=True)
    ]


def local_fast(
    n,
    nz,
    tokens,
    cotangent,
    seq_lengths,
    token_order,
    attn_norm_gain,
    attn_norm_bias,
    input_weight,
    query_bias,
    value_bias,
    output_weight,
    output_bias,
    mlp_norm_gain,
    mlp_norm_bias,
    expand_weight,
    expand_bias,
    shrink_weight,
    shrink_bias,
):
    rows = tokens.shape[1]
    part = input_weight.shape[0]
    hp = HEADS // n
    own = hp * HD

    vectors = (
        attn_norm_gain,
        attn_norm_bias,
        query_bias,
        value_bias,
        output_bias,
        mlp_norm_gain,
        mlp_norm_bias,
        shrink_bias,
    )
    width = tokens.shape[2]
    both = pack_rows(tokens[0], cotangent[0])
    lead = pack_first(input_weight, output_weight, vectors, expand_bias, n, own)
    packed = pack_ffn(after(expand_weight, lead), shrink_weight, n, nz)
    far = relay_far(both, n, "rows")
    first = after(lead, packed, far[2 % n])
    leads = [lead] + [
        swap(first if j == 1 else lead, "wshard", nz, j, "lead") for j in range(1, nz)
    ]
    arrived = lax.optimization_barrier((packed, tuple(leads), far))
    packed, leads, far = arrived
    boths = gather_near(far, n, "rows")
    ffn_w = lax.all_gather(packed, "wshard")
    shared_far = gather_far(pack_shared(leads, part), n, "shared")

    n1, hidden, w_nat, q, k, v, at_own, vec = attend(
        token_order, seq_lengths, boths, leads, hp, width
    )
    shared = gather_near({k: after(shared_far[k], at_own) for k in shared_far}, n, "shared")
    at_far = gather_far(at_own, n, "attn")
    wr, q_r, k_r, v_r, at_rest, wo, wo_own = attend_rest(
        seq_lengths, hidden, vec, shared, nz, part
    )
    ats = gather_near({k: after(at_far[k], at_rest) for k in at_far}, n, "attn")
    att, h2, x2 = mix(token_order, boths, ats, at_rest, wo, vec)
    e_odd, e_even, act, du, wd = mlp(boths, ffn_w, h2, vec)

    e_sums = pair_sums(e_even, swap(e_odd, "ctx", n, 1, "e2_"), rows)
    e_terms = spread_ctx(e_sums, n, "e2_far")
    f_chunks, du_sum = ffn_grads(boths, h2, act, after(du, *e_sums), nz)
    m_odd, m_even = shrink_part(after(act, du_sum), wd)
    dx2, db_own, sums_mid = middle(e_terms, after(x2, m_odd), both, vec)
    f_chunks = after(f_chunks, *e_terms)
    f_sum = lax.psum_scatter(f_chunks, "wshard", scatter_dimension=0, tiled=True)
    db_far = gather_far(db_own, n, "db")
    m_other = swap(after(m_odd, db_own), "ctx", n, 1, "out_")
    m_sums = pair_sums(m_even, m_other, rows)
    dbs = gather_near({k: after(db_far[k], *m_sums) for k in db_far}, n, "db")
    m_terms = spread_ctx([after(item, *dbs) for item in m_sums], n, "out_far")

    e1_odd, e1_even, dj, das_rest = back(
        token_order, seq_lengths, dbs, wo_own, w_nat, q, k, v
    )
    e1_other = swap(e1_odd, "ctx", n, 1, "e1_")
    p_chunks, sums_proj = proj_grads(dbs, after(n1, *m_terms), dj, w_nat, vec, att, nz)
    p_terms = scatter_z(p_chunks, nz, "proj")
    e1_sums = pair_sums(after(e1_even, *p_chunks), e1_other, rows)
    e1_terms = spread_ctx(e1_sums, n, "e1_far")
    dj_rest, e1_rest = back_rest(
        token_order, seq_lengths, after(das_rest, *e1_sums), q_r, k_r, v_r, wr, rows
    )
    f_blocks = lax.all_gather(after(f_sum, dj), "ctx")
    r_chunks = rest_grads(dbs, n1, dj_rest, wr, vec, att, sums_mid, sums_proj, du_sum, nz)
    r_terms = scatter_z(r_chunks, nz, "rest")
    p_terms[0] = after(p_terms[0], *e1_terms)

    grads_far = gather_far(joined_sums(p_terms, r_terms), n, "grads")
    block_out = block_out_of(m_terms, x2, vec)[None]
    input_grad = last(e1_terms, e1_rest, both, dx2, vec)[None]
    out_up, out_down = ffn_out(f_blocks, nz)
    blocks = {k: after(grads_far[k], block_out, input_grad, out_up) for k in grads_far}
    blocks = gather_near(blocks, n, "grads")
    out_in, out_o, *small = proj_out(blocks, part)
    return (
        block_out,
        input_grad,
        small[0],
        small[1],
        out_in,
        small[2],
        small[3],
        out_o,
        small[4],
        small[5],
        small[6],
        out_up,
        small[8],
        out_down,
        small[7],
    )


def layer_norm(values, scale_gain, shift_bias):
    center = values - jnp.mean(values, axis=-1, keepdims=True)
    spread = jnp.mean(center * center, axis=-1, keepdims=True)
    return center * lax.rsqrt(spread + EPSILON) * scale_gain + shift_bias


def gelu_act(values):
    return jax.nn.gelu(values, approximate=True)


def outer_sum(left, right):
    return lax.dot_general(
        left, right, (((0,), (0,)), ((), ())), preferred_element_type=jnp.float32
    )


def times_t(left, right):
    return lax.dot_general(
        left, right, (((1,), (1,)), ((), ())), preferred_element_type=jnp.float32
    )


def seq_starts(positions, lengths_row):
    ends = jnp.cumsum(lengths_row, dtype=jnp.int32)
    begins = ends - lengths_row
    inside = (positions[:, None] >= begins[None, :]) & (positions[:, None] < ends[None, :])
    return jnp.sum(jnp.where(inside, begins[None, :], 0), axis=1)


def take_rows(source, block_index, size):
    return lax.dynamic_slice_in_dim(source, block_index * size, size)


def scores_of(query_heads, key_heads, query_pos, query_start, key_pos):
    scores = (
        jnp.einsum("qhd,khd->hqk", query_heads, key_heads, preferred_element_type=jnp.float32)
        * 0.125
    )
    allowed = (key_pos[None, :] >= query_start[:, None]) & (key_pos[None, :] <= query_pos[:, None])
    return jnp.where(allowed[None], scores, masked_fill)


def local_plain(
    tokens,
    cotangent,
    seq_lengths,
    token_order,
    attn_norm_gain,
    attn_norm_bias,
    input_weight,
    query_bias,
    value_bias,
    output_weight,
    output_bias,
    mlp_norm_gain,
    mlp_norm_bias,
    expand_weight,
    expand_bias,
    shrink_weight,
    shrink_bias,
):
    gathered = (
        lax.all_gather(input_weight, "wshard", axis=0, tiled=True),
        lax.all_gather(output_weight, "wshard", axis=0, tiled=True),
        lax.all_gather(expand_weight, "wshard", axis=0, tiled=True),
        lax.all_gather(shrink_weight, "wshard", axis=0, tiled=True),
        lax.all_gather(attn_norm_gain, "wshard", axis=0, tiled=True),
        lax.all_gather(attn_norm_bias, "wshard", axis=0, tiled=True),
        lax.all_gather(query_bias, "wshard", axis=0, tiled=True),
        lax.all_gather(value_bias, "wshard", axis=0, tiled=True),
        lax.all_gather(output_bias, "wshard", axis=0, tiled=True),
        lax.all_gather(mlp_norm_gain, "wshard", axis=0, tiled=True),
        lax.all_gather(mlp_norm_bias, "wshard", axis=0, tiled=True),
        lax.all_gather(expand_bias, "wshard", axis=0, tiled=True),
        lax.all_gather(shrink_bias, "wshard", axis=0, tiled=True),
    )
    (
        weight_in,
        weight_out,
        weight_up,
        weight_down,
        gain_attn,
        bias_attn,
        bias_query,
        bias_value,
        bias_out,
        gain_mlp,
        bias_mlp,
        bias_up,
        bias_down,
    ) = gathered
    head_count = HEADS
    head_dim = HD
    inputs = tokens[0].astype(jnp.float32)
    row_count, model_width = inputs.shape
    group_len = token_order.shape[1]
    ctx_index = lax.axis_index("ctx")
    all_pos = token_order[0]
    all_start = seq_starts(all_pos, seq_lengths[0])
    my_pos = lax.dynamic_slice_in_dim(all_pos, ctx_index * row_count, row_count)
    my_start = lax.dynamic_slice_in_dim(all_start, ctx_index * row_count, row_count)
    block_rows = min(512, group_len)
    block_count = group_len // block_rows
    block_ids = jnp.arange(block_count, dtype=jnp.int32)
    normed_full, norm_pull = jax.vjp(
        layer_norm, inputs, gain_attn.astype(jnp.float32), bias_attn.astype(jnp.float32)
    )
    normed = normed_full.astype(jnp.bfloat16)
    joint = jnp.dot(normed, weight_in, preferred_element_type=jnp.float32)
    queries = (joint[:, :model_width] + bias_query.astype(jnp.float32)).astype(jnp.bfloat16)
    keys_own = joint[:, model_width : 2 * model_width].astype(jnp.bfloat16)
    values_own = (joint[:, 2 * model_width :] + bias_value.astype(jnp.float32)).astype(jnp.bfloat16)
    keys_all, values_all = (
        lax.all_gather(keys_own, "ctx", axis=0, tiled=True),
        lax.all_gather(values_own, "ctx", axis=0, tiled=True),
    )
    query_heads = queries.reshape(row_count, head_count, head_dim)

    def key_block(block_index):
        key_heads = take_rows(keys_all, block_index, block_rows).reshape(
            block_rows, head_count, head_dim
        )
        value_heads = take_rows(values_all, block_index, block_rows).reshape(
            block_rows, head_count, head_dim
        )
        return (key_heads, value_heads, take_rows(all_pos, block_index, block_rows))

    def stat_step(carried, block_index):
        row_peak, row_total = carried
        key_heads, value_heads, key_pos = key_block(block_index)
        scores = scores_of(query_heads, key_heads, my_pos, my_start, key_pos)
        new_peak = jnp.maximum(row_peak, jnp.max(scores, axis=-1))
        row_total = row_total * jnp.exp(row_peak - new_peak) + jnp.sum(
            jnp.exp(scores - new_peak[..., None]), axis=-1
        )
        return ((new_peak, row_total), None)

    start_stats = (
        jnp.full((head_count, row_count), masked_fill, jnp.float32),
        jnp.zeros((head_count, row_count), jnp.float32),
    )
    (row_peak, row_total), _ = lax.scan(stat_step, start_stats, block_ids)
    log_total = row_peak + jnp.log(row_total)

    def out_step(summed, block_index):
        key_heads, value_heads, key_pos = key_block(block_index)
        scores = scores_of(query_heads, key_heads, my_pos, my_start, key_pos)
        soft_low = jnp.exp(scores - log_total[..., None]).astype(jnp.bfloat16)
        return (
            summed
            + jnp.einsum("hqk,khd->qhd", soft_low, value_heads, preferred_element_type=jnp.float32),
            None,
        )

    attn_full, _ = lax.scan(
        out_step, jnp.zeros((row_count, head_count, head_dim), jnp.float32), block_ids
    )
    attn = attn_full.reshape(row_count, model_width).astype(jnp.bfloat16)
    mixed = (
        inputs
        + jnp.dot(attn, weight_out, preferred_element_type=jnp.float32)
        + bias_out.astype(jnp.float32)
    )
    normed_mlp_full, norm_mlp_pull = jax.vjp(
        layer_norm, mixed, gain_mlp.astype(jnp.float32), bias_mlp.astype(jnp.float32)
    )
    normed_mlp = normed_mlp_full.astype(jnp.bfloat16)
    hidden = jnp.dot(normed_mlp, weight_up, preferred_element_type=jnp.float32) + bias_up.astype(
        jnp.float32
    )
    active_full, gelu_pull = jax.vjp(gelu_act, hidden)
    active = active_full.astype(jnp.bfloat16)
    result = (
        mixed
        + jnp.dot(active, weight_down, preferred_element_type=jnp.float32)
        + bias_down.astype(jnp.float32)
    )
    block_out = result.astype(jnp.bfloat16)[None]
    upstream = cotangent[0].astype(jnp.float32)
    down_grad = upstream.astype(jnp.bfloat16)
    grad_down_bias = jnp.sum(down_grad.astype(jnp.float32), axis=0)
    grad_down = outer_sum(active, down_grad)
    (hidden_grad,) = gelu_pull(times_t(down_grad, weight_down))
    hidden_low = hidden_grad.astype(jnp.bfloat16)
    grad_up_bias = jnp.sum(hidden_low.astype(jnp.float32), axis=0)
    grad_up = outer_sum(normed_mlp, hidden_low)
    mixed_norm_grad, grad_mlp_gain, grad_mlp_bias = norm_mlp_pull(times_t(hidden_low, weight_up))
    mixed_grad = upstream + mixed_norm_grad
    branch_low = mixed_grad.astype(jnp.bfloat16)
    grad_out_bias = jnp.sum(branch_low.astype(jnp.float32), axis=0)
    grad_out = outer_sum(attn, branch_low)
    attn_grad = times_t(branch_low, weight_out).astype(jnp.bfloat16)
    grad_heads = attn_grad.reshape(row_count, head_count, head_dim)
    zero_delta = jnp.zeros((head_count, row_count), jnp.float32)
    zero_query = jnp.zeros((row_count, head_count, head_dim), jnp.float32)

    def first_step(summed, block_index):
        key_heads, value_heads, key_pos = key_block(block_index)
        scores = scores_of(query_heads, key_heads, my_pos, my_start, key_pos)
        soft_full = jnp.exp(scores - log_total[..., None])
        soft_grad = jnp.einsum(
            "qhd,khd->hqk", grad_heads, value_heads, preferred_element_type=jnp.float32
        )
        value_part = jnp.einsum(
            "hqk,qhd->khd",
            soft_full.astype(jnp.bfloat16),
            grad_heads,
            preferred_element_type=jnp.float32,
        )
        return (
            summed + jnp.sum(soft_full * soft_grad, axis=-1),
            value_part.reshape(block_rows, model_width),
        )

    delta, value_parts = lax.scan(first_step, zero_delta, block_ids)

    def second_step(summed, block_index):
        key_heads, value_heads, key_pos = key_block(block_index)
        scores = scores_of(query_heads, key_heads, my_pos, my_start, key_pos)
        soft_full = jnp.exp(scores - log_total[..., None])
        soft_grad = jnp.einsum(
            "qhd,khd->hqk", grad_heads, value_heads, preferred_element_type=jnp.float32
        )
        score_grad = (soft_full * (soft_grad - delta[..., None])).astype(jnp.bfloat16)
        query_part = (
            jnp.einsum("hqk,khd->qhd", score_grad, key_heads, preferred_element_type=jnp.float32)
            * 0.125
        )
        key_part = (
            jnp.einsum("hqk,qhd->khd", score_grad, query_heads, preferred_element_type=jnp.float32)
            * 0.125
        )
        return (summed + query_part, key_part.reshape(block_rows, model_width))

    query_summed, key_parts = lax.scan(second_step, zero_query, block_ids)
    key_terms = jnp.concatenate(
        [key_parts.reshape(group_len, model_width), value_parts.reshape(group_len, model_width)],
        axis=1,
    )
    owned_terms = lax.psum_scatter(
        key_terms.astype(jnp.bfloat16), "ctx", scatter_dimension=0, tiled=True
    ).astype(jnp.float32)
    key_grad = owned_terms[:, :model_width]
    value_grad = owned_terms[:, model_width:]
    query_low = query_summed.reshape(row_count, model_width).astype(jnp.bfloat16)
    key_low = key_grad.astype(jnp.bfloat16)
    value_low = value_grad.astype(jnp.bfloat16)
    grad_query_bias = jnp.sum(query_low.astype(jnp.float32), axis=0)
    grad_value_bias = jnp.sum(value_low.astype(jnp.float32), axis=0)
    joint_grad = jnp.concatenate([query_low, key_low, value_low], axis=1)
    grad_in = outer_sum(normed, joint_grad)
    input_norm_grad, grad_attn_gain, grad_attn_bias = norm_pull(times_t(joint_grad, weight_in))
    input_grad = (mixed_grad + input_norm_grad).astype(jnp.bfloat16)[None]
    owned = (
        lax.psum_scatter(
            grad_attn_gain.astype(jnp.bfloat16), "wshard", scatter_dimension=0, tiled=True
        ).astype(jnp.float32),
        lax.psum_scatter(
            grad_attn_bias.astype(jnp.bfloat16), "wshard", scatter_dimension=0, tiled=True
        ).astype(jnp.float32),
        lax.psum_scatter(
            grad_in.astype(jnp.bfloat16), "wshard", scatter_dimension=0, tiled=True
        ).astype(jnp.float32),
        lax.psum_scatter(
            grad_query_bias.astype(jnp.bfloat16), "wshard", scatter_dimension=0, tiled=True
        ).astype(jnp.float32),
        lax.psum_scatter(
            grad_value_bias.astype(jnp.bfloat16), "wshard", scatter_dimension=0, tiled=True
        ).astype(jnp.float32),
        lax.psum_scatter(
            grad_out.astype(jnp.bfloat16), "wshard", scatter_dimension=0, tiled=True
        ).astype(jnp.float32),
        lax.psum_scatter(
            grad_out_bias.astype(jnp.bfloat16), "wshard", scatter_dimension=0, tiled=True
        ).astype(jnp.float32),
        lax.psum_scatter(
            grad_mlp_gain.astype(jnp.bfloat16), "wshard", scatter_dimension=0, tiled=True
        ).astype(jnp.float32),
        lax.psum_scatter(
            grad_mlp_bias.astype(jnp.bfloat16), "wshard", scatter_dimension=0, tiled=True
        ).astype(jnp.float32),
        lax.psum_scatter(
            grad_up.astype(jnp.bfloat16), "wshard", scatter_dimension=0, tiled=True
        ).astype(jnp.float32),
        lax.psum_scatter(
            grad_up_bias.astype(jnp.bfloat16), "wshard", scatter_dimension=0, tiled=True
        ).astype(jnp.float32),
        lax.psum_scatter(
            grad_down.astype(jnp.bfloat16), "wshard", scatter_dimension=0, tiled=True
        ).astype(jnp.float32),
        lax.psum_scatter(
            grad_down_bias.astype(jnp.bfloat16), "wshard", scatter_dimension=0, tiled=True
        ).astype(jnp.float32),
    )
    summed_grads = (
        lax.psum(owned[0].astype(jnp.bfloat16), "ctx").astype(jnp.float32),
        lax.psum(owned[1].astype(jnp.bfloat16), "ctx").astype(jnp.float32),
        lax.psum(owned[2].astype(jnp.bfloat16), "ctx").astype(jnp.float32),
        lax.psum(owned[3].astype(jnp.bfloat16), "ctx").astype(jnp.float32),
        lax.psum(owned[4].astype(jnp.bfloat16), "ctx").astype(jnp.float32),
        lax.psum(owned[5].astype(jnp.bfloat16), "ctx").astype(jnp.float32),
        lax.psum(owned[6].astype(jnp.bfloat16), "ctx").astype(jnp.float32),
        lax.psum(owned[7].astype(jnp.bfloat16), "ctx").astype(jnp.float32),
        lax.psum(owned[8].astype(jnp.bfloat16), "ctx").astype(jnp.float32),
        lax.psum(owned[9].astype(jnp.bfloat16), "ctx").astype(jnp.float32),
        lax.psum(owned[10].astype(jnp.bfloat16), "ctx").astype(jnp.float32),
        lax.psum(owned[11].astype(jnp.bfloat16), "ctx").astype(jnp.float32),
        lax.psum(owned[12].astype(jnp.bfloat16), "ctx").astype(jnp.float32),
    )
    return (block_out, input_grad) + tuple(summed_grads)


def fits(n, nz):
    power = n & (n - 1) == 0 and nz & (nz - 1) == 0
    return power and HEADS % n == 1 and (HEADS // n * HD) % 128 == 0


def solution(mesh):
    placed = (
        P("wshard", "ctx", None),
        P("wshard", "ctx", None),
        P("wshard", None),
        P("wshard", None),
        P("wshard"),
        P("wshard"),
        P("wshard", None),
        P("wshard"),
        P("wshard"),
        P("wshard", None),
        P("wshard"),
        P("wshard"),
        P("wshard"),
        P("wshard", None),
        P("wshard"),
        P("wshard", None),
        P("wshard"),
    )
    n, nz = mesh.shape["ctx"], mesh.shape["wshard"]
    local = functools.partial(local_fast, n, nz) if fits(n, nz) else local_plain
    return jax.shard_map(
        local,
        mesh=mesh,
        in_specs=placed,
        out_specs=(
            P("wshard", "ctx", None),
            P("wshard", "ctx", None),
            P("wshard"),
            P("wshard"),
            P("wshard", None),
            P("wshard"),
            P("wshard"),
            P("wshard", None),
            P("wshard"),
            P("wshard"),
            P("wshard"),
            P("wshard", None),
            P("wshard"),
            P("wshard", None),
            P("wshard"),
        ),
        check_vma=False,
    )
```
